32 devices in a mesh: group: 4 (over y, core), tok: 8 (over z, x).
Axes of the slice: x: 2, y: 2, z: 4, core: 2. Of those that a mesh axis runs over, the one named last changes fastest.
Arguments:
- queries: bfloat16 [4, 1024, 1536], P('group', 'tok'), may hold values from -60 to 60
- suffix_cache: bfloat16 [4, 1024, 1024], P('group', 'tok'), may hold values from -30 to 30
- stream_in: bfloat16 [4, 1024, 1536], P('group', 'tok'), may hold values from -6 to 6
- page_pool: bfloat16 [4, 32, 128, 1024], P('group', 'tok'), may hold values from -30 to 30
- page_table: int32 [4, 32], P('group'), may hold values from 0 to 31, each once within a row
- segment_ids: int32 [4, 1024], P('group'), may hold values from 0 to 15, never falling along the last dimension, each value on 1 to 256 neighbouring positions
- dealing: int32 [4, 1024], P('group'), may hold values from 0 to 1023, each once within a row
- out_proj: bfloat16 [1536, 1536], replicated, may hold values from -0.15625 to 0.15625
- norm_gain: float32 [1536], replicated, may hold values from 0.1 to 1.9
- expert_ids: int32 [4, 1024, 8], P('group', 'tok'), may hold values from 0 to 31, all different within a row; in each aligned block of 128 rows (0 to 127, 128 to 255, ..., all dimensions but the last counted through in order) at most 40 rows name the same one
- expert_gates: float32 [4, 1024, 8], P('group', 'tok'), may hold values from 0.05 to 0.35
- gate_proj: bfloat16 [32, 1536, 512], P('tok'), may hold values from -0.15625 to 0.15625
- up_proj: bfloat16 [32, 1536, 512], P('tok'), may hold values from -0.15625 to 0.15625
- down_proj: bfloat16 [32, 512, 1536], P('tok'), may hold values from -0.25 to 0.25
Outputs:
- stream_out: bfloat16 [4, 1024, 1536], P('group', 'tok')
The draws below stay inside these ranges and needn't reach their ends.
Inputs may be any that keep to these rules, and one draw needn't show every extreme that they name: page_table[g] is a permutation of the 32 slots. dealing[g] is a permutation of the 1024 packed positions. `segment_ids`: segment numbers never fall along a group's packed positions; each request holds 1 to 256 positions and one holds exactly 256. `expert_ids`: each row names 8 different experts; within the rows of one device no expert is named by more than 40 rows, a bound that some block reaches.
All inputs are finite; a program needn't handle non-finite values.
Results may differ from the reference program's by a relative error of at most 0.008.
The reference program's roundings to bfloat16 on the way count: a program that leaves them out, or rounds other values in their place, can miss the bound.
Values may be sent and summed in bfloat16 or wider, within the bound.
A program may use at most 128 MiB of HBM per device.

```python
import math
import jax
import jax.numpy as jnp
import numpy as np
from jax import lax

D = 1536
QH = 24
KVH = 8
HD = 64
FF = 512
TOPK = 8
EXPERTS = 32
PAGE = 128
REQS = 16
PREFIX_PAGES = 32
TOK_DEV = 128
CAP = 40
SUF = 1024
GROUPS = 4
N_TOK = 8


def draw_queries(key, part):
    shape = (GROUPS, SUF, QH * HD)
    base_key = jax.random.fold_in(key, 7)
    first_key = jax.random.fold_in(base_key, 0)
    values = jnp.clip(1.5 * jax.random.normal(first_key, shape, jnp.float32), -9.0, 9.0)
    return values.astype(jnp.bfloat16)


def cache_rows(key, shape):
    width = KVH * HD
    column = jnp.arange(2 * width)
    is_key = column < width
    base = jnp.clip(jax.random.normal(key, shape, jnp.float32), -6.0, 6.0)
    values = jnp.where(is_key, 2.0 * base, base)
    return values.astype(jnp.bfloat16)


def draw_suffix_cache(key, part):
    return cache_rows(jax.random.fold_in(key, 13), (GROUPS, SUF, 2 * KVH * HD))


def draw_page_pool(key, part):
    return cache_rows(jax.random.fold_in(key, 17), (GROUPS, PREFIX_PAGES, PAGE, 2 * KVH * HD))


def level_of(rng, dims, pieces, least, top_value):
    loudness, own = 1.0, jax.random.fold_in(rng, 6)
    for axis_at, parts in pieces:
        steps = jnp.exp(jax.random.uniform(jax.random.fold_in(own, axis_at), (parts,), jnp.float32, least / len(pieces), top_value / len(pieces)))
        loudness = loudness * jnp.repeat(steps, dims[axis_at] // parts).reshape([-1 if axis == axis_at else 1 for axis in range(len(dims))])
    return loudness


def split_up(amount, total, bound, skew):
    weights = [(1 << 20) // math.isqrt(rank ** skew) + 1 for rank in range(2, amount + 1)]
    surplus, holding = total - bound - (amount - 1), [1] * (amount - 1)
    while surplus > 0:
        free = [i for i in range(amount - 1) if holding[i] < bound]
        whole, remaining = sum([weights[i] for i in free]), surplus
        for i in free:
            more = min(bound - holding[i], max(1, remaining * weights[i] // whole), surplus)
            holding[i] = holding[i] + more
            surplus = surplus - more
    return np.array([bound] + holding)


def ragged_sizes(rng, amount, total, limit, lean):
    if amount == 2:
        one = jax.random.randint(rng, (), max(1, total - limit), min(limit, total - 1) + 1)
        return jnp.stack([one, total - one])
    sizes = jnp.asarray(split_up(amount, total, limit, lean), jnp.int32)
    couples = (amount - 1) // 2
    source_of, taker = sizes[1:1 + 2 * couples:2], sizes[2:2 + 2 * couples:2]
    room = jnp.minimum(source_of - 1, limit - taker)
    passed = jax.random.randint(jax.random.fold_in(rng, 1), (couples,), 0, 1 << 20) % (room + 1)
    sizes = sizes.at[1:1 + 2 * couples:2].set(source_of - passed).at[2:2 + 2 * couples:2].set(taker + passed)
    return sizes[jax.random.permutation(jax.random.fold_in(rng, 2), amount)]


def assign_block(key, own, number, rows, amount, top, reach, slope):
    sequence = jax.random.permutation(key, amount)
    crowded, usual = shares(amount, rows * top, reach, slope, True), shares(amount, rows * top, reach, slope, False)
    places = jnp.arange(amount)

    def named(tallies, turn):
        used = int((tallies > 0).sum())
        fixed = max(1, used // 4)
        shifted = fixed + (places - fixed + turn * (used - fixed)) % max(1, amount - fixed)
        return jnp.zeros((amount,), jnp.int32).at[sequence[jnp.where(places < fixed, places, shifted)]].set(jnp.asarray(tallies, jnp.int32))

    tallies = jnp.where(number % 4 == 0, named(crowded, number // 4), named(usual, number - number // 4 - 1))
    mixed = jax.random.permutation(jax.random.fold_in(own, 3), amount)
    source_of, taker = mixed[0:amount // 2 * 2:2], mixed[1:amount // 2 * 2:2]
    room = jnp.minimum(tallies[source_of] - 1, reach - tallies[taker]) // 2
    room = jnp.where((source_of == sequence[0]) | (taker == sequence[0]) | (tallies[taker] == 0), 0, jnp.maximum(room, 0))
    shifted = jax.random.randint(jax.random.fold_in(own, 4), (amount // 2,), 0, 1 << 20) % (room + 1)
    tallies = tallies.at[source_of].add(-shifted).at[taker].add(shifted)
    items = jnp.searchsorted(jnp.cumsum(tallies), jnp.arange(rows * top), side="right").astype(jnp.int32)
    listing = items.reshape(top, rows).T
    listing = listing[jax.random.permutation(jax.random.fold_in(own, 1), rows)]
    turn = jax.random.randint(jax.random.fold_in(own, 2), (rows, 1), 0, top)
    return jnp.take_along_axis(listing, (jnp.arange(top)[None, :] + turn) % top, axis=1)


def shares(amount, total, limit, slope, full):
    portions = [(1 << 20) // math.isqrt(standing ** slope) + 1 for standing in range(1, amount + 1)]
    largest = limit if full else min(limit, max(-(-total // amount), total * portions[0] // sum(portions)))
    least = 1 if total - largest >= amount - 1 else 0
    counts, surplus = [largest] + [least] * (amount - 1), total - largest - least * (amount - 1)
    while surplus > 0:
        candidates = [i for i in range(1, amount) if counts[i] < largest] or [i for i in range(1, amount) if counts[i] < limit]
        pool, remaining = sum([portions[i] for i in candidates]), surplus
        for i in candidates:
            more = min(limit - counts[i], max(1, remaining * portions[i] // pool), surplus)
            counts[i] = counts[i] + more
            surplus = surplus - more
    return np.array(counts)


def centred(own_key, shape, scale, most, cuts=(), kind=jnp.bfloat16):
    drawn = scale * jax.random.normal(own_key, shape, jnp.float32)
    if cuts:
        drawn = drawn * level_of(own_key, shape, cuts, -0.22, 0.18)
    return jnp.clip(drawn, -most, most).astype(kind)


def setup_inputs(seed: int = 0) -> dict:
    keys = jax.random.split(jax.random.key(seed), 15)
    queries = draw_queries(jax.random.fold_in(keys[14], 71), 0)
    suffix_cache = draw_suffix_cache(jax.random.fold_in(keys[14], 71), 0)
    stream_in = centred(keys[2], (GROUPS, SUF, D), 1.0, 6.0, ((0, 4), (1, 8)))
    page_pool = draw_page_pool(jax.random.fold_in(keys[14], 71), 0)
    page_table = jax.vmap(lambda own: jax.random.permutation(own, PREFIX_PAGES))(jax.random.split(keys[4], GROUPS)).reshape((GROUPS, PREFIX_PAGES)).astype(jnp.int32)
    segment_ids = jax.vmap(lambda own: jnp.searchsorted(jnp.cumsum(ragged_sizes(own, REQS, SUF, SUF // 4, 2)), jnp.arange(SUF), side="right"))(jax.random.split(keys[5], GROUPS)).reshape((GROUPS, SUF)).astype(jnp.int32)
    dealing = jax.vmap(lambda own: jax.random.permutation(own, SUF))(jax.random.split(keys[6], GROUPS)).reshape((GROUPS, SUF)).astype(jnp.int32)
    out_proj = centred(keys[7], (QH * HD, D), (QH * HD) ** -0.5, 0.15625)
    norm_gain = jnp.clip(1.0 + 0.18 * jax.random.normal(keys[8], (D,), jnp.float32), 0.1, 1.9)
    expert_ids_keys = jax.random.split(jax.random.fold_in(keys[9], 1), GROUPS * SUF // TOK_DEV)
    expert_ids_turns = jax.random.permutation(jax.random.fold_in(keys[9], 3), GROUPS * SUF // TOK_DEV)
    expert_ids = jax.vmap(lambda own, number: assign_block(jax.random.fold_in(keys[9], 2), own, number, TOK_DEV, EXPERTS, TOPK, CAP, 2))(expert_ids_keys, expert_ids_turns).reshape((GROUPS, SUF, TOPK))
    expert_gates = jnp.clip(0.05 + 0.29999999 * jax.random.uniform(keys[10], (GROUPS, SUF, TOPK), jnp.float32) ** level_of(keys[10], (GROUPS, SUF, TOPK), ((0, 4), (1, 8)), -0.2, 0.2), 0.05, 0.35)
    gate_proj = centred(keys[11], (EXPERTS, D, FF), D ** -0.5, 0.15625, ((0, 8),))
    up_proj = centred(keys[12], (EXPERTS, D, FF), D ** -0.5, 0.15625, ((0, 8),))
    down_proj = centred(keys[13], (EXPERTS, FF, D), FF ** -0.5, 0.25, ((0, 8),))
    return dict(queries=queries, suffix_cache=suffix_cache, stream_in=stream_in, page_pool=page_pool, page_table=page_table, segment_ids=segment_ids, dealing=dealing, out_proj=out_proj, norm_gain=norm_gain, expert_ids=expert_ids, expert_gates=expert_gates, gate_proj=gate_proj, up_proj=up_proj, down_proj=down_proj)


ROPE_BASE = 10000.0
NEG_FILL = -1e+30

def rotate(vectors, positions):
    half_dim = vectors.shape[-1] // 2
    frequency = ROPE_BASE ** (-jnp.arange(half_dim, dtype=jnp.float32) / half_dim)
    angles = positions.astype(jnp.float32)[:, None] * frequency[None, :]
    cosine = jnp.cos(angles)[:, None, :]
    sine_part = jnp.sin(angles)[:, None, :]
    first_half = vectors[..., :half_dim].astype(jnp.float32)
    second = vectors[..., half_dim:].astype(jnp.float32)
    joined = jnp.concatenate([first_half * cosine - second * sine_part, first_half * sine_part + second * cosine], axis=-1)
    return joined.astype(jnp.bfloat16)

def request_positions(packed_segments, dealt):
    requests = jnp.arange(REQS, dtype=jnp.int32)
    starts = lax.optimization_barrier(jnp.sum((packed_segments[:, None] < requests[None, :]).astype(jnp.int32), axis=0))
    dealt_segments = packed_segments[dealt]
    onehot = (dealt_segments[:, None] == requests[None, :]).astype(jnp.int32)
    dealt_starts = lax.optimization_barrier(jnp.sum(onehot * starts[None, :], axis=1))
    return (dealt_segments, dealt - dealt_starts)

def one_group(queries, suffix_cache, stream_in, page_pool, page_table, segment_ids, dealing, out_proj, norm_gain, expert_ids, expert_gates, gate_proj, up_proj, down_proj):
    width = KVH * HD
    ratio = QH // KVH
    prefix_len = PREFIX_PAGES * PAGE
    seg_rows, offsets = request_positions(segment_ids, dealing)
    positions = offsets + prefix_len
    logical_pool = page_pool[page_table].reshape(prefix_len, 2 * width)
    prefix_keys = rotate(logical_pool[:, :width].reshape(prefix_len, KVH, HD), jnp.arange(prefix_len, dtype=jnp.int32))
    prefix_values = logical_pool[:, width:].reshape(prefix_len, KVH, HD)
    suffix_keys = rotate(suffix_cache[:, :width].reshape(SUF, KVH, HD), positions)
    suffix_values = suffix_cache[:, width:].reshape(SUF, KVH, HD)
    all_keys = jnp.concatenate([prefix_keys, suffix_keys], axis=0).astype(jnp.float32)
    all_values = jnp.concatenate([prefix_values, suffix_values], axis=0).astype(jnp.float32)
    roped = rotate(queries.reshape(SUF, QH, HD), positions).reshape(SUF, KVH, ratio, HD)
    blocks = SUF // TOK_DEV
    scale = HD ** (-0.5)

    def attend(inputs):
        query_block, seg_block, packed_block = inputs
        scores = jnp.einsum('qgjd,rgd->qgjr', query_block.astype(jnp.float32), all_keys, precision=lax.Precision.HIGHEST) * scale
        suffix_seen = (seg_block[:, None] == seg_rows[None, :]) & (dealing[None, :] <= packed_block[:, None])
        visible = jnp.concatenate([jnp.ones((TOK_DEV, prefix_len), bool), suffix_seen], axis=1)
        masked = jnp.where(visible[:, None, None, :], scores, NEG_FILL)
        largest = lax.optimization_barrier(jnp.max(masked, axis=-1))
        weights = jnp.where(visible[:, None, None, :], jnp.exp(masked - largest[..., None]), 0.0)
        total = lax.optimization_barrier(jnp.sum(weights, axis=-1))
        rounded = lax.optimization_barrier(weights.astype(jnp.bfloat16)).astype(jnp.float32)
        numer = jnp.einsum('qgjr,rgd->qgjd', rounded, all_values, precision=lax.Precision.HIGHEST)
        return (numer / total[..., None]).reshape(TOK_DEV, QH * HD).astype(jnp.bfloat16)
    attended = lax.map(attend, (roped.reshape(blocks, TOK_DEV, KVH, ratio, HD), seg_rows.reshape(blocks, TOK_DEV), dealing.reshape(blocks, TOK_DEV)))
    attended = attended.reshape(SUF, QH * HD)
    mid_round = lax.optimization_barrier((stream_in.astype(jnp.float32) + jnp.dot(attended, out_proj, preferred_element_type=jnp.float32)).astype(jnp.bfloat16))
    mid_float = mid_round.astype(jnp.float32)
    normed = (mid_float * lax.rsqrt(lax.optimization_barrier(jnp.mean(mid_float * mid_float, axis=-1, keepdims=True)) + 1e-05) * norm_gain).astype(jnp.bfloat16)
    routes = expert_ids.reshape(N_TOK, TOK_DEV * TOPK)
    member = (routes[..., None] == jnp.arange(EXPERTS, dtype=jnp.int32)[None, None, :]).astype(jnp.int32)
    before = jnp.cumsum(member, axis=1) - member
    slots = lax.optimization_barrier(jnp.sum(before * member, axis=-1))
    block_base = (jnp.arange(N_TOK, dtype=jnp.int32) * (EXPERTS * CAP))[:, None]
    target = (routes * CAP + slots + block_base).reshape(SUF, TOPK)
    token_rows = jnp.repeat(jnp.arange(SUF, dtype=jnp.int32), TOPK)
    buffer = jnp.zeros((N_TOK * EXPERTS * CAP, D), jnp.bfloat16).at[target.reshape(-1)].set(normed[token_rows])
    buffer = buffer.reshape(N_TOK, EXPERTS, CAP, D)

    def expert(index):
        rows_in = buffer[:, index].reshape(N_TOK * CAP, D)
        gate_vals = jnp.dot(rows_in, gate_proj[index], preferred_element_type=jnp.float32)
        up_vals = jnp.dot(rows_in, up_proj[index], preferred_element_type=jnp.float32)
        hidden = (jax.nn.silu(gate_vals) * up_vals).astype(jnp.bfloat16)
        return jnp.dot(hidden, down_proj[index], preferred_element_type=jnp.float32).astype(jnp.bfloat16)
    produced = lax.map(expert, jnp.arange(EXPERTS, dtype=jnp.int32))
    produced = produced.reshape(EXPERTS, N_TOK, CAP, D).transpose(1, 0, 2, 3).reshape(N_TOK * EXPERTS * CAP, D)
    picked = produced[target].astype(jnp.float32)
    mixed = lax.optimization_barrier(jnp.sum(expert_gates[..., None] * picked, axis=1))
    return (mid_float + mixed).astype(jnp.bfloat16)

def reference(queries, suffix_cache, stream_in, page_pool, page_table, segment_ids, dealing, out_proj, norm_gain, expert_ids, expert_gates, gate_proj, up_proj, down_proj):
    results = []
    for group_index in range(GROUPS):
        results.append(one_group(queries[group_index], suffix_cache[group_index], stream_in[group_index], page_pool[group_index], page_table[group_index], segment_ids[group_index], dealing[group_index], out_proj, norm_gain, expert_ids[group_index], expert_gates[group_index], gate_proj, up_proj, down_proj))
    return jnp.stack(results)
```

```python
import functools

import jax
import jax.numpy as jnp
from jax import lax
from jax.experimental import pallas as pl
from jax.experimental.pallas import tpu as pltpu
from jax.sharding import PartitionSpec as P

QH = 24
KVH = 8
HD = 64
RATIO = QH // KVH
EXPERTS = 32
REQS = 16
ROPE_BASE = 10000.0
NEG_FILL = -1e30
KEY_CHUNK = 1024


def rotate(vectors, positions):
    half_dim = vectors.shape[-1] // 2
    frequency = ROPE_BASE ** (-jnp.arange(half_dim, dtype=jnp.float32) / half_dim)
    angles = positions.astype(jnp.float32)[:, None] * frequency[None, :]
    cosine = jnp.cos(angles)[:, None, :]
    sine_part = jnp.sin(angles)[:, None, :]
    first_half = vectors[..., :half_dim].astype(jnp.float32)
    second = vectors[..., half_dim:].astype(jnp.float32)
    joined = jnp.concatenate(
        [first_half * cosine - second * sine_part, first_half * sine_part + second * cosine],
        axis=-1,
    )
    return joined.astype(jnp.bfloat16)


def attention_kernel(prefix_len, q_ref, kv_ref, lo_ref, hi_ref, pk_ref, o_ref, vx_ref):
    keys = kv_ref.shape[0]
    rows = q_ref.shape[2]

    @pl.when(pl.program_id(0) == 0)
    def _():
        lane = lax.broadcasted_iota(jnp.int32, kv_ref.shape, 1)
        vx_ref[...] = jnp.where(lane < HD, jnp.ones_like(kv_ref), kv_ref[...])

    q = q_ref[0].reshape(RATIO * rows, 2 * HD)
    best = jnp.full((RATIO * rows, 1), NEG_FILL, jnp.float32)
    accum = jnp.zeros((RATIO * rows, 2 * HD), jnp.float32)
    scale = HD ** (-0.5)
    for first in range(0, keys, KEY_CHUNK):
        part = slice(first, first + KEY_CHUNK)
        scores = (
            lax.dot_general(
                q, kv_ref[part, :], (((1,), (1,)), ((), ())), preferred_element_type=jnp.float32
            )
            * scale
        )
        if first >= prefix_len:
            pk = pk_ref[:, first - prefix_len : first - prefix_len + KEY_CHUNK]
            seen = (pk >= lo_ref[0]) & (pk <= hi_ref[0])
            seen = jnp.concatenate([seen.astype(jnp.float32)] * RATIO, axis=0) > 0.5
            scores = jnp.where(seen, scores, NEG_FILL)
        new_best = jnp.maximum(best, jnp.max(scores, axis=-1, keepdims=True))
        weights = jnp.exp(scores - new_best).astype(jnp.bfloat16)
        factor = jnp.exp(best - new_best)
        accum = accum * factor + jnp.dot(
            weights, vx_ref[part, :], preferred_element_type=jnp.float32
        )
        best = new_best
    out = (accum[:, HD:] / accum[:, :HD]).astype(jnp.bfloat16).reshape(RATIO, rows, HD)
    o_ref[0] = jnp.concatenate([out[:, : rows // 2], out[:, rows // 2 :]], axis=-1)


def attention(q, kv, low, high, packed, prefix_len):
    sources, _, rows, _ = q.shape
    keys = kv.shape[0]
    suffix = keys - prefix_len
    return pl.pallas_call(
        functools.partial(attention_kernel, prefix_len),
        out_shape=jax.ShapeDtypeStruct((sources, RATIO, rows // 2, 2 * HD), jnp.bfloat16),
        grid=(sources,),
        in_specs=[
            pl.BlockSpec((1, RATIO, rows, 2 * HD), lambda i: (i, 0, 0, 0)),
            pl.BlockSpec((keys, 2 * HD), lambda i: (0, 0)),
            pl.BlockSpec((1, rows, 1), lambda i: (i, 0, 0)),
            pl.BlockSpec((1, rows, 1), lambda i: (i, 0, 0)),
            pl.BlockSpec((1, suffix), lambda i: (0, 0)),
        ],
        out_specs=pl.BlockSpec((1, RATIO, rows // 2, 2 * HD), lambda i: (i, 0, 0, 0)),
        scratch_shapes=[pltpu.VMEM((keys, 2 * HD), jnp.bfloat16)],
        compiler_params=pltpu.CompilerParams(vmem_limit_bytes=48 << 20),
    )(q, kv, low.reshape(sources, rows, 1), high.reshape(sources, rows, 1), packed.reshape(1, suffix))


def expert_kernel(x_ref, gates_ref, gate_ref, up_ref, down_ref, o_ref, acc_ref):
    expert = pl.program_id(1)
    x = x_ref[...]
    gate_vals = jnp.dot(x, gate_ref[0], preferred_element_type=jnp.float32)
    up_vals = jnp.dot(x, up_ref[0], preferred_element_type=jnp.float32)
    hidden = (gate_vals / (1.0 + jnp.exp(-gate_vals)) * up_vals).astype(jnp.bfloat16)
    produced = jnp.dot(hidden, down_ref[0], preferred_element_type=jnp.float32)
    term = gates_ref[0] * produced.astype(jnp.bfloat16).astype(jnp.float32)

    @pl.when(expert == 0)
    def _():
        acc_ref[...] = term

    @pl.when(expert > 0)
    def _():
        acc_ref[...] += term

    @pl.when(expert == pl.num_programs(1) - 1)
    def _():
        o_ref[...] = acc_ref[...].astype(jnp.bfloat16)


def expert_sums(x, gates, gate_proj, up_proj, down_proj):
    rows, width = x.shape
    experts, _, hidden = gate_proj.shape
    block = min(512, rows)
    return pl.pallas_call(
        expert_kernel,
        out_shape=jax.ShapeDtypeStruct((rows, width), jnp.bfloat16),
        grid=(rows // block, experts),
        in_specs=[
            pl.BlockSpec((block, width), lambda i, e: (i, 0)),
            pl.BlockSpec((1, block, 1), lambda i, e: (e, i, 0)),
            pl.BlockSpec((1, width, hidden), lambda i, e: (e, 0, 0)),
            pl.BlockSpec((1, width, hidden), lambda i, e: (e, 0, 0)),
            pl.BlockSpec((1, hidden, width), lambda i, e: (e, 0, 0)),
        ],
        out_specs=pl.BlockSpec((block, width), lambda i, e: (i, 0)),
        scratch_shapes=[pltpu.VMEM((block, width), jnp.float32)],
        compiler_params=pltpu.CompilerParams(vmem_limit_bytes=56 << 20),
    )(x, gates, gate_proj, up_proj, down_proj)


def moe_kernel(
    x_ref,
    mid_ref,
    wg_hbm,
    wu_hbm,
    wd_hbm,
    o_ref,
    wg,
    wu,
    wd,
    buf,
    acc,
    sendx,
    recvx,
    stage,
    recv_r,
    recv_l,
    sendf,
    recvf,
    w_sem,
    ag_send,
    ag_recv,
    sx_sem,
    rx_sem,
    st_sem,
    rr_sem,
    rl_sem,
    f_sem,
):
    me = lax.axis_index("tok")
    z = me // 2
    x = me % 2
    partner = z * 2 + 1 - x
    width = mid_ref.shape[1]
    local = wg.shape[0]
    half = buf.shape[2]

    def weight_copies(e):
        return [
            pltpu.make_async_copy(src.at[e], dst.at[e], w_sem.at[e, i])
            for i, (src, dst) in enumerate([(wg_hbm, wg), (wu_hbm, wu), (wd_hbm, wd)])
        ]

    for e in range(local):
        for copy in weight_copies(e):
            copy.start()

    barrier = pltpu.get_barrier_semaphore()

    def greet(device):
        pl.semaphore_signal(
            barrier, inc=1, device_id={"tok": device}, device_id_type=pl.DeviceIdType.MESH
        )

    greet(partner)
    pl.when(z > 0)(lambda: greet(me - 2))
    pl.when(z < 3)(lambda: greet(me + 2))
    pl.semaphore_wait(barrier, 2 + ((z + 1) // 2) % 2)

    buf[me] = x_ref[...].reshape(2, half, x_ref.shape[1])

    def send(src, dst, send_sem, recv_sem, device):
        return pltpu.make_async_remote_copy(
            src_ref=src,
            dst_ref=dst,
            send_sem=send_sem,
            recv_sem=recv_sem,
            device_id={"tok": device},
            device_id_type=pl.DeviceIdType.MESH,
        )

    def token_copy(shard, part, way):
        device = (partner, me - 2, me + 2)[way]
        return send(
            buf.at[shard, part],
            buf.at[shard, part],
            ag_send.at[shard, part, way],
            ag_recv.at[shard, part],
            device,
        )

    pending = []

    def go(cond, shard, part, way):
        if cond is None:
            token_copy(shard, part, way).start()
        else:
            pl.when(cond)(lambda: token_copy(shard, part, way).start())
        pending.append((cond, shard, part, way))

    for part in (1, 0):
        go(None, me, part, 0)
        go(z > 0, me, part, 1)
        go(z < 3, me, part, 2)
    token_copy(partner, 1, 0).wait_recv()
    go(z > 0, partner, 1, 1)
    go(z < 3, partner, 1, 2)
    token_copy(partner, 0, 0).wait_recv()

    def receive(distance):
        sides = [(-1, z >= distance, z < 3, 2), (1, z + distance <= 3, z > 0, 1)]
        for side, there, onward, way in sides:
            pair = 2 * (z + side * distance)
            same, other = pair + x, pair + 1 - x

            def arrived(shard, part, there=there):
                pl.when(there)(lambda: token_copy(shard, part, 0).wait_recv())

            arrived(same, 1)
            go(there & onward, same, 1, way)
            arrived(same, 0)
            go(there, same, 0, 0)
            go(there & onward, same, 0, way)
            arrived(other, 1)
            go(there & onward, other, 1, way)
        for side, there, onward, way in sides:
            other = 2 * (z + side * distance) + 1 - x
            pl.when(there)(lambda other=other: token_copy(other, 0, 0).wait_recv())

    def compute(c, first):
        rows = buf[pl.ds(2 * c, 2)].reshape(4 * half, buf.shape[3])
        tokens = rows[:, :width]
        coded = rows[:, width:].astype(jnp.float32)
        lane = lax.broadcasted_iota(jnp.int32, coded.shape, 1)

        def one(e, carry):
            if first:
                for copy in weight_copies(e):
                    copy.wait()
            picked = (lane % EXPERTS == me * local + e) & (lane < 3 * EXPERTS)
            gates = jnp.sum(jnp.where(picked, coded, 0.0), axis=-1, keepdims=True)
            gate_vals = jnp.dot(tokens, wg[e], preferred_element_type=jnp.float32)
            up_vals = jnp.dot(tokens, wu[e], preferred_element_type=jnp.float32)
            hidden = (gate_vals / (1.0 + jnp.exp(-gate_vals)) * up_vals).astype(jnp.bfloat16)
            produced = jnp.dot(hidden, wd[e], preferred_element_type=jnp.float32)
            term = gates * produced.astype(jnp.bfloat16).astype(jnp.float32)
            acc[pl.ds(2 * c, 2)] += term.reshape(2, 2, half, width)
            return carry

        acc[pl.ds(2 * c, 2)] = jnp.zeros((2, 2, half, width), jnp.float32)
        lax.fori_loop(0, local, one, 0)
        sendx[c] = acc[2 * c + 1 - x, 0].astype(jnp.bfloat16)
        across(c).start()

    def across(c):
        return send(sendx.at[c], recvx.at[c], sx_sem.at[c], rx_sem.at[c], partner)

    def rightward(c):
        return send(stage.at[c], recv_r.at[c], st_sem.at[c], rr_sem.at[c], me + 2)

    def leftward(c):
        return send(stage.at[c], recv_l.at[c], st_sem.at[c], rl_sem.at[c], me - 2)

    compute(z, True)
    receive(1)
    compute(1 + z % 2, False)
    receive(2)
    compute((2 + 3 * z) % 5, False)
    receive(3)
    compute(3 - 3 * (z // 2), False)

    def places(c):
        return [(2 * c + x, 0), (2 * c, 1), (2 * c + 1, 1)]

    def add_across(c):
        across(c).wait()
        acc[2 * c + x, 0] += recvx[c].astype(jnp.float32)

    def add_from(c, copy, ref):
        copy(c).wait_recv()
        for i, (shard, part) in enumerate(places(c)):
            acc[shard, part] += ref[c, i].astype(jnp.float32)

    def pass_on(c, more, copy, ref):
        add_across(c)
        pl.when(more)(lambda: add_from(c, copy, ref))
        for i, (shard, part) in enumerate(places(c)):
            stage[c, i] = acc[shard, part].astype(jnp.bfloat16)
        copy(c).start()

    for distance in (3, 2, 1):
        pl.when(z + distance <= 3)(
            lambda d=distance: pass_on(z + d, z > 0, rightward, recv_r)
        )
        pl.when(z >= distance)(lambda d=distance: pass_on(z - d, z < 3, leftward, recv_l))
    add_across(z)
    pl.when(z > 0)(lambda: add_from(z, rightward, recv_r))
    pl.when(z < 3)(lambda: add_from(z, leftward, recv_l))
    sendf[...] = acc[partner, 1].astype(jnp.bfloat16)
    last = send(sendf, recvf, f_sem.at[0], f_sem.at[1], partner)
    last.start()
    first_half, second_half = slice(0, half), slice(half, 2 * half)
    o_ref[first_half, :] = (mid_ref[first_half, :].astype(jnp.float32) + acc[me, 0]).astype(
        jnp.bfloat16
    )
    last.wait()
    o_ref[second_half, :] = (
        mid_ref[second_half, :].astype(jnp.float32) + (acc[me, 1] + recvf[...].astype(jnp.float32))
    ).astype(jnp.bfloat16)

    for distance in (3, 2, 1):
        pl.when(z + distance <= 3)(lambda d=distance: rightward(z + d).wait_send())
        pl.when(z >= distance)(lambda d=distance: leftward(z - d).wait_send())
    for cond, shard, part, way in pending:
        if cond is None:
            token_copy(shard, part, way).wait_send()
        else:
            pl.when(cond)(
                lambda shard=shard, part=part, way=way: token_copy(shard, part, way).wait_send()
            )


def moe(normed, gate_dense, mid, gate_proj, up_proj, down_proj):
    rows, width = normed.shape
    local, _, hidden = gate_proj.shape
    half = rows // 2
    high = lax.reduce_precision(gate_dense, 8, 7)
    middle = lax.reduce_precision(gate_dense - high, 8, 7)
    low = gate_dense - high - middle
    pad = jnp.zeros((rows, 128 - 3 * EXPERTS), jnp.bfloat16)
    parts = [normed] + [p.astype(jnp.bfloat16) for p in (high, middle, low)] + [pad]
    message = jnp.concatenate(parts, axis=1)
    vmem = pl.BlockSpec(memory_space=pltpu.VMEM)
    anywhere = pl.BlockSpec(memory_space=pl.ANY)
    bf16, f32 = jnp.bfloat16, jnp.float32
    dma = pltpu.SemaphoreType.DMA
    return pl.pallas_call(
        moe_kernel,
        out_shape=jax.ShapeDtypeStruct((rows, width), bf16),
        in_specs=[vmem, vmem, anywhere, anywhere, anywhere],
        out_specs=vmem,
        scratch_shapes=[
            pltpu.VMEM((local, width, hidden), bf16),
            pltpu.VMEM((local, width, hidden), bf16),
            pltpu.VMEM((local, hidden, width), bf16),
            pltpu.VMEM((8, 2, half, width + 128), bf16),
            pltpu.VMEM((8, 2, half, width), f32),
            pltpu.VMEM((4, half, width), bf16),
            pltpu.VMEM((4, half, width), bf16),
            pltpu.VMEM((4, 3, half, width), bf16),
            pltpu.VMEM((4, 3, half, width), bf16),
            pltpu.VMEM((4, 3, half, width), bf16),
            pltpu.VMEM((half, width), bf16),
            pltpu.VMEM((half, width), bf16),
            dma((local, 3)),
            dma((8, 2, 3)),
            dma((8, 2)),
            dma((4,)),
            dma((4,)),
            dma((4,)),
            dma((4,)),
            dma((4,)),
            dma((2,)),
        ],
        compiler_params=pltpu.CompilerParams(
            collective_id=1, has_side_effects=True, vmem_limit_bytes=58 << 20
        ),
    )(message, mid, gate_proj, up_proj, down_proj)


def attend_kernel(
    q_ref,
    suffix_ref,
    pool_ref,
    cos_ref,
    sin_ref,
    low_ref,
    high_ref,
    packed_ref,
    stream_ref,
    gain_ref,
    proj_hbm,
    mid_ref,
    normed_ref,
    proj,
    q_out,
    q_in,
    q_all,
    p_out,
    p_in,
    s_out,
    s_in,
    vx,
    bounds,
    best,
    acc,
    o_out,
    o_in,
    attended,
    proj_sem,
    qs_sem,
    qr_sem,
    ps_sem,
    pr_sem,
    ss_sem,
    sr_sem,
    os_sem,
    or_sem,
):
    me = lax.axis_index("tok")
    z = me // 2
    x = me % 2
    partner = z * 2 + 1 - x
    rows = q_ref.shape[0]
    half = rows // 2
    page_rows = pool_ref.shape[0]
    width = KVH * HD
    f32, bf16 = jnp.float32, jnp.bfloat16

    proj_copy = pltpu.make_async_copy(proj_hbm, proj, proj_sem)
    proj_copy.start()

    barrier = pltpu.get_barrier_semaphore()
    chunks = [z, 1 + z % 2, (2 + 3 * z) % 5, 3 - 3 * (z // 2)]
    near = [partner]
    for c in chunks[1:]:
        near += [2 * c + x, 2 * c + 1 - x]
    far = near[::-1]
    for peer in near:
        pl.semaphore_signal(
            barrier, inc=1, device_id={"tok": peer}, device_id_type=pl.DeviceIdType.MESH
        )

    def send(src, dst, send_sem, recv_sem, device):
        return pltpu.make_async_remote_copy(
            src_ref=src,
            dst_ref=dst,
            send_sem=send_sem,
            recv_sem=recv_sem,
            device_id={"tok": device},
            device_id_type=pl.DeviceIdType.MESH,
        )

    def exchange(out, into, send_sem, recv_sem):
        def to(peer):
            return send(out.at[peer], into.at[me], send_sem.at[peer], recv_sem.at[me], peer)

        def came(peer):
            return send(out.at[peer], into.at[peer], send_sem.at[peer], recv_sem.at[peer], peer)

        return to, came

    q_to, q_from = exchange(q_out, q_in, qs_sem, qr_sem)
    p_to, p_from = exchange(p_out, p_in, ps_sem, pr_sem)
    s_to, s_from = exchange(s_out, s_in, ss_sem, sr_sem)
    o_to, o_from = exchange(o_out, o_in, os_sem, or_sem)

    def lanes(shape):
        return lax.broadcasted_iota(jnp.int32, shape, 1)

    def turn(v, cosine, sine):
        first = lanes(v.shape) % HD < HD // 2
        swapped = jnp.where(first, pltpu.roll(v, 128 - HD // 2, 1), pltpu.roll(v, HD // 2, 1))
        return (v * cosine + swapped * sine).astype(bf16).astype(f32)

    def mix(left, right):
        return jnp.where(lanes(left.shape) < HD, left, right)

    def flip(v):
        return pltpu.roll(v, HD, 1)

    cosine, sine = cos_ref[page_rows:, :], sin_ref[page_rows:, :]
    for pair in range(QH // 2):
        v = q_ref[:, 128 * pair : 128 * pair + 128].astype(f32)
        v = turn(v, cosine, sine) * (HD**-0.5)
        top, low = v[:half], v[half:]
        for n, packed in ((2 * pair, mix(top, flip(low))), (2 * pair + 1, mix(flip(top), low))):
            q_out[n // RATIO, n % RATIO] = packed.astype(bf16)
    pl.semaphore_wait(barrier, 7)
    for peer in far:
        q_to(peer).start()

    def caches(src, first, table, out, at):
        span = pl.ds(first, 128)
        cosine, sine = cos_ref[pl.ds(table, 128), :], sin_ref[pl.ds(table, 128), :]
        for pair in range(KVH // 2):
            k = src[span, 128 * pair : 128 * pair + 128].astype(f32)
            k = turn(k, cosine, sine)
            v = src[span, width + 128 * pair : width + 128 * pair + 128].astype(f32)
            out[2 * pair, span, :] = mix(k, flip(v)).astype(bf16)
            out[2 * pair + 1, span, :] = mix(flip(k), v).astype(bf16)

    caches(suffix_ref, 0, page_rows, s_out, 0)
    for peer in far:
        s_to(peer).start()

    def prepare(i, carry):
        first = pl.multiple_of(i * 128, 128)
        caches(pool_ref, first, first, p_out, 0)
        return carry

    lax.fori_loop(0, page_rows // 128, prepare, 0)
    for peer in near:
        p_to(peer).start()

    q_in[me] = q_out[me]
    s_in[me] = s_out[me]
    bounds[0] = low_ref[...].astype(f32).T
    bounds[1] = high_ref[...].astype(f32).T

    def column(which, r):
        v = bounds[which]
        return jnp.sum(jnp.where(lanes(v.shape) == r, v, 0.0), axis=1, keepdims=True)

    def values(keys):
        return jnp.where(lanes(keys.shape) < HD, jnp.ones_like(keys), keys)

    def unpack(r):
        for j in range(RATIO):
            v = q_in[r, j].astype(f32)
            zero = jnp.zeros_like(v)
            q_all[r, pl.ds(j * rows, half), :] = mix(v, zero).astype(bf16)
            q_all[r, pl.ds(j * rows + half, half), :] = mix(flip(v), zero).astype(bf16)

    def block(r, keys, count, masked=False, first=False):
        s = lax.dot_general(
            q_all[r], keys, (((1,), (1,)), ((), ())), preferred_element_type=f32
        )
        if masked:
            at = packed_ref[...].astype(f32)
            seen = (at >= column(0, r)) & (at <= column(1, r))
            bias = jnp.where(seen, 0.0, NEG_FILL)
            s = (s.reshape(RATIO, rows, count) + bias[None]).reshape(RATIO * rows, count)
        peak = jnp.max(s, axis=-1, keepdims=True)
        if first:
            top = peak
        else:
            old = best[r][:, :1]
            top = jnp.maximum(old, peak)
        weights = jnp.exp(s - top).astype(bf16)
        total = jnp.dot(weights, vx[:count], preferred_element_type=f32)
        if not first:
            total = acc[r] * jnp.exp(old - top) + total
        acc[r] = total
        best[r] = jnp.broadcast_to(top, (RATIO * rows, 128))

    def step(keys_ref, count, masked=False, first=False, last=False):
        vx[:count] = values(keys_ref())

        def body(i, carry):
            c = lax.rem(z + 1 + i, 4) if last else lax.rem(z + i, 4)
            for side in range(2):
                r = 2 * c + side
                if first:
                    pl.when(r != me)(lambda r=r: q_from(r).wait_recv())
                    unpack(r)
            for side in range(2):
                block(2 * c + side, keys_ref(), count, masked, first)
            if last:
                for side in range(2):
                    r = 2 * c + side
                    for j in range(RATIO):
                        v = acc[r, pl.ds(j * rows, rows), :]
                        v = v / flip(v)
                        o_out[r, j] = mix(flip(v[:half]), v[half:]).astype(bf16)
                    pl.when(r != me)(lambda r=r: o_to(r).start())
            return carry

        lax.fori_loop(0, 4, body, 0)

    step(lambda: p_out[me], page_rows, first=True)
    for peer in near:
        s_from(peer).wait_recv()
    step(lambda: s_in[...].reshape(8 * rows, 128), 8 * rows, masked=True)
    p_from(partner).wait_recv()
    step(lambda: p_in[partner], page_rows)
    for i in range(1, 4):
        c = chunks[i]
        p_from(2 * c + x).wait_recv()
        p_from(2 * c + 1 - x).wait_recv()
        step(
            lambda c=c: p_in[pl.ds(2 * c, 2)].reshape(2 * page_rows, 128),
            2 * page_rows,
            last=i == 3,
        )
    o_in[me] = o_out[me]
    for peer in far:
        o_from(peer).wait_recv()
    for pair in range(QH // 2):
        n, m = 2 * pair, 2 * pair + 1
        one = o_in[n // RATIO, n % RATIO].astype(f32)
        two = o_in[m // RATIO, m % RATIO].astype(f32)
        span = slice(128 * pair, 128 * pair + 128)
        attended[:half, span] = mix(one, flip(two)).astype(bf16)
        attended[half:, span] = mix(flip(one), two).astype(bf16)
    proj_copy.wait()
    for first in range(0, proj.shape[1], 512):
        span = slice(first, first + 512)
        mid_ref[:, span] = (
            stream_ref[:, span].astype(f32)
            + jnp.dot(attended[...], proj[:, span], preferred_element_type=f32)
        ).astype(bf16)
    mid = mid_ref[...].astype(f32)
    normed_ref[...] = (
        mid * lax.rsqrt(jnp.mean(mid * mid, axis=-1, keepdims=True) + 1e-05) * gain_ref[...]
    ).astype(bf16)
    for to in (q_to, s_to, p_to, o_to):
        for peer in near:
            to(peer).wait_send()


def attend(q, suffix, pool, positions, low, high, packed, stream, gain, proj):
    rows = q.shape[0]
    half_dim = HD // 2
    frequency = ROPE_BASE ** (-jnp.arange(half_dim, dtype=jnp.float32) / half_dim)
    angles = positions.astype(jnp.float32)[:, None] * frequency[None, :]
    cosine, sine = jnp.cos(angles), jnp.sin(angles)
    cosine = jnp.concatenate([cosine] * 4, axis=1)
    sine = jnp.concatenate([-sine, sine] * 2, axis=1)
    page_rows = pool.shape[0]
    vmem = pl.BlockSpec(memory_space=pltpu.VMEM)
    bf16, f32 = jnp.bfloat16, jnp.float32
    dma = pltpu.SemaphoreType.DMA
    out = jax.ShapeDtypeStruct(stream.shape, bf16)
    return pl.pallas_call(
        attend_kernel,
        out_shape=(out, out),
        in_specs=[vmem] * 10 + [pl.BlockSpec(memory_space=pl.ANY)],
        out_specs=(vmem, vmem),
        scratch_shapes=[
            pltpu.VMEM(proj.shape, bf16),
            pltpu.VMEM((8, RATIO, rows // 2, 128), bf16),
            pltpu.VMEM((8, RATIO, rows // 2, 128), bf16),
            pltpu.VMEM((8, RATIO * rows, 128), bf16),
            pltpu.VMEM((8, page_rows, 128), bf16),
            pltpu.VMEM((8, page_rows, 128), bf16),
            pltpu.VMEM((8, rows, 128), bf16),
            pltpu.VMEM((8, rows, 128), bf16),
            pltpu.VMEM((2 * page_rows, 128), bf16),
            pltpu.VMEM((2, rows, 8), f32),
            pltpu.VMEM((8, RATIO * rows, 128), f32),
            pltpu.VMEM((8, RATIO * rows, 128), f32),
            pltpu.VMEM((8, RATIO, rows // 2, 128), bf16),
            pltpu.VMEM((8, RATIO, rows // 2, 128), bf16),
            pltpu.VMEM(q.shape, bf16),
            dma(()),
        ]
        + [dma((8,))] * 8,
        compiler_params=pltpu.CompilerParams(
            collective_id=2, has_side_effects=True, vmem_limit_bytes=58 << 20
        ),
    )(
        q,
        suffix,
        pool,
        cosine,
        sine,
        low.reshape(8, rows),
        high.reshape(8, rows),
        packed.reshape(1, 8 * rows),
        stream,
        gain.reshape(1, -1),
        proj,
    )


def shards(
    queries,
    suffix_cache,
    stream_in,
    page_pool,
    page_table,
    segment_ids,
    dealing,
    out_proj,
    norm_gain,
    expert_ids,
    expert_gates,
    gate_proj,
    up_proj,
    down_proj,
):
    tok_count = lax.axis_size("tok")
    tok_index = lax.axis_index("tok")
    rows_dev = queries.shape[1]
    width = KVH * HD
    table = page_table[0]
    pages_all = table.shape[0]
    pages_dev = page_pool.shape[1]
    page_len = page_pool.shape[2]
    pool_rows = pages_dev * page_len
    prefix_len = pages_all * page_len
    repeats = tok_count // KVH
    head_groups = [[r * KVH + h for h in range(KVH)] for r in range(repeats)]
    same_head = [[r * KVH + h for r in range(repeats)] for h in range(KVH)]
    sub = dict(axis_index_groups=head_groups) if repeats > 1 else {}

    gate_dense = jnp.sum(
        jnp.where(
            expert_ids[0][:, :, None] == jnp.arange(EXPERTS, dtype=jnp.int32)[None, None, :],
            expert_gates[0][:, :, None],
            0.0,
        ),
        axis=1,
    )

    my_slots = tok_index * pages_dev + jnp.arange(pages_dev, dtype=jnp.int32)
    logical_page = jnp.sum(
        jnp.where(
            table[:, None] == my_slots[None, :],
            jnp.arange(pages_all, dtype=jnp.int32)[:, None],
            0,
        ),
        axis=0,
    )
    pool_positions = (
        logical_page[:, None] * page_len + jnp.arange(page_len, dtype=jnp.int32)[None, :]
    ).reshape(-1)
    dealt = dealing[0]
    requests = jnp.arange(REQS, dtype=jnp.int32)
    starts = jnp.sum((segment_ids[0][:, None] < requests[None, :]).astype(jnp.int32), axis=0)
    low_all = jnp.max(
        jnp.where(starts[None, :] <= dealt[:, None], starts[None, :], 0), axis=1
    )
    my_start = tok_index * rows_dev
    my_dealt = lax.dynamic_slice_in_dim(dealt, my_start, rows_dev)
    my_low = lax.dynamic_slice_in_dim(low_all, my_start, rows_dev)
    my_positions = prefix_len + my_dealt - my_low

    if tok_count == 8:
        mid_round, normed = attend(
            queries[0],
            suffix_cache[0],
            page_pool.reshape(pool_rows, 2 * width),
            jnp.concatenate([pool_positions, my_positions]),
            low_all,
            dealt,
            dealt,
            stream_in[0],
            norm_gain,
            out_proj,
        )
        return moe(normed, gate_dense, mid_round, gate_proj, up_proj, down_proj)[None]

    cache = jnp.concatenate([page_pool.reshape(pool_rows, 2 * width), suffix_cache[0]], axis=0)
    positions = jnp.concatenate([pool_positions, my_positions])
    count = pool_rows + rows_dev
    keys = rotate(cache[:, :width].reshape(count, KVH, HD), positions)
    values = cache[:, width:].reshape(count, KVH, HD)
    outgoing = jnp.concatenate([keys, values], axis=-1).transpose(1, 0, 2)
    arrived = lax.all_to_all(outgoing, "tok", split_axis=0, concat_axis=0, tiled=True, **sub)
    if repeats > 1:
        arrived = lax.all_gather(
            arrived, "tok", axis=0, tiled=True, axis_index_groups=same_head
        )
    kv = jnp.concatenate(
        [
            arrived[:, :pool_rows].reshape(-1, 2 * HD),
            arrived[:, pool_rows:].reshape(-1, 2 * HD),
        ],
        axis=0,
    )

    half = rows_dev // 2
    roped = rotate(queries[0].reshape(rows_dev, QH, HD), my_positions)
    packed_q = (
        roped.reshape(2, half, KVH, RATIO, HD)
        .transpose(2, 3, 1, 0, 4)
        .reshape(KVH, RATIO, half, 2 * HD)
    )
    got_q = lax.all_to_all(packed_q, "tok", split_axis=0, concat_axis=0, tiled=True, **sub)
    got_q = jnp.concatenate([got_q[..., :HD], got_q[..., HD:]], axis=2)
    got_q = jnp.pad(got_q, ((0, 0), (0, 0), (0, 0), (0, HD)))
    row_count = KVH * rows_dev
    first_row = (tok_index // KVH) * row_count
    low_q = lax.dynamic_slice_in_dim(low_all, first_row, row_count)
    high_q = lax.dynamic_slice_in_dim(dealt, first_row, row_count)
    out = attention(got_q, kv, low_q, high_q, dealt, prefix_len)
    back = lax.all_to_all(out, "tok", split_axis=0, concat_axis=0, tiled=True, **sub)
    attended = (
        back.reshape(KVH, RATIO, half, 2, HD)
        .transpose(3, 2, 0, 1, 4)
        .reshape(rows_dev, QH * HD)
    )

    mid_round = lax.optimization_barrier(
        (
            stream_in[0].astype(jnp.float32)
            + jnp.dot(attended, out_proj, preferred_element_type=jnp.float32)
        ).astype(jnp.bfloat16)
    )
    mid_float = mid_round.astype(jnp.float32)
    normed = (
        mid_float
        * lax.rsqrt(jnp.mean(mid_float * mid_float, axis=-1, keepdims=True) + 1e-05)
        * norm_gain
    ).astype(jnp.bfloat16)

    local = gate_proj.shape[0]
    gates_all = lax.all_gather(gate_dense, "tok", axis=0, tiled=True)
    gates_mine = lax.dynamic_slice_in_dim(gates_all, tok_index * local, local, axis=1)
    gates_mine = gates_mine.T.reshape(local, tok_count * rows_dev, 1)
    tokens = lax.all_gather(normed, "tok", axis=0, tiled=True)
    sums = expert_sums(tokens, gates_mine, gate_proj, up_proj, down_proj)
    mixed = lax.psum_scatter(sums, "tok", scatter_dimension=0, tiled=True)
    return (mid_float + mixed.astype(jnp.float32)).astype(jnp.bfloat16)[None]


def solution(mesh):
    placed = (
        P("group", "tok", None),
        P("group", "tok", None),
        P("group", "tok", None),
        P("group", "tok", None, None),
        P("group", None),
        P("group", None),
        P("group", None),
        P(),
        P(),
        P("group", "tok", None),
        P("group", "tok", None),
        P("tok", None, None),
        P("tok", None, None),
        P("tok", None, None),
    )
    return jax.shard_map(
        shards, mesh=mesh, in_specs=placed, out_specs=P("group", "tok", None), check_vma=False
    )
```

```python
import functools

import jax
import jax.numpy as jnp
from jax import lax
from jax.experimental import pallas as pl
from jax.experimental.pallas import tpu as pltpu
from jax.sharding import PartitionSpec as P

QH = 24
KVH = 8
HD = 64
RATIO = QH // KVH
EXPERTS = 32
REQS = 16
CAP = 40
ROPE_BASE = 10000.0
NEG_FILL = -1e30
KEY_CHUNK = 1024


def rotate(vectors, positions):
    half_dim = vectors.shape[-1] // 2
    frequency = ROPE_BASE ** (-jnp.arange(half_dim, dtype=jnp.float32) / half_dim)
    angles = positions.astype(jnp.float32)[:, None] * frequency[None, :]
    cosine = jnp.cos(angles)[:, None, :]
    sine_part = jnp.sin(angles)[:, None, :]
    first_half = vectors[..., :half_dim].astype(jnp.float32)
    second = vectors[..., half_dim:].astype(jnp.float32)
    joined = jnp.concatenate(
        [first_half * cosine - second * sine_part, first_half * sine_part + second * cosine],
        axis=-1,
    )
    return joined.astype(jnp.bfloat16)


def attention_kernel(prefix_len, q_ref, kv_ref, lo_ref, hi_ref, pk_ref, o_ref, vx_ref):
    keys = kv_ref.shape[0]
    rows = q_ref.shape[2]

    @pl.when(pl.program_id(0) == 0)
    def _():
        lane = lax.broadcasted_iota(jnp.int32, kv_ref.shape, 1)
        vx_ref[...] = jnp.where(lane < HD, jnp.ones_like(kv_ref), kv_ref[...])

    q = q_ref[0].reshape(RATIO * rows, 2 * HD)
    best = jnp.full((RATIO * rows, 1), NEG_FILL, jnp.float32)
    accum = jnp.zeros((RATIO * rows, 2 * HD), jnp.float32)
    scale = HD ** (-0.5)
    for first in range(0, keys, KEY_CHUNK):
        part = slice(first, first + KEY_CHUNK)
        scores = (
            lax.dot_general(
                q, kv_ref[part, :], (((1,), (1,)), ((), ())), preferred_element_type=jnp.float32
            )
            * scale
        )
        if first >= prefix_len:
            pk = pk_ref[:, first - prefix_len : first - prefix_len + KEY_CHUNK]
            seen = (pk >= lo_ref[0]) & (pk <= hi_ref[0])
            seen = jnp.concatenate([seen.astype(jnp.float32)] * RATIO, axis=0) > 0.5
            scores = jnp.where(seen, scores, NEG_FILL)
        new_best = jnp.maximum(best, jnp.max(scores, axis=-1, keepdims=True))
        weights = jnp.exp(scores - new_best).astype(jnp.bfloat16)
        factor = jnp.exp(best - new_best)
        accum = accum * factor + jnp.dot(
            weights, vx_ref[part, :], preferred_element_type=jnp.float32
        )
        best = new_best
    out = (accum[:, HD:] / accum[:, :HD]).astype(jnp.bfloat16).reshape(RATIO, rows, HD)
    o_ref[0] = jnp.concatenate([out[:, : rows // 2], out[:, rows // 2 :]], axis=-1)


def attention(q, kv, low, high, packed, prefix_len):
    sources, _, rows, _ = q.shape
    keys = kv.shape[0]
    suffix = keys - prefix_len
    return pl.pallas_call(
        functools.partial(attention_kernel, prefix_len),
        out_shape=jax.ShapeDtypeStruct((sources, RATIO, rows // 2, 2 * HD), jnp.bfloat16),
        grid=(sources,),
        in_specs=[
            pl.BlockSpec((1, RATIO, rows, 2 * HD), lambda i: (i, 0, 0, 0)),
            pl.BlockSpec((keys, 2 * HD), lambda i: (0, 0)),
            pl.BlockSpec((1, rows, 1), lambda i: (i, 0, 0)),
            pl.BlockSpec((1, rows, 1), lambda i: (i, 0, 0)),
            pl.BlockSpec((1, suffix), lambda i: (0, 0)),
        ],
        out_specs=pl.BlockSpec((1, RATIO, rows // 2, 2 * HD), lambda i: (i, 0, 0, 0)),
        scratch_shapes=[pltpu.VMEM((keys, 2 * HD), jnp.bfloat16)],
        compiler_params=pltpu.CompilerParams(vmem_limit_bytes=48 << 20),
    )(q, kv, low.reshape(sources, rows, 1), high.reshape(sources, rows, 1), packed.reshape(1, suffix))


def expert_kernel(x_ref, gates_ref, gate_ref, up_ref, down_ref, o_ref, acc_ref):
    expert = pl.program_id(1)
    x = x_ref[...]
    gate_vals = jnp.dot(x, gate_ref[0], preferred_element_type=jnp.float32)
    up_vals = jnp.dot(x, up_ref[0], preferred_element_type=jnp.float32)
    hidden = (gate_vals / (1.0 + jnp.exp(-gate_vals)) * up_vals).astype(jnp.bfloat16)
    produced = jnp.dot(hidden, down_ref[0], preferred_element_type=jnp.float32)
    term = gates_ref[0] * produced.astype(jnp.bfloat16).astype(jnp.float32)

    @pl.when(expert == 0)
    def _():
        acc_ref[...] = term

    @pl.when(expert > 0)
    def _():
        acc_ref[...] += term

    @pl.when(expert == pl.num_programs(1) - 1)
    def _():
        o_ref[...] = acc_ref[...].astype(jnp.bfloat16)


def expert_sums(x, gates, gate_proj, up_proj, down_proj):
    rows, width = x.shape
    experts, _, hidden = gate_proj.shape
    block = min(512, rows)
    return pl.pallas_call(
        expert_kernel,
        out_shape=jax.ShapeDtypeStruct((rows, width), jnp.bfloat16),
        grid=(rows // block, experts),
        in_specs=[
            pl.BlockSpec((block, width), lambda i, e: (i, 0)),
            pl.BlockSpec((1, block, 1), lambda i, e: (e, i, 0)),
            pl.BlockSpec((1, width, hidden), lambda i, e: (e, 0, 0)),
            pl.BlockSpec((1, width, hidden), lambda i, e: (e, 0, 0)),
            pl.BlockSpec((1, hidden, width), lambda i, e: (e, 0, 0)),
        ],
        out_specs=pl.BlockSpec((block, width), lambda i, e: (i, 0)),
        scratch_shapes=[pltpu.VMEM((block, width), jnp.float32)],
        compiler_params=pltpu.CompilerParams(vmem_limit_bytes=56 << 20),
    )(x, gates, gate_proj, up_proj, down_proj)


def moe_kernel(
    x_ref,
    codes_ref,
    mid_ref,
    wg_hbm,
    wu_hbm,
    wd_hbm,
    o_ref,
    wg,
    wu,
    wd,
    buf,
    acc,
    picked,
    produced,
    spread,
    sendx,
    recvx,
    stage,
    recv_out,
    recv_in,
    sendf,
    recvf,
    w_sem,
    ag_send,
    ag_recv,
    sx_sem,
    rx_sem,
    st_sem,
    ro_sem,
    ri_sem,
    f_sem,
):
    me = lax.axis_index("tok")
    z = me // 2
    x = me % 2
    partner = z * 2 + 1 - x
    f32, bf16 = jnp.float32, jnp.bfloat16
    rows, width = mid_ref.shape
    local = wg.shape[0]
    cut = sendx.shape[1]
    tail = rows - cut
    parts = [pl.ds(0, cut), pl.ds(cut, tail)]
    chunks = [z, 1 + z % 2, (2 + 3 * z) % 5, 3 - 3 * (z // 2)]
    inner = (z + 1) // 2 % 2 == 1
    outer = (z + 1) // 2 % 2 == 0
    toward = me + 2 - 4 * (z // 2)
    outside = me - 2 + 4 * (z // 2)

    def weight_copies(e):
        return [
            pltpu.make_async_copy(src.at[e], dst.at[e], w_sem.at[e, i])
            for i, (src, dst) in enumerate([(wg_hbm, wg), (wu_hbm, wu), (wd_hbm, wd)])
        ]

    for e in range(local):
        for copy in weight_copies(e):
            copy.start()

    barrier = pltpu.get_barrier_semaphore()

    def greet(device):
        pl.semaphore_signal(
            barrier, inc=1, device_id={"tok": device}, device_id_type=pl.DeviceIdType.MESH
        )

    greet(partner)
    pl.when(z > 0)(lambda: greet(me - 2))
    pl.when(z < 3)(lambda: greet(me + 2))
    pl.semaphore_wait(barrier, 2 + ((z + 1) // 2) % 2)

    buf[me] = x_ref[...]

    def send(src, dst, send_sem, recv_sem, device):
        return pltpu.make_async_remote_copy(
            src_ref=src,
            dst_ref=dst,
            send_sem=send_sem,
            recv_sem=recv_sem,
            device_id={"tok": device},
            device_id_type=pl.DeviceIdType.MESH,
        )

    def token_copy(shard, part, way):
        device = (partner, me - 2, me + 2)[way]
        return send(
            buf.at[shard, parts[part]],
            buf.at[shard, parts[part]],
            ag_send.at[shard, part, way],
            ag_recv.at[shard, part],
            device,
        )

    pending = []

    def go(cond, shard, part, way):
        if cond is None:
            token_copy(shard, part, way).start()
        else:
            pl.when(cond)(lambda: token_copy(shard, part, way).start())
        pending.append((cond, shard, part, way))

    for part in (1, 0):
        go(None, me, part, 0)
        go(z > 0, me, part, 1)
        go(z < 3, me, part, 2)
    token_copy(partner, 1, 0).wait_recv()
    go(z > 0, partner, 1, 1)
    go(z < 3, partner, 1, 2)
    token_copy(partner, 0, 0).wait_recv()

    def receive(distance):
        sides = [(-1, z >= distance, z < 3, 2), (1, z + distance <= 3, z > 0, 1)]
        for side, there, onward, way in sides:
            pair = 2 * (z + side * distance)
            same, other = pair + x, pair + 1 - x

            def arrived(shard, part, there=there):
                pl.when(there)(lambda: token_copy(shard, part, 0).wait_recv())

            arrived(same, 1)
            go(there & onward, same, 1, way)
            arrived(same, 0)
            go(there, same, 0, 0)
            go(there & onward, same, 0, way)
            arrived(other, 1)
            go(there & onward, other, 1, way)
        for side, there, onward, way in sides:
            other = 2 * (z + side * distance) + 1 - x
            pl.when(there)(lambda other=other: token_copy(other, 0, 0).wait_recv())

    slots = picked.shape[0] // local

    def compute(c, first):
        tokens = buf[pl.ds(2 * c, 2)].reshape(2 * rows, width)
        code = codes_ref[pl.ds(2 * c, 2)].astype(f32)
        code = jnp.concatenate([code[0], code[1]], axis=1)
        shape = (slots, 2 * rows)
        row = lax.broadcasted_iota(jnp.int32, shape, 0).astype(f32)
        second = lax.broadcasted_iota(jnp.int32, (1, 2 * rows), 1) >= rows
        chosen = []
        for e in range(local):
            slot = code[e : e + 1, :]
            place = jnp.where(slot < 0.0, -1.0, jnp.where(second, slot + slots // 2, slot))
            hit = row == place
            chosen.append(jnp.where(hit, 1.0, 0.0).astype(bf16))
            for i in range(2):
                gate = code[(i + 1) * local + e : (i + 1) * local + e + 1, :]
                spread[i, e * slots : (e + 1) * slots, :] = jnp.where(hit, gate, 0.0).astype(bf16)
        picked[...] = jnp.dot(
            jnp.concatenate(chosen, axis=0), tokens, preferred_element_type=f32
        ).astype(bf16)

        def one(e, carry):
            if first:
                for copy in weight_copies(e):
                    copy.wait()
            span = pl.ds(pl.multiple_of(e * slots, 16), slots)
            some = picked[span, :]
            gate_vals = jnp.dot(some, wg[e], preferred_element_type=f32)
            up_vals = jnp.dot(some, wu[e], preferred_element_type=f32)
            hidden = (gate_vals / (1.0 + jnp.exp(-gate_vals)) * up_vals).astype(bf16)
            produced[span, :] = jnp.dot(hidden, wd[e], preferred_element_type=f32).astype(bf16)
            return carry

        lax.fori_loop(0, local, one, 0)
        total = sum(
            lax.dot_general(
                spread[i], produced[...], (((0,), (0,)), ((), ())), preferred_element_type=f32
            )
            for i in range(2)
        )
        acc[pl.ds(2 * c, 2)] = total.reshape(2, rows, width)
        sendx[c] = acc[2 * c + 1 - x, parts[0]].astype(bf16)
        across(c).start()

    def across(c):
        return send(sendx.at[c], recvx.at[c], sx_sem.at[c], rx_sem.at[c], partner)

    def add_across(c):
        across(c).wait()
        acc[2 * c + x, parts[0]] += recvx[c].astype(f32)

    def place(c, piece):
        if piece == 0:
            return acc.at[2 * c + x, parts[0]], pl.ds(0, cut)
        return acc.at[2 * c + piece - 1, parts[1]], pl.ds(cut + (piece - 1) * tail, tail)

    def hop(c, piece, into, sem, device):
        span = place(c, piece)[1]
        return send(
            stage.at[c, span], into.at[c, span], st_sem.at[c, piece], sem.at[c, piece], device
        )

    def outward_hop(c, piece):
        return hop(c, piece, recv_out, ro_sem, toward)

    def center_hop(c, piece):
        return hop(c, piece, recv_in, ri_sem, toward)

    def back_hop(c, piece):
        return hop(c, piece, recv_in, ri_sem, outside)

    def emit(c, piece, hop_of):
        part, span = place(c, piece)
        stage[c, span] = part[...].astype(bf16)
        hop_of(c, piece).start()

    def fold(c, piece, hop_of, ref):
        hop_of(c, piece).wait_recv()
        part, span = place(c, piece)
        part[...] += ref[c, span].astype(f32)

    def relay(c, came, ref, hop_of):
        for piece in (1, 2, 0):
            if piece == 0:
                add_across(c)
            fold(c, piece, came, ref)
            emit(c, piece, hop_of)

    def early(c):
        emit(c, 1, outward_hop)
        emit(c, 2, outward_hop)

    def late(c):
        add_across(c)
        emit(c, 0, outward_hop)

    compute(chunks[0], True)
    receive(1)
    compute(chunks[1], False)
    pl.when(outer)(lambda: early(chunks[1]))
    receive(2)
    pl.when(outer)(lambda: late(chunks[1]))
    compute(chunks[2], False)
    pl.when(outer)(lambda: early(chunks[2]))
    receive(3)
    pl.when(outer)(lambda: late(chunks[2]))
    compute(chunks[3], False)
    pl.when(outer)(lambda: early(chunks[3]))
    pl.when(outer)(lambda: late(chunks[3]))

    @pl.when(inner)
    def _():
        relay(chunks[1], outward_hop, recv_out, center_hop)
        relay(chunks[3], outward_hop, recv_out, center_hop)
        relay(chunks[2], center_hop, recv_in, back_hop)

    add_across(z)
    for piece in (1, 2, 0):
        pl.when(inner)(lambda piece=piece: fold(z, piece, outward_hop, recv_out))
        fold(z, piece, center_hop, recv_in)
        if piece == 2:
            sendf[...] = acc[partner, parts[1]].astype(bf16)
            last = send(sendf, recvf, f_sem.at[0], f_sem.at[1], partner)
            last.start()
    o_ref[:cut, :] = (mid_ref[:cut, :].astype(f32) + acc[me, parts[0]]).astype(bf16)
    last.wait()
    o_ref[cut:, :] = (
        mid_ref[cut:, :].astype(f32) + (acc[me, parts[1]] + recvf[...].astype(f32))
    ).astype(bf16)

    for c in chunks[1:]:
        for piece in range(3):
            center_hop(c, piece).wait_send()
    for cond, shard, part, way in pending:
        if cond is None:
            token_copy(shard, part, way).wait_send()
        else:
            pl.when(cond)(
                lambda shard=shard, part=part, way=way: token_copy(shard, part, way).wait_send()
            )


def moe(normed, codes, mid, gate_proj, up_proj, down_proj):
    rows, width = normed.shape
    local, _, hidden = gate_proj.shape
    cut = 5 * rows // 8
    legs = 2 * rows - cut
    vmem = pl.BlockSpec(memory_space=pltpu.VMEM)
    anywhere = pl.BlockSpec(memory_space=pl.ANY)
    bf16, f32 = jnp.bfloat16, jnp.float32
    dma = pltpu.SemaphoreType.DMA
    return pl.pallas_call(
        moe_kernel,
        out_shape=jax.ShapeDtypeStruct((rows, width), bf16),
        in_specs=[vmem, vmem, vmem, anywhere, anywhere, anywhere],
        out_specs=vmem,
        scratch_shapes=[
            pltpu.VMEM((local, width, hidden), bf16),
            pltpu.VMEM((local, width, hidden), bf16),
            pltpu.VMEM((local, hidden, width), bf16),
            pltpu.VMEM((8, rows, width), bf16),
            pltpu.VMEM((8, rows, width), f32),
            pltpu.VMEM((local * 2 * CAP, width), bf16),
            pltpu.VMEM((local * 2 * CAP, width), bf16),
            pltpu.VMEM((2, local * 2 * CAP, 2 * rows), bf16),
            pltpu.VMEM((4, cut, width), bf16),
            pltpu.VMEM((4, cut, width), bf16),
            pltpu.VMEM((4, legs, width), bf16),
            pltpu.VMEM((4, legs, width), bf16),
            pltpu.VMEM((4, legs, width), bf16),
            pltpu.VMEM((rows - cut, width), bf16),
            pltpu.VMEM((rows - cut, width), bf16),
            dma((local, 3)),
            dma((8, 2, 3)),
            dma((8, 2)),
            dma((4,)),
            dma((4,)),
            dma((4, 3)),
            dma((4, 3)),
            dma((4, 3)),
            dma((2,)),
        ],
        compiler_params=pltpu.CompilerParams(
            collective_id=1, has_side_effects=True, vmem_limit_bytes=58 << 20
        ),
    )(normed, codes, mid, gate_proj, up_proj, down_proj)


def route(ids_ref, gates_ref, out):
    ids = ids_ref[...].astype(jnp.float32).T
    gates = gates_ref[...].T
    devices = out.shape[0]
    local = EXPERTS // devices
    rows = ids.shape[1]
    expert = lax.broadcasted_iota(jnp.int32, (EXPERTS, rows), 0).astype(jnp.float32)
    chosen = jnp.zeros((EXPERTS, rows), jnp.float32)
    gate = jnp.zeros((EXPERTS, rows), jnp.float32)
    for k in range(ids.shape[0]):
        hit = expert == ids[k : k + 1, :]
        chosen = jnp.where(hit, 1.0, chosen)
        gate = jnp.where(hit, gates[k : k + 1, :], gate)
    row = lax.broadcasted_iota(jnp.int32, (rows, rows), 0)
    column = lax.broadcasted_iota(jnp.int32, (rows, rows), 1)
    before = jnp.where(row < column, 1.0, 0.0).astype(jnp.bfloat16)
    slot = jnp.dot(chosen.astype(jnp.bfloat16), before, preferred_element_type=jnp.float32)
    slot = jnp.where(chosen > 0.5, slot, -1.0)
    high = gate.astype(jnp.bfloat16).astype(jnp.float32)
    rest = gate - high
    for device in range(devices):
        span = slice(device * local, (device + 1) * local)
        out[device] = jnp.concatenate(
            [slot[span], high[span], rest[span], jnp.zeros((16 - 3 * local, rows), jnp.float32)],
            axis=0,
        ).astype(jnp.bfloat16)


def attend_kernel(
    q_ref,
    suffix_ref,
    pool_ref,
    cos_ref,
    sin_ref,
    low_ref,
    high_ref,
    packed_ref,
    stream_ref,
    gain_ref,
    ids_ref,
    gates_ref,
    proj_hbm,
    mid_ref,
    normed_ref,
    codes_ref,
    proj,
    c_out,
    c_in,
    q_out,
    q_in,
    q_all,
    p_out,
    p_in,
    s_out,
    s_in,
    vx,
    bounds,
    best,
    acc,
    o_out,
    o_in,
    attended,
    proj_sem,
    qs_sem,
    qr_sem,
    ps_sem,
    pr_sem,
    ss_sem,
    sr_sem,
    os_sem,
    or_sem,
    cs_sem,
    cr_sem,
):
    me = lax.axis_index("tok")
    z = me // 2
    x = me % 2
    partner = z * 2 + 1 - x
    rows = q_ref.shape[0]
    half = rows // 2
    page_rows = pool_ref.shape[0]
    width = KVH * HD
    f32, bf16 = jnp.float32, jnp.bfloat16

    proj_copy = pltpu.make_async_copy(proj_hbm, proj, proj_sem)
    proj_copy.start()

    barrier = pltpu.get_barrier_semaphore()
    chunks = [z, 1 + z % 2, (2 + 3 * z) % 5, 3 - 3 * (z // 2)]
    near = [partner]
    for c in chunks[1:]:
        near += [2 * c + x, 2 * c + 1 - x]
    far = near[::-1]
    for peer in near:
        pl.semaphore_signal(
            barrier, inc=1, device_id={"tok": peer}, device_id_type=pl.DeviceIdType.MESH
        )

    def send(src, dst, send_sem, recv_sem, device):
        return pltpu.make_async_remote_copy(
            src_ref=src,
            dst_ref=dst,
            send_sem=send_sem,
            recv_sem=recv_sem,
            device_id={"tok": device},
            device_id_type=pl.DeviceIdType.MESH,
        )

    def exchange(out, into, send_sem, recv_sem):
        def to(peer):
            return send(out.at[peer], into.at[me], send_sem.at[peer], recv_sem.at[me], peer)

        def came(peer):
            return send(out.at[peer], into.at[peer], send_sem.at[peer], recv_sem.at[peer], peer)

        return to, came

    q_to, q_from = exchange(q_out, q_in, qs_sem, qr_sem)
    p_to, p_from = exchange(p_out, p_in, ps_sem, pr_sem)
    s_to, s_from = exchange(s_out, s_in, ss_sem, sr_sem)
    o_to, o_from = exchange(o_out, o_in, os_sem, or_sem)
    c_to, c_from = exchange(c_out, c_in, cs_sem, cr_sem)

    def lanes(shape):
        return lax.broadcasted_iota(jnp.int32, shape, 1)

    def turn(v, cosine, sine):
        first = lanes(v.shape) % HD < HD // 2
        swapped = jnp.where(first, pltpu.roll(v, 128 - HD // 2, 1), pltpu.roll(v, HD // 2, 1))
        return (v * cosine + swapped * sine).astype(bf16).astype(f32)

    def mix(left, right):
        return jnp.where(lanes(left.shape) < HD, left, right)

    def flip(v):
        return pltpu.roll(v, HD, 1)

    cosine, sine = cos_ref[page_rows:, :], sin_ref[page_rows:, :]
    for pair in range(QH // 2):
        v = q_ref[:, 128 * pair : 128 * pair + 128].astype(f32)
        v = turn(v, cosine, sine) * (HD**-0.5)
        top, low = v[:half], v[half:]
        for n, packed in ((2 * pair, mix(top, flip(low))), (2 * pair + 1, mix(flip(top), low))):
            q_out[n // RATIO, n % RATIO] = packed.astype(bf16)
    pl.semaphore_wait(barrier, 7)
    for peer in far:
        q_to(peer).start()

    def caches(src, first, table, out, at):
        span = pl.ds(first, 128)
        cosine, sine = cos_ref[pl.ds(table, 128), :], sin_ref[pl.ds(table, 128), :]
        for pair in range(KVH // 2):
            k = src[span, 128 * pair : 128 * pair + 128].astype(f32)
            k = turn(k, cosine, sine)
            v = src[span, width + 128 * pair : width + 128 * pair + 128].astype(f32)
            out[2 * pair, span, :] = mix(k, flip(v)).astype(bf16)
            out[2 * pair + 1, span, :] = mix(flip(k), v).astype(bf16)

    caches(suffix_ref, 0, page_rows, s_out, 0)
    for peer in far:
        s_to(peer).start()

    def prepare(i, carry):
        first = pl.multiple_of(i * 128, 128)
        caches(pool_ref, first, first, p_out, 0)
        return carry

    lax.fori_loop(0, page_rows // 128, prepare, 0)
    for peer in near:
        p_to(peer).start()

    route(ids_ref, gates_ref, c_out)
    for peer in near:
        c_to(peer).start()
    c_in[me] = c_out[me]
    q_in[me] = q_out[me]
    s_in[me] = s_out[me]
    bounds[0] = low_ref[...].astype(f32).T
    bounds[1] = high_ref[...].astype(f32).T

    def column(which, r):
        v = bounds[which]
        return jnp.sum(jnp.where(lanes(v.shape) == r, v, 0.0), axis=1, keepdims=True)

    def values(keys):
        return jnp.where(lanes(keys.shape) < HD, jnp.ones_like(keys), keys)

    def unpack(r):
        for j in range(RATIO):
            v = q_in[r, j].astype(f32)
            zero = jnp.zeros_like(v)
            q_all[r, pl.ds(j * rows, half), :] = mix(v, zero).astype(bf16)
            q_all[r, pl.ds(j * rows + half, half), :] = mix(flip(v), zero).astype(bf16)

    def block(r, keys, count, masked=False, first=False):
        s = lax.dot_general(
            q_all[r], keys, (((1,), (1,)), ((), ())), preferred_element_type=f32
        )
        if masked:
            at = packed_ref[...].astype(f32)
            seen = (at >= column(0, r)) & (at <= column(1, r))
            bias = jnp.where(seen, 0.0, NEG_FILL)
            s = (s.reshape(RATIO, rows, count) + bias[None]).reshape(RATIO * rows, count)
        peak = jnp.max(s, axis=-1, keepdims=True)
        if first:
            top = peak
        else:
            old = best[r][:, :1]
            top = jnp.maximum(old, peak)
        weights = jnp.exp(s - top).astype(bf16)
        total = jnp.dot(weights, vx[:count], preferred_element_type=f32)
        if not first:
            total = acc[r] * jnp.exp(old - top) + total
        acc[r] = total
        best[r] = jnp.broadcast_to(top, (RATIO * rows, 128))

    def step(keys_ref, count, masked=False, first=False, last=False):
        vx[:count] = values(keys_ref())

        def body(i, carry):
            c = lax.rem(z + 1 + i, 4) if last else lax.rem(z + i, 4)
            for side in range(2):
                r = 2 * c + side
                if first:
                    pl.when(r != me)(lambda r=r: q_from(r).wait_recv())
                    unpack(r)
            for side in range(2):
                block(2 * c + side, keys_ref(), count, masked, first)
            if last:
                for side in range(2):
                    r = 2 * c + side
                    for j in range(RATIO):
                        v = acc[r, pl.ds(j * rows, rows), :]
                        v = v / flip(v)
                        o_out[r, j] = mix(flip(v[:half]), v[half:]).astype(bf16)
                    pl.when(r != me)(lambda r=r: o_to(r).start())
            return carry

        lax.fori_loop(0, 4, body, 0)

    step(lambda: p_out[me], page_rows, first=True)
    for peer in near:
        s_from(peer).wait_recv()
    step(lambda: s_in[...].reshape(8 * rows, 128), 8 * rows, masked=True)
    p_from(partner).wait_recv()
    step(lambda: p_in[partner], page_rows)
    for i in range(1, 4):
        c = chunks[i]
        p_from(2 * c + x).wait_recv()
        p_from(2 * c + 1 - x).wait_recv()
        step(
            lambda c=c: p_in[pl.ds(2 * c, 2)].reshape(2 * page_rows, 128),
            2 * page_rows,
            last=i == 3,
        )
    o_in[me] = o_out[me]
    for peer in far:
        o_from(peer).wait_recv()
    for pair in range(QH // 2):
        n, m = 2 * pair, 2 * pair + 1
        one = o_in[n // RATIO, n % RATIO].astype(f32)
        two = o_in[m // RATIO, m % RATIO].astype(f32)
        span = slice(128 * pair, 128 * pair + 128)
        attended[:half, span] = mix(one, flip(two)).astype(bf16)
        attended[half:, span] = mix(flip(one), two).astype(bf16)
    proj_copy.wait()
    for first in range(0, proj.shape[1], 512):
        span = slice(first, first + 512)
        mid_ref[:, span] = (
            stream_ref[:, span].astype(f32)
            + jnp.dot(attended[...], proj[:, span], preferred_element_type=f32)
        ).astype(bf16)
    mid = mid_ref[...].astype(f32)
    normed_ref[...] = (
        mid * lax.rsqrt(jnp.mean(mid * mid, axis=-1, keepdims=True) + 1e-05) * gain_ref[...]
    ).astype(bf16)
    for peer in near:
        c_from(peer).wait_recv()
    codes_ref[...] = c_in[...]
    for to in (q_to, s_to, p_to, o_to, c_to):
        for peer in near:
            to(peer).wait_send()


def attend(q, suffix, pool, positions, low, high, packed, stream, gain, ids, gates, proj):
    rows = q.shape[0]
    half_dim = HD // 2
    frequency = ROPE_BASE ** (-jnp.arange(half_dim, dtype=jnp.float32) / half_dim)
    angles = positions.astype(jnp.float32)[:, None] * frequency[None, :]
    cosine, sine = jnp.cos(angles), jnp.sin(angles)
    cosine = jnp.concatenate([cosine] * 4, axis=1)
    sine = jnp.concatenate([-sine, sine] * 2, axis=1)
    page_rows = pool.shape[0]
    vmem = pl.BlockSpec(memory_space=pltpu.VMEM)
    bf16, f32 = jnp.bfloat16, jnp.float32
    dma = pltpu.SemaphoreType.DMA
    out = jax.ShapeDtypeStruct(stream.shape, bf16)
    return pl.pallas_call(
        attend_kernel,
        out_shape=(out, out, jax.ShapeDtypeStruct((8, 16, rows), bf16)),
        in_specs=[vmem] * 12 + [pl.BlockSpec(memory_space=pl.ANY)],
        out_specs=(vmem, vmem, vmem),
        scratch_shapes=[
            pltpu.VMEM(proj.shape, bf16),
            pltpu.VMEM((8, 16, rows), bf16),
            pltpu.VMEM((8, 16, rows), bf16),
            pltpu.VMEM((8, RATIO, rows // 2, 128), bf16),
            pltpu.VMEM((8, RATIO, rows // 2, 128), bf16),
            pltpu.VMEM((8, RATIO * rows, 128), bf16),
            pltpu.VMEM((8, page_rows, 128), bf16),
            pltpu.VMEM((8, page_rows, 128), bf16),
            pltpu.VMEM((8, rows, 128), bf16),
            pltpu.VMEM((8, rows, 128), bf16),
            pltpu.VMEM((2 * page_rows, 128), bf16),
            pltpu.VMEM((2, rows, 8), f32),
            pltpu.VMEM((8, RATIO * rows, 128), f32),
            pltpu.VMEM((8, RATIO * rows, 128), f32),
            pltpu.VMEM((8, RATIO, rows // 2, 128), bf16),
            pltpu.VMEM((8, RATIO, rows // 2, 128), bf16),
            pltpu.VMEM(q.shape, bf16),
            dma(()),
        ]
        + [dma((8,))] * 10,
        compiler_params=pltpu.CompilerParams(
            collective_id=2, has_side_effects=True, vmem_limit_bytes=58 << 20
        ),
    )(
        q,
        suffix,
        pool,
        cosine,
        sine,
        low.reshape(8, rows),
        high.reshape(8, rows),
        packed.reshape(1, 8 * rows),
        stream,
        gain.reshape(1, -1),
        ids,
        gates,
        proj,
    )


def shards(
    queries,
    suffix_cache,
    stream_in,
    page_pool,
    page_table,
    segment_ids,
    dealing,
    out_proj,
    norm_gain,
    expert_ids,
    expert_gates,
    gate_proj,
    up_proj,
    down_proj,
):
    tok_count = lax.axis_size("tok")
    tok_index = lax.axis_index("tok")
    rows_dev = queries.shape[1]
    width = KVH * HD
    table = page_table[0]
    pages_all = table.shape[0]
    pages_dev = page_pool.shape[1]
    page_len = page_pool.shape[2]
    pool_rows = pages_dev * page_len
    prefix_len = pages_all * page_len
    repeats = tok_count // KVH
    head_groups = [[r * KVH + h for h in range(KVH)] for r in range(repeats)]
    same_head = [[r * KVH + h for r in range(repeats)] for h in range(KVH)]
    sub = dict(axis_index_groups=head_groups) if repeats > 1 else {}

    gate_dense = jnp.sum(
        jnp.where(
            expert_ids[0][:, :, None] == jnp.arange(EXPERTS, dtype=jnp.int32)[None, None, :],
            expert_gates[0][:, :, None],
            0.0,
        ),
        axis=1,
    )

    my_slots = tok_index * pages_dev + jnp.arange(pages_dev, dtype=jnp.int32)
    logical_page = jnp.sum(
        jnp.where(
            table[:, None] == my_slots[None, :],
            jnp.arange(pages_all, dtype=jnp.int32)[:, None],
            0,
        ),
        axis=0,
    )
    pool_positions = (
        logical_page[:, None] * page_len + jnp.arange(page_len, dtype=jnp.int32)[None, :]
    ).reshape(-1)
    dealt = dealing[0]
    requests = jnp.arange(REQS, dtype=jnp.int32)
    starts = jnp.sum((segment_ids[0][:, None] < requests[None, :]).astype(jnp.int32), axis=0)
    low_all = jnp.max(
        jnp.where(starts[None, :] <= dealt[:, None], starts[None, :], 0), axis=1
    )
    my_start = tok_index * rows_dev
    my_dealt = lax.dynamic_slice_in_dim(dealt, my_start, rows_dev)
    my_low = lax.dynamic_slice_in_dim(low_all, my_start, rows_dev)
    my_positions = prefix_len + my_dealt - my_low

    if tok_count == 8:
        mid_round, normed, codes = attend(
            queries[0],
            suffix_cache[0],
            page_pool.reshape(pool_rows, 2 * width),
            jnp.concatenate([pool_positions, my_positions]),
            low_all,
            dealt,
            dealt,
            stream_in[0],
            norm_gain,
            expert_ids[0],
            expert_gates[0],
            out_proj,
        )
        return moe(normed, codes, mid_round, gate_proj, up_proj, down_proj)[None]

    cache = jnp.concatenate([page_pool.reshape(pool_rows, 2 * width), suffix_cache[0]], axis=0)
    positions = jnp.concatenate([pool_positions, my_positions])
    count = pool_rows + rows_dev
    keys = rotate(cache[:, :width].reshape(count, KVH, HD), positions)
    values = cache[:, width:].reshape(count, KVH, HD)
    outgoing = jnp.concatenate([keys, values], axis=-1).transpose(1, 0, 2)
    arrived = lax.all_to_all(outgoing, "tok", split_axis=0, concat_axis=0, tiled=True, **sub)
    if repeats > 1:
        arrived = lax.all_gather(
            arrived, "tok", axis=0, tiled=True, axis_index_groups=same_head
        )
    kv = jnp.concatenate(
        [
            arrived[:, :pool_rows].reshape(-1, 2 * HD),
            arrived[:, pool_rows:].reshape(-1, 2 * HD),
        ],
        axis=0,
    )

    half = rows_dev // 2
    roped = rotate(queries[0].reshape(rows_dev, QH, HD), my_positions)
    packed_q = (
        roped.reshape(2, half, KVH, RATIO, HD)
        .transpose(2, 3, 1, 0, 4)
        .reshape(KVH, RATIO, half, 2 * HD)
    )
    got_q = lax.all_to_all(packed_q, "tok", split_axis=0, concat_axis=0, tiled=True, **sub)
    got_q = jnp.concatenate([got_q[..., :HD], got_q[..., HD:]], axis=2)
    got_q = jnp.pad(got_q, ((0, 0), (0, 0), (0, 0), (0, HD)))
    row_count = KVH * rows_dev
    first_row = (tok_index // KVH) * row_count
    low_q = lax.dynamic_slice_in_dim(low_all, first_row, row_count)
    high_q = lax.dynamic_slice_in_dim(dealt, first_row, row_count)
    out = attention(got_q, kv, low_q, high_q, dealt, prefix_len)
    back = lax.all_to_all(out, "tok", split_axis=0, concat_axis=0, tiled=True, **sub)
    attended = (
        back.reshape(KVH, RATIO, half, 2, HD)
        .transpose(3, 2, 0, 1, 4)
        .reshape(rows_dev, QH * HD)
    )

    mid_round = lax.optimization_barrier(
        (
            stream_in[0].astype(jnp.float32)
            + jnp.dot(attended, out_proj, preferred_element_type=jnp.float32)
        ).astype(jnp.bfloat16)
    )
    mid_float = mid_round.astype(jnp.float32)
    normed = (
        mid_float
        * lax.rsqrt(jnp.mean(mid_float * mid_float, axis=-1, keepdims=True) + 1e-05)
        * norm_gain
    ).astype(jnp.bfloat16)

    local = gate_proj.shape[0]
    gates_all = lax.all_gather(gate_dense, "tok", axis=0, tiled=True)
    gates_mine = lax.dynamic_slice_in_dim(gates_all, tok_index * local, local, axis=1)
    gates_mine = gates_mine.T.reshape(local, tok_count * rows_dev, 1)
    tokens = lax.all_gather(normed, "tok", axis=0, tiled=True)
    sums = expert_sums(tokens, gates_mine, gate_proj, up_proj, down_proj)
    mixed = lax.psum_scatter(sums, "tok", scatter_dimension=0, tiled=True)
    return (mid_float + mixed.astype(jnp.float32)).astype(jnp.bfloat16)[None]


def solution(mesh):
    placed = (
        P("group", "tok", None),
        P("group", "tok", None),
        P("group", "tok", None),
        P("group", "tok", None, None),
        P("group", None),
        P("group", None),
        P("group", None),
        P(),
        P(),
        P("group", "tok", None),
        P("group", "tok", None),
        P("tok", None, None),
        P("tok", None, None),
        P("tok", None, None),
    )
    return jax.shard_map(
        shards, mesh=mesh, in_specs=placed, out_specs=P("group", "tok", None), check_vma=False
    )
```

```python
import functools

import jax
import jax.numpy as jnp
from jax import lax
from jax.experimental import pallas as pl
from jax.experimental.pallas import tpu as pltpu
from jax.sharding import PartitionSpec as P

QH = 24
KVH = 8
HD = 64
RATIO = QH // KVH
EXPERTS = 32
REQS = 16
CAP = 40
ROPE_BASE = 10000.0
NEG_FILL = -1e30
KEY_CHUNK = 1024


def rotate(vectors, positions):
    half_dim = vectors.shape[-1] // 2
    frequency = ROPE_BASE ** (-jnp.arange(half_dim, dtype=jnp.float32) / half_dim)
    angles = positions.astype(jnp.float32)[:, None] * frequency[None, :]
    cosine = jnp.cos(angles)[:, None, :]
    sine_part = jnp.sin(angles)[:, None, :]
    first_half = vectors[..., :half_dim].astype(jnp.float32)
    second = vectors[..., half_dim:].astype(jnp.float32)
    joined = jnp.concatenate(
        [first_half * cosine - second * sine_part, first_half * sine_part + second * cosine],
        axis=-1,
    )
    return joined.astype(jnp.bfloat16)


def attention_kernel(prefix_len, q_ref, kv_ref, lo_ref, hi_ref, pk_ref, o_ref, vx_ref):
    keys = kv_ref.shape[0]
    rows = q_ref.shape[2]

    @pl.when(pl.program_id(0) == 0)
    def _():
        lane = lax.broadcasted_iota(jnp.int32, kv_ref.shape, 1)
        vx_ref[...] = jnp.where(lane < HD, jnp.ones_like(kv_ref), kv_ref[...])

    q = q_ref[0].reshape(RATIO * rows, 2 * HD)
    best = jnp.full((RATIO * rows, 1), NEG_FILL, jnp.float32)
    accum = jnp.zeros((RATIO * rows, 2 * HD), jnp.float32)
    scale = HD ** (-0.5)
    for first in range(0, keys, KEY_CHUNK):
        part = slice(first, first + KEY_CHUNK)
        scores = (
            lax.dot_general(
                q, kv_ref[part, :], (((1,), (1,)), ((), ())), preferred_element_type=jnp.float32
            )
            * scale
        )
        if first >= prefix_len:
            pk = pk_ref[:, first - prefix_len : first - prefix_len + KEY_CHUNK]
            seen = (pk >= lo_ref[0]) & (pk <= hi_ref[0])
            seen = jnp.concatenate([seen.astype(jnp.float32)] * RATIO, axis=0) > 0.5
            scores = jnp.where(seen, scores, NEG_FILL)
        new_best = jnp.maximum(best, jnp.max(scores, axis=-1, keepdims=True))
        weights = jnp.exp(scores - new_best).astype(jnp.bfloat16)
        factor = jnp.exp(best - new_best)
        accum = accum * factor + jnp.dot(
            weights, vx_ref[part, :], preferred_element_type=jnp.float32
        )
        best = new_best
    out = (accum[:, HD:] / accum[:, :HD]).astype(jnp.bfloat16).reshape(RATIO, rows, HD)
    o_ref[0] = jnp.concatenate([out[:, : rows // 2], out[:, rows // 2 :]], axis=-1)


def attention(q, kv, low, high, packed, prefix_len):
    sources, _, rows, _ = q.shape
    keys = kv.shape[0]
    suffix = keys - prefix_len
    return pl.pallas_call(
        functools.partial(attention_kernel, prefix_len),
        out_shape=jax.ShapeDtypeStruct((sources, RATIO, rows // 2, 2 * HD), jnp.bfloat16),
        grid=(sources,),
        in_specs=[
            pl.BlockSpec((1, RATIO, rows, 2 * HD), lambda i: (i, 0, 0, 0)),
            pl.BlockSpec((keys, 2 * HD), lambda i: (0, 0)),
            pl.BlockSpec((1, rows, 1), lambda i: (i, 0, 0)),
            pl.BlockSpec((1, rows, 1), lambda i: (i, 0, 0)),
            pl.BlockSpec((1, suffix), lambda i: (0, 0)),
        ],
        out_specs=pl.BlockSpec((1, RATIO, rows // 2, 2 * HD), lambda i: (i, 0, 0, 0)),
        scratch_shapes=[pltpu.VMEM((keys, 2 * HD), jnp.bfloat16)],
        compiler_params=pltpu.CompilerParams(vmem_limit_bytes=48 << 20),
    )(q, kv, low.reshape(sources, rows, 1), high.reshape(sources, rows, 1), packed.reshape(1, suffix))


def expert_kernel(x_ref, gates_ref, gate_ref, up_ref, down_ref, o_ref, acc_ref):
    expert = pl.program_id(1)
    x = x_ref[...]
    gate_vals = jnp.dot(x, gate_ref[0], preferred_element_type=jnp.float32)
    up_vals = jnp.dot(x, up_ref[0], preferred_element_type=jnp.float32)
    hidden = (gate_vals / (1.0 + jnp.exp(-gate_vals)) * up_vals).astype(jnp.bfloat16)
    produced = jnp.dot(hidden, down_ref[0], preferred_element_type=jnp.float32)
    term = gates_ref[0] * produced.astype(jnp.bfloat16).astype(jnp.float32)

    @pl.when(expert == 0)
    def _():
        acc_ref[...] = term

    @pl.when(expert > 0)
    def _():
        acc_ref[...] += term

    @pl.when(expert == pl.num_programs(1) - 1)
    def _():
        o_ref[...] = acc_ref[...].astype(jnp.bfloat16)


def expert_sums(x, gates, gate_proj, up_proj, down_proj):
    rows, width = x.shape
    experts, _, hidden = gate_proj.shape
    block = min(512, rows)
    return pl.pallas_call(
        expert_kernel,
        out_shape=jax.ShapeDtypeStruct((rows, width), jnp.bfloat16),
        grid=(rows // block, experts),
        in_specs=[
            pl.BlockSpec((block, width), lambda i, e: (i, 0)),
            pl.BlockSpec((1, block, 1), lambda i, e: (e, i, 0)),
            pl.BlockSpec((1, width, hidden), lambda i, e: (e, 0, 0)),
            pl.BlockSpec((1, width, hidden), lambda i, e: (e, 0, 0)),
            pl.BlockSpec((1, hidden, width), lambda i, e: (e, 0, 0)),
        ],
        out_specs=pl.BlockSpec((block, width), lambda i, e: (i, 0)),
        scratch_shapes=[pltpu.VMEM((block, width), jnp.float32)],
        compiler_params=pltpu.CompilerParams(vmem_limit_bytes=56 << 20),
    )(x, gates, gate_proj, up_proj, down_proj)


def moe_kernel(
    x_ref,
    codes_ref,
    mid_ref,
    wg_hbm,
    wu_hbm,
    wd_hbm,
    o_ref,
    wg,
    wu,
    wd,
    buf,
    acc,
    picked,
    produced,
    spread,
    sendx,
    recvx,
    stage,
    recv_out,
    recv_in,
    sendf,
    recvf,
    w_sem,
    ag_send,
    ag_recv,
    sx_sem,
    rx_sem,
    st_sem,
    ro_sem,
    ri_sem,
    f_sem,
):
    me = lax.axis_index("tok")
    z = me // 2
    x = me % 2
    partner = z * 2 + 1 - x
    f32, bf16 = jnp.float32, jnp.bfloat16
    rows, width = mid_ref.shape
    local = wg.shape[0]
    cut = sendx.shape[1]
    tail = rows - cut
    parts = [pl.ds(0, cut), pl.ds(cut, tail)]
    chunks = [z, 1 + z % 2, (2 + 3 * z) % 5, 3 - 3 * (z // 2)]
    inner = (z + 1) // 2 % 2 == 1
    outer = (z + 1) // 2 % 2 == 0
    toward = me + 2 - 4 * (z // 2)
    outside = me - 2 + 4 * (z // 2)

    def weight_copies(e):
        return [
            pltpu.make_async_copy(src.at[e], dst.at[e], w_sem.at[e, i])
            for i, (src, dst) in enumerate([(wg_hbm, wg), (wu_hbm, wu), (wd_hbm, wd)])
        ]

    for e in range(local):
        for copy in weight_copies(e):
            copy.start()

    barrier = pltpu.get_barrier_semaphore()

    def greet(device):
        pl.semaphore_signal(
            barrier, inc=1, device_id={"tok": device}, device_id_type=pl.DeviceIdType.MESH
        )

    greet(partner)
    pl.when(z > 0)(lambda: greet(me - 2))
    pl.when(z < 3)(lambda: greet(me + 2))
    pl.semaphore_wait(barrier, 2 + ((z + 1) // 2) % 2)

    buf[me] = x_ref[...]

    def send(src, dst, send_sem, recv_sem, device):
        return pltpu.make_async_remote_copy(
            src_ref=src,
            dst_ref=dst,
            send_sem=send_sem,
            recv_sem=recv_sem,
            device_id={"tok": device},
            device_id_type=pl.DeviceIdType.MESH,
        )

    def token_copy(shard, part, way):
        return send(
            buf.at[shard, parts[part]],
            buf.at[shard, parts[part]],
            ag_send.at[shard, part, way],
            ag_recv.at[shard, part],
            partner,
        )

    def to_partner(shard, part):
        token_copy(shard, part, 0).start()

    def way_copy(shard, part, device, way):
        return send(
            buf.at[shard, parts[part]],
            buf.at[shard, parts[part]],
            ag_send.at[shard, part, way],
            ag_recv.at[shard, part],
            device,
        )

    def to_center(shard, part):
        way_copy(shard, part, toward, 1).start()

    def to_outside(shard, part):
        way_copy(shard, part, outside, 2).start()

    def arrived(shard, part):
        token_copy(shard, part, 0).wait_recv()

    slots = picked.shape[0] // local

    def compute(c, first):
        tokens = buf[pl.ds(2 * c, 2)].reshape(2 * rows, width)
        code = codes_ref[pl.ds(2 * c, 2)].astype(f32)
        code = jnp.concatenate([code[0], code[1]], axis=1)
        shape = (slots, 2 * rows)
        row = lax.broadcasted_iota(jnp.int32, shape, 0).astype(f32)
        second = lax.broadcasted_iota(jnp.int32, (1, 2 * rows), 1) >= rows
        chosen = []
        for e in range(local):
            slot = code[e : e + 1, :]
            place = jnp.where(slot < 0.0, -1.0, jnp.where(second, slot + slots // 2, slot))
            hit = row == place
            chosen.append(jnp.where(hit, 1.0, 0.0).astype(bf16))
            for i in range(2):
                gate = code[(i + 1) * local + e : (i + 1) * local + e + 1, :]
                spread[i, e * slots : (e + 1) * slots, :] = jnp.where(hit, gate, 0.0).astype(bf16)
        picked[...] = jnp.dot(
            jnp.concatenate(chosen, axis=0), tokens, preferred_element_type=f32
        ).astype(bf16)

        def one(e, carry):
            if first:
                for copy in weight_copies(e):
                    copy.wait()
            span = pl.ds(pl.multiple_of(e * slots, 16), slots)
            some = picked[span, :]
            gate_vals = jnp.dot(some, wg[e], preferred_element_type=f32)
            up_vals = jnp.dot(some, wu[e], preferred_element_type=f32)
            hidden = (gate_vals / (1.0 + jnp.exp(-gate_vals)) * up_vals).astype(bf16)
            produced[span, :] = jnp.dot(hidden, wd[e], preferred_element_type=f32).astype(bf16)
            return carry

        lax.fori_loop(0, local, one, 0)
        total = sum(
            lax.dot_general(
                spread[i], produced[...], (((0,), (0,)), ((), ())), preferred_element_type=f32
            )
            for i in range(2)
        )
        acc[pl.ds(2 * c, 2)] = total.reshape(2, rows, width)
        sendx[c] = acc[2 * c + 1 - x, parts[0]].astype(bf16)
        across(c).start()

    def across(c):
        return send(sendx.at[c], recvx.at[c], sx_sem.at[c], rx_sem.at[c], partner)

    def add_across(c):
        across(c).wait()
        acc[2 * c + x, parts[0]] += recvx[c].astype(f32)

    def place(c, piece):
        if piece == 0:
            return acc.at[2 * c + x, parts[0]], pl.ds(0, cut)
        return acc.at[2 * c + piece - 1, parts[1]], pl.ds(cut + (piece - 1) * tail, tail)

    def hop(c, piece, into, sem, device):
        span = place(c, piece)[1]
        return send(
            stage.at[c, span], into.at[c, span], st_sem.at[c, piece], sem.at[c, piece], device
        )

    def outward_hop(c, piece):
        return hop(c, piece, recv_out, ro_sem, toward)

    def center_hop(c, piece):
        return hop(c, piece, recv_in, ri_sem, toward)

    def back_hop(c, piece):
        return hop(c, piece, recv_in, ri_sem, outside)

    def emit(c, piece, hop_of):
        part, span = place(c, piece)
        stage[c, span] = part[...].astype(bf16)
        hop_of(c, piece).start()

    def fold(c, piece, hop_of, ref):
        hop_of(c, piece).wait_recv()
        part, span = place(c, piece)
        part[...] += ref[c, span].astype(f32)

    def relay(c, pieces, came, ref, hop_of):
        for piece in pieces:
            if piece == 0:
                add_across(c)
            fold(c, piece, came, ref)
            emit(c, piece, hop_of)

    def early(c):
        emit(c, 1, outward_hop)
        emit(c, 2, outward_hop)

    def late(c):
        add_across(c)
        emit(c, 0, outward_hop)

    upper = z // 2
    is_inner = (z + 1) // 2 % 2

    def mirrored(c):
        return c + upper * (3 - 2 * c)

    turns = [mirrored(c) for c in (0 * z, 1 + 2 * is_inner, 3 - is_inner, 2 - is_inner)]
    near_c, far_c, mid_c = mirrored(1), mirrored(3), mirrored(2)
    out_c = mirrored(0)

    def pair(c):
        return 2 * c + x, 2 * c + 1 - x

    to_partner(me, 1)

    @pl.when(outer)
    def _():
        same, other = pair(near_c)
        to_center(me, 1)
        to_partner(me, 0)
        to_center(me, 0)
        arrived(partner, 1)
        to_center(partner, 1)
        arrived(partner, 0)
        arrived(same, 1)
        arrived(same, 0)
        to_partner(same, 0)

    @pl.when(inner)
    def _():
        same, other = pair(out_c)
        far_same, far_other = pair(far_c)
        to_outside(me, 1)
        to_center(me, 1)
        to_partner(me, 0)
        to_outside(me, 0)
        arrived(same, 1)
        to_center(same, 1)
        arrived(partner, 1)
        to_outside(partner, 1)
        to_center(partner, 1)
        arrived(same, 0)
        to_center(same, 0)
        to_partner(same, 0)
        arrived(other, 1)
        to_center(other, 1)
        to_center(me, 0)
        arrived(partner, 0)
        arrived(far_same, 1)
        to_outside(far_same, 1)
        in_same, in_other = pair(mid_c)
        arrived(in_same, 1)
        to_outside(in_same, 1)
        arrived(other, 0)

    compute(turns[0], True)

    @pl.when(outer)
    def _():
        same, other = pair(near_c)
        arrived(other, 1)
        arrived(other, 0)

    @pl.when(inner)
    def _():
        far_same, far_other = pair(far_c)
        in_same, in_other = pair(mid_c)
        arrived(far_same, 0)
        to_outside(far_same, 0)
        to_partner(far_same, 0)
        arrived(far_other, 1)
        to_outside(far_other, 1)
        arrived(in_same, 0)
        to_outside(in_same, 0)
        to_partner(in_same, 0)
        arrived(in_other, 1)
        to_outside(in_other, 1)
        arrived(far_other, 0)

    compute(turns[1], False)

    @pl.when(outer)
    def _():
        far_same, far_other = pair(far_c)
        early(near_c)
        arrived(far_same, 1)
        arrived(far_same, 0)
        to_partner(far_same, 0)
        late(near_c)
        arrived(far_other, 1)
        arrived(far_other, 0)

    @pl.when(inner)
    def _():
        arrived(pair(mid_c)[1], 0)

    compute(turns[2], False)

    @pl.when(outer)
    def _():
        in_same, in_other = pair(mid_c)
        early(far_c)
        arrived(in_same, 1)
        arrived(in_same, 0)
        to_partner(in_same, 0)
        late(far_c)
        arrived(in_other, 1)
        arrived(in_other, 0)

    @pl.when(inner)
    def _():
        relay(far_c, (1, 2), outward_hop, recv_out, center_hop)

    compute(turns[3], False)

    @pl.when(outer)
    def _():
        early(mid_c)
        late(mid_c)

    @pl.when(inner)
    def _():
        relay(far_c, (0,), outward_hop, recv_out, center_hop)
        relay(out_c, (1, 2, 0), center_hop, recv_in, back_hop)
        relay(mid_c, (1, 2, 0), outward_hop, recv_out, center_hop)

    add_across(z)
    for piece in (1, 2, 0):
        pl.when(inner)(lambda piece=piece: fold(z, piece, outward_hop, recv_out))
        fold(z, piece, center_hop, recv_in)
        if piece == 2:
            sendf[...] = acc[partner, parts[1]].astype(bf16)
            last = send(sendf, recvf, f_sem.at[0], f_sem.at[1], partner)
            last.start()
    o_ref[:cut, :] = (mid_ref[:cut, :].astype(f32) + acc[me, parts[0]]).astype(bf16)
    last.wait()
    o_ref[cut:, :] = (
        mid_ref[cut:, :].astype(f32) + (acc[me, parts[1]] + recvf[...].astype(f32))
    ).astype(bf16)

    for c in chunks[1:]:
        for piece in range(3):
            center_hop(c, piece).wait_send()

    for shard, part in [(me, 0), (me, 1)] + [(2 * c + x, 0) for c in chunks[1:]]:
        token_copy(shard, part, 0).wait_send()
    for shard, part in ((me, 0), (me, 1), (partner, 1)):
        way_copy(shard, part, toward, 1).wait_send()

    @pl.when(inner)
    def _():
        for way, cs in ((1, (out_c,)), (2, (z, mid_c, far_c))):
            for c in cs:
                same, other = pair(c)
                for shard, part in ((same, 0), (same, 1), (other, 1)):
                    way_copy(shard, part, toward, way).wait_send()


def moe(normed, codes, mid, gate_proj, up_proj, down_proj):
    rows, width = normed.shape
    local, _, hidden = gate_proj.shape
    cut = 5 * rows // 8
    legs = 2 * rows - cut
    vmem = pl.BlockSpec(memory_space=pltpu.VMEM)
    anywhere = pl.BlockSpec(memory_space=pl.ANY)
    bf16, f32 = jnp.bfloat16, jnp.float32
    dma = pltpu.SemaphoreType.DMA
    return pl.pallas_call(
        moe_kernel,
        out_shape=jax.ShapeDtypeStruct((rows, width), bf16),
        in_specs=[vmem, vmem, vmem, anywhere, anywhere, anywhere],
        out_specs=vmem,
        scratch_shapes=[
            pltpu.VMEM((local, width, hidden), bf16),
            pltpu.VMEM((local, width, hidden), bf16),
            pltpu.VMEM((local, hidden, width), bf16),
            pltpu.VMEM((8, rows, width), bf16),
            pltpu.VMEM((8, rows, width), f32),
            pltpu.VMEM((local * 2 * CAP, width), bf16),
            pltpu.VMEM((local * 2 * CAP, width), bf16),
            pltpu.VMEM((2, local * 2 * CAP, 2 * rows), bf16),
            pltpu.VMEM((4, cut, width), bf16),
            pltpu.VMEM((4, cut, width), bf16),
            pltpu.VMEM((4, legs, width), bf16),
            pltpu.VMEM((4, legs, width), bf16),
            pltpu.VMEM((4, legs, width), bf16),
            pltpu.VMEM((rows - cut, width), bf16),
            pltpu.VMEM((rows - cut, width), bf16),
            dma((local, 3)),
            dma((8, 2, 3)),
            dma((8, 2)),
            dma((4,)),
            dma((4,)),
            dma((4, 3)),
            dma((4, 3)),
            dma((4, 3)),
            dma((2,)),
        ],
        compiler_params=pltpu.CompilerParams(
            collective_id=1, has_side_effects=True, vmem_limit_bytes=58 << 20
        ),
    )(normed, codes, mid, gate_proj, up_proj, down_proj)


def route(ids_ref, gates_ref, out):
    ids = ids_ref[...].astype(jnp.float32).T
    gates = gates_ref[...].T
    devices = out.shape[0]
    local = EXPERTS // devices
    rows = ids.shape[1]
    expert = lax.broadcasted_iota(jnp.int32, (EXPERTS, rows), 0).astype(jnp.float32)
    chosen = jnp.zeros((EXPERTS, rows), jnp.float32)
    gate = jnp.zeros((EXPERTS, rows), jnp.float32)
    for k in range(ids.shape[0]):
        hit = expert == ids[k : k + 1, :]
        chosen = jnp.where(hit, 1.0, chosen)
        gate = jnp.where(hit, gates[k : k + 1, :], gate)
    row = lax.broadcasted_iota(jnp.int32, (rows, rows), 0)
    column = lax.broadcasted_iota(jnp.int32, (rows, rows), 1)
    before = jnp.where(row < column, 1.0, 0.0).astype(jnp.bfloat16)
    slot = jnp.dot(chosen.astype(jnp.bfloat16), before, preferred_element_type=jnp.float32)
    slot = jnp.where(chosen > 0.5, slot, -1.0)
    high = gate.astype(jnp.bfloat16).astype(jnp.float32)
    rest = gate - high
    for device in range(devices):
        span = slice(device * local, (device + 1) * local)
        out[device] = jnp.concatenate(
            [slot[span], high[span], rest[span], jnp.zeros((16 - 3 * local, rows), jnp.float32)],
            axis=0,
        ).astype(jnp.bfloat16)


def attend_kernel(
    q_ref,
    suffix_ref,
    pool_ref,
    cos_ref,
    sin_ref,
    low_ref,
    high_ref,
    packed_ref,
    stream_ref,
    gain_ref,
    ids_ref,
    gates_ref,
    proj_hbm,
    mid_ref,
    normed_ref,
    codes_ref,
    proj,
    c_out,
    c_in,
    q_out,
    q_in,
    q_all,
    p_out,
    p_in,
    s_out,
    s_in,
    vx,
    bounds,
    best,
    acc,
    o_out,
    o_in,
    attended,
    proj_sem,
    qs_sem,
    qr_sem,
    ps_sem,
    pr_sem,
    ss_sem,
    sr_sem,
    os_sem,
    or_sem,
    cs_sem,
    cr_sem,
):
    me = lax.axis_index("tok")
    z = me // 2
    x = me % 2
    partner = z * 2 + 1 - x
    rows = q_ref.shape[0]
    half = rows // 2
    page_rows = pool_ref.shape[0]
    width = KVH * HD
    f32, bf16 = jnp.float32, jnp.bfloat16

    proj_copy = pltpu.make_async_copy(proj_hbm, proj, proj_sem)
    proj_copy.start()

    barrier = pltpu.get_barrier_semaphore()
    chunks = [z, 1 + z % 2, (2 + 3 * z) % 5, 3 - 3 * (z // 2)]
    near = [partner]
    for c in chunks[1:]:
        near += [2 * c + x, 2 * c + 1 - x]
    far = near[::-1]
    for peer in near:
        pl.semaphore_signal(
            barrier, inc=1, device_id={"tok": peer}, device_id_type=pl.DeviceIdType.MESH
        )

    def send(src, dst, send_sem, recv_sem, device):
        return pltpu.make_async_remote_copy(
            src_ref=src,
            dst_ref=dst,
            send_sem=send_sem,
            recv_sem=recv_sem,
            device_id={"tok": device},
            device_id_type=pl.DeviceIdType.MESH,
        )

    def exchange(out, into, send_sem, recv_sem):
        def to(peer):
            return send(out.at[peer], into.at[me], send_sem.at[peer], recv_sem.at[me], peer)

        def came(peer):
            return send(out.at[peer], into.at[peer], send_sem.at[peer], recv_sem.at[peer], peer)

        return to, came

    q_to, q_from = exchange(q_out, q_in, qs_sem, qr_sem)
    p_to, p_from = exchange(p_out, p_in, ps_sem, pr_sem)
    s_to, s_from = exchange(s_out, s_in, ss_sem, sr_sem)
    o_to, o_from = exchange(o_out, o_in, os_sem, or_sem)
    c_to, c_from = exchange(c_out, c_in, cs_sem, cr_sem)

    def lanes(shape):
        return lax.broadcasted_iota(jnp.int32, shape, 1)

    def turn(v, cosine, sine):
        first = lanes(v.shape) % HD < HD // 2
        swapped = jnp.where(first, pltpu.roll(v, 128 - HD // 2, 1), pltpu.roll(v, HD // 2, 1))
        return (v * cosine + swapped * sine).astype(bf16).astype(f32)

    def mix(left, right):
        return jnp.where(lanes(left.shape) < HD, left, right)

    def flip(v):
        return pltpu.roll(v, HD, 1)

    cosine, sine = cos_ref[page_rows:, :], sin_ref[page_rows:, :]
    for pair in range(QH // 2):
        v = q_ref[:, 128 * pair : 128 * pair + 128].astype(f32)
        v = turn(v, cosine, sine) * (HD**-0.5)
        top, low = v[:half], v[half:]
        for n, packed in ((2 * pair, mix(top, flip(low))), (2 * pair + 1, mix(flip(top), low))):
            q_out[n // RATIO, n % RATIO] = packed.astype(bf16)
    pl.semaphore_wait(barrier, 7)
    for peer in far:
        q_to(peer).start()

    def caches(src, first, table, out, at):
        span = pl.ds(first, 128)
        cosine, sine = cos_ref[pl.ds(table, 128), :], sin_ref[pl.ds(table, 128), :]
        for pair in range(KVH // 2):
            k = src[span, 128 * pair : 128 * pair + 128].astype(f32)
            k = turn(k, cosine, sine)
            v = src[span, width + 128 * pair : width + 128 * pair + 128].astype(f32)
            out[2 * pair, span, :] = mix(k, flip(v)).astype(bf16)
            out[2 * pair + 1, span, :] = mix(flip(k), v).astype(bf16)

    caches(suffix_ref, 0, page_rows, s_out, 0)
    for peer in far:
        s_to(peer).start()

    def prepare(i, carry):
        first = pl.multiple_of(i * 128, 128)
        caches(pool_ref, first, first, p_out, 0)
        return carry

    lax.fori_loop(0, page_rows // 128, prepare, 0)
    for peer in near:
        p_to(peer).start()

    route(ids_ref, gates_ref, c_out)
    for peer in near:
        c_to(peer).start()
    c_in[me] = c_out[me]
    q_in[me] = q_out[me]
    s_in[me] = s_out[me]
    bounds[0] = low_ref[...].astype(f32).T
    bounds[1] = high_ref[...].astype(f32).T

    def column(which, r):
        v = bounds[which]
        return jnp.sum(jnp.where(lanes(v.shape) == r, v, 0.0), axis=1, keepdims=True)

    def values(keys):
        return jnp.where(lanes(keys.shape) < HD, jnp.ones_like(keys), keys)

    def unpack(r):
        for j in range(RATIO):
            v = q_in[r, j].astype(f32)
            zero = jnp.zeros_like(v)
            q_all[r, pl.ds(j * rows, half), :] = mix(v, zero).astype(bf16)
            q_all[r, pl.ds(j * rows + half, half), :] = mix(flip(v), zero).astype(bf16)

    def scored(r, keys, count, masked):
        s = lax.dot_general(
            q_all[r], keys, (((1,), (1,)), ((), ())), preferred_element_type=f32
        )
        if masked:
            at = packed_ref[...].astype(f32)
            seen = (at >= column(0, r)) & (at <= column(1, r))
            bias = jnp.where(seen, 0.0, NEG_FILL)
            s = (s.reshape(RATIO, rows, count) + bias[None]).reshape(RATIO * rows, count)
        return s

    def blocks(rs, keys, count, masked=False, first=False):
        olds = [None if first else best[r][:, :1] for r in rs]
        sums = [None if first else acc[r] for r in rs]
        scores = [scored(r, keys, count, masked) for r in rs]
        tops, totals = [], []
        for s, old, before in zip(scores, olds, sums):
            top = jnp.max(s, axis=-1, keepdims=True)
            if not first:
                top = jnp.maximum(old, top)
            weights = jnp.exp(s - top).astype(bf16)
            total = jnp.dot(weights, vx[:count], preferred_element_type=f32)
            if not first:
                total = before * jnp.exp(old - top) + total
            tops.append(top)
            totals.append(total)
        for r, top, total in zip(rs, tops, totals):
            acc[r] = total
            best[r] = jnp.broadcast_to(top, (RATIO * rows, 128))

    def step(keys_ref, count, masked=False, first=False, last=False):
        vx[:count] = values(keys_ref())

        def body(i, carry):
            c = lax.rem(z + 1 + i, 4) if last else lax.rem(z + i, 4)
            for side in range(2):
                r = 2 * c + side
                if first:
                    pl.when(r != me)(lambda r=r: q_from(r).wait_recv())
                    unpack(r)
            blocks([2 * c, 2 * c + 1], keys_ref(), count, masked, first)
            if last:
                for side in range(2):
                    r = 2 * c + side
                    for j in range(RATIO):
                        v = acc[r, pl.ds(j * rows, rows), :]
                        v = v / flip(v)
                        o_out[r, j] = mix(flip(v[:half]), v[half:]).astype(bf16)
                    pl.when(r != me)(lambda r=r: o_to(r).start())
            return carry

        lax.fori_loop(0, 4, body, 0)

    step(lambda: p_out[me], page_rows, first=True)
    for peer in near:
        s_from(peer).wait_recv()
    step(lambda: s_in[...].reshape(8 * rows, 128), 8 * rows, masked=True)
    p_from(partner).wait_recv()
    step(lambda: p_in[partner], page_rows)
    for i in range(1, 4):
        c = chunks[i]
        p_from(2 * c + x).wait_recv()
        p_from(2 * c + 1 - x).wait_recv()
        step(
            lambda c=c: p_in[pl.ds(2 * c, 2)].reshape(2 * page_rows, 128),
            2 * page_rows,
            last=i == 3,
        )
    o_in[me] = o_out[me]
    for peer in far:
        o_from(peer).wait_recv()
    for pair in range(QH // 2):
        n, m = 2 * pair, 2 * pair + 1
        one = o_in[n // RATIO, n % RATIO].astype(f32)
        two = o_in[m // RATIO, m % RATIO].astype(f32)
        span = slice(128 * pair, 128 * pair + 128)
        attended[:half, span] = mix(one, flip(two)).astype(bf16)
        attended[half:, span] = mix(flip(one), two).astype(bf16)
    proj_copy.wait()
    for first in range(0, proj.shape[1], 512):
        span = slice(first, first + 512)
        mid_ref[:, span] = (
            stream_ref[:, span].astype(f32)
            + jnp.dot(attended[...], proj[:, span], preferred_element_type=f32)
        ).astype(bf16)
    mid = mid_ref[...].astype(f32)
    normed_ref[...] = (
        mid * lax.rsqrt(jnp.mean(mid * mid, axis=-1, keepdims=True) + 1e-05) * gain_ref[...]
    ).astype(bf16)
    for peer in near:
        c_from(peer).wait_recv()
    codes_ref[...] = c_in[...]
    for to in (q_to, s_to, p_to, o_to, c_to):
        for peer in near:
            to(peer).wait_send()


def attend(q, suffix, pool, positions, low, high, packed, stream, gain, ids, gates, proj):
    rows = q.shape[0]
    half_dim = HD // 2
    frequency = ROPE_BASE ** (-jnp.arange(half_dim, dtype=jnp.float32) / half_dim)
    angles = positions.astype(jnp.float32)[:, None] * frequency[None, :]
    cosine, sine = jnp.cos(angles), jnp.sin(angles)
    cosine = jnp.concatenate([cosine] * 4, axis=1)
    sine = jnp.concatenate([-sine, sine] * 2, axis=1)
    page_rows = pool.shape[0]
    vmem = pl.BlockSpec(memory_space=pltpu.VMEM)
    bf16, f32 = jnp.bfloat16, jnp.float32
    dma = pltpu.SemaphoreType.DMA
    out = jax.ShapeDtypeStruct(stream.shape, bf16)
    return pl.pallas_call(
        attend_kernel,
        out_shape=(out, out, jax.ShapeDtypeStruct((8, 16, rows), bf16)),
        in_specs=[vmem] * 12 + [pl.BlockSpec(memory_space=pl.ANY)],
        out_specs=(vmem, vmem, vmem),
        scratch_shapes=[
            pltpu.VMEM(proj.shape, bf16),
            pltpu.VMEM((8, 16, rows), bf16),
            pltpu.VMEM((8, 16, rows), bf16),
            pltpu.VMEM((8, RATIO, rows // 2, 128), bf16),
            pltpu.VMEM((8, RATIO, rows // 2, 128), bf16),
            pltpu.VMEM((8, RATIO * rows, 128), bf16),
            pltpu.VMEM((8, page_rows, 128), bf16),
            pltpu.VMEM((8, page_rows, 128), bf16),
            pltpu.VMEM((8, rows, 128), bf16),
            pltpu.VMEM((8, rows, 128), bf16),
            pltpu.VMEM((2 * page_rows, 128), bf16),
            pltpu.VMEM((2, rows, 8), f32),
            pltpu.VMEM((8, RATIO * rows, 128), f32),
            pltpu.VMEM((8, RATIO * rows, 128), f32),
            pltpu.VMEM((8, RATIO, rows // 2, 128), bf16),
            pltpu.VMEM((8, RATIO, rows // 2, 128), bf16),
            pltpu.VMEM(q.shape, bf16),
            dma(()),
        ]
        + [dma((8,))] * 10,
        compiler_params=pltpu.CompilerParams(
            collective_id=2, has_side_effects=True, vmem_limit_bytes=58 << 20
        ),
    )(
        q,
        suffix,
        pool,
        cosine,
        sine,
        low.reshape(8, rows),
        high.reshape(8, rows),
        packed.reshape(1, 8 * rows),
        stream,
        gain.reshape(1, -1),
        ids,
        gates,
        proj,
    )


def shards(
    queries,
    suffix_cache,
    stream_in,
    page_pool,
    page_table,
    segment_ids,
    dealing,
    out_proj,
    norm_gain,
    expert_ids,
    expert_gates,
    gate_proj,
    up_proj,
    down_proj,
):
    tok_count = lax.axis_size("tok")
    tok_index = lax.axis_index("tok")
    rows_dev = queries.shape[1]
    width = KVH * HD
    table = page_table[0]
    pages_all = table.shape[0]
    pages_dev = page_pool.shape[1]
    page_len = page_pool.shape[2]
    pool_rows = pages_dev * page_len
    prefix_len = pages_all * page_len
    repeats = tok_count // KVH
    head_groups = [[r * KVH + h for h in range(KVH)] for r in range(repeats)]
    same_head = [[r * KVH + h for r in range(repeats)] for h in range(KVH)]
    sub = dict(axis_index_groups=head_groups) if repeats > 1 else {}

    gate_dense = jnp.sum(
        jnp.where(
            expert_ids[0][:, :, None] == jnp.arange(EXPERTS, dtype=jnp.int32)[None, None, :],
            expert_gates[0][:, :, None],
            0.0,
        ),
        axis=1,
    )

    my_slots = tok_index * pages_dev + jnp.arange(pages_dev, dtype=jnp.int32)
    logical_page = jnp.sum(
        jnp.where(
            table[:, None] == my_slots[None, :],
            jnp.arange(pages_all, dtype=jnp.int32)[:, None],
            0,
        ),
        axis=0,
    )
    pool_positions = (
        logical_page[:, None] * page_len + jnp.arange(page_len, dtype=jnp.int32)[None, :]
    ).reshape(-1)
    dealt = dealing[0]
    requests = jnp.arange(REQS, dtype=jnp.int32)
    starts = jnp.sum((segment_ids[0][:, None] < requests[None, :]).astype(jnp.int32), axis=0)
    low_all = jnp.max(
        jnp.where(starts[None, :] <= dealt[:, None], starts[None, :], 0), axis=1
    )
    my_start = tok_index * rows_dev
    my_dealt = lax.dynamic_slice_in_dim(dealt, my_start, rows_dev)
    my_low = lax.dynamic_slice_in_dim(low_all, my_start, rows_dev)
    my_positions = prefix_len + my_dealt - my_low

    if tok_count == 8:
        mid_round, normed, codes = attend(
            queries[0],
            suffix_cache[0],
            page_pool.reshape(pool_rows, 2 * width),
            jnp.concatenate([pool_positions, my_positions]),
            low_all,
            dealt,
            dealt,
            stream_in[0],
            norm_gain,
            expert_ids[0],
            expert_gates[0],
            out_proj,
        )
        return moe(normed, codes, mid_round, gate_proj, up_proj, down_proj)[None]

    cache = jnp.concatenate([page_pool.reshape(pool_rows, 2 * width), suffix_cache[0]], axis=0)
    positions = jnp.concatenate([pool_positions, my_positions])
    count = pool_rows + rows_dev
    keys = rotate(cache[:, :width].reshape(count, KVH, HD), positions)
    values = cache[:, width:].reshape(count, KVH, HD)
    outgoing = jnp.concatenate([keys, values], axis=-1).transpose(1, 0, 2)
    arrived = lax.all_to_all(outgoing, "tok", split_axis=0, concat_axis=0, tiled=True, **sub)
    if repeats > 1:
        arrived = lax.all_gather(
            arrived, "tok", axis=0, tiled=True, axis_index_groups=same_head
        )
    kv = jnp.concatenate(
        [
            arrived[:, :pool_rows].reshape(-1, 2 * HD),
            arrived[:, pool_rows:].reshape(-1, 2 * HD),
        ],
        axis=0,
    )

    half = rows_dev // 2
    roped = rotate(queries[0].reshape(rows_dev, QH, HD), my_positions)
    packed_q = (
        roped.reshape(2, half, KVH, RATIO, HD)
        .transpose(2, 3, 1, 0, 4)
        .reshape(KVH, RATIO, half, 2 * HD)
    )
    got_q = lax.all_to_all(packed_q, "tok", split_axis=0, concat_axis=0, tiled=True, **sub)
    got_q = jnp.concatenate([got_q[..., :HD], got_q[..., HD:]], axis=2)
    got_q = jnp.pad(got_q, ((0, 0), (0, 0), (0, 0), (0, HD)))
    row_count = KVH * rows_dev
    first_row = (tok_index // KVH) * row_count
    low_q = lax.dynamic_slice_in_dim(low_all, first_row, row_count)
    high_q = lax.dynamic_slice_in_dim(dealt, first_row, row_count)
    out = attention(got_q, kv, low_q, high_q, dealt, prefix_len)
    back = lax.all_to_all(out, "tok", split_axis=0, concat_axis=0, tiled=True, **sub)
    attended = (
        back.reshape(KVH, RATIO, half, 2, HD)
        .transpose(3, 2, 0, 1, 4)
        .reshape(rows_dev, QH * HD)
    )

    mid_round = lax.optimization_barrier(
        (
            stream_in[0].astype(jnp.float32)
            + jnp.dot(attended, out_proj, preferred_element_type=jnp.float32)
        ).astype(jnp.bfloat16)
    )
    mid_float = mid_round.astype(jnp.float32)
    normed = (
        mid_float
        * lax.rsqrt(jnp.mean(mid_float * mid_float, axis=-1, keepdims=True) + 1e-05)
        * norm_gain
    ).astype(jnp.bfloat16)

    local = gate_proj.shape[0]
    gates_all = lax.all_gather(gate_dense, "tok", axis=0, tiled=True)
    gates_mine = lax.dynamic_slice_in_dim(gates_all, tok_index * local, local, axis=1)
    gates_mine = gates_mine.T.reshape(local, tok_count * rows_dev, 1)
    tokens = lax.all_gather(normed, "tok", axis=0, tiled=True)
    sums = expert_sums(tokens, gates_mine, gate_proj, up_proj, down_proj)
    mixed = lax.psum_scatter(sums, "tok", scatter_dimension=0, tiled=True)
    return (mid_float + mixed.astype(jnp.float32)).astype(jnp.bfloat16)[None]


def solution(mesh):
    placed = (
        P("group", "tok", None),
        P("group", "tok", None),
        P("group", "tok", None),
        P("group", "tok", None, None),
        P("group", None),
        P("group", None),
        P("group", None),
        P(),
        P(),
        P("group", "tok", None),
        P("group", "tok", None),
        P("tok", None, None),
        P("tok", None, None),
        P("tok", None, None),
    )
    return jax.shard_map(
        shards, mesh=mesh, in_specs=placed, out_specs=P("group", "tok", None), check_vma=False
    )
```

```python
import functools

import jax
import jax.numpy as jnp
import numpy as np
from jax import lax
from jax.experimental import pallas as pl
from jax.experimental.pallas import tpu as pltpu
from jax.sharding import PartitionSpec as P

QH = 24
KVH = 8
HD = 64
RATIO = QH // KVH
EXPERTS = 32
REQS = 16
CAP = 40
ROPE_BASE = 10000.0
NEG_FILL = -1e30
KEY_CHUNK = 1024


def rotate(vectors, positions):
    half_dim = vectors.shape[-1] // 2
    frequency = ROPE_BASE ** (-jnp.arange(half_dim, dtype=jnp.float32) / half_dim)
    angles = positions.astype(jnp.float32)[:, None] * frequency[None, :]
    cosine = jnp.cos(angles)[:, None, :]
    sine_part = jnp.sin(angles)[:, None, :]
    first_half = vectors[..., :half_dim].astype(jnp.float32)
    second = vectors[..., half_dim:].astype(jnp.float32)
    joined = jnp.concatenate(
        [first_half * cosine - second * sine_part, first_half * sine_part + second * cosine],
        axis=-1,
    )
    return joined.astype(jnp.bfloat16)


def attention_kernel(prefix_len, q_ref, kv_ref, lo_ref, hi_ref, pk_ref, o_ref, vx_ref):
    keys = kv_ref.shape[0]
    rows = q_ref.shape[2]

    @pl.when(pl.program_id(0) == 0)
    def _():
        lane = lax.broadcasted_iota(jnp.int32, kv_ref.shape, 1)
        vx_ref[...] = jnp.where(lane < HD, jnp.ones_like(kv_ref), kv_ref[...])

    q = q_ref[0].reshape(RATIO * rows, 2 * HD)
    best = jnp.full((RATIO * rows, 1), NEG_FILL, jnp.float32)
    accum = jnp.zeros((RATIO * rows, 2 * HD), jnp.float32)
    scale = HD ** (-0.5)
    for first in range(0, keys, KEY_CHUNK):
        part = slice(first, first + KEY_CHUNK)
        scores = (
            lax.dot_general(
                q, kv_ref[part, :], (((1,), (1,)), ((), ())), preferred_element_type=jnp.float32
            )
            * scale
        )
        if first >= prefix_len:
            pk = pk_ref[:, first - prefix_len : first - prefix_len + KEY_CHUNK]
            seen = (pk >= lo_ref[0]) & (pk <= hi_ref[0])
            seen = jnp.concatenate([seen.astype(jnp.float32)] * RATIO, axis=0) > 0.5
            scores = jnp.where(seen, scores, NEG_FILL)
        new_best = jnp.maximum(best, jnp.max(scores, axis=-1, keepdims=True))
        weights = jnp.exp(scores - new_best).astype(jnp.bfloat16)
        factor = jnp.exp(best - new_best)
        accum = accum * factor + jnp.dot(
            weights, vx_ref[part, :], preferred_element_type=jnp.float32
        )
        best = new_best
    out = (accum[:, HD:] / accum[:, :HD]).astype(jnp.bfloat16).reshape(RATIO, rows, HD)
    o_ref[0] = jnp.concatenate([out[:, : rows // 2], out[:, rows // 2 :]], axis=-1)


def attention(q, kv, low, high, packed, prefix_len):
    sources, _, rows, _ = q.shape
    keys = kv.shape[0]
    suffix = keys - prefix_len
    return pl.pallas_call(
        functools.partial(attention_kernel, prefix_len),
        out_shape=jax.ShapeDtypeStruct((sources, RATIO, rows // 2, 2 * HD), jnp.bfloat16),
        grid=(sources,),
        in_specs=[
            pl.BlockSpec((1, RATIO, rows, 2 * HD), lambda i: (i, 0, 0, 0)),
            pl.BlockSpec((keys, 2 * HD), lambda i: (0, 0)),
            pl.BlockSpec((1, rows, 1), lambda i: (i, 0, 0)),
            pl.BlockSpec((1, rows, 1), lambda i: (i, 0, 0)),
            pl.BlockSpec((1, suffix), lambda i: (0, 0)),
        ],
        out_specs=pl.BlockSpec((1, RATIO, rows // 2, 2 * HD), lambda i: (i, 0, 0, 0)),
        scratch_shapes=[pltpu.VMEM((keys, 2 * HD), jnp.bfloat16)],
        compiler_params=pltpu.CompilerParams(vmem_limit_bytes=48 << 20),
    )(q, kv, low.reshape(sources, rows, 1), high.reshape(sources, rows, 1), packed.reshape(1, suffix))


def expert_kernel(x_ref, gates_ref, gate_ref, up_ref, down_ref, o_ref, acc_ref):
    expert = pl.program_id(1)
    x = x_ref[...]
    gate_vals = jnp.dot(x, gate_ref[0], preferred_element_type=jnp.float32)
    up_vals = jnp.dot(x, up_ref[0], preferred_element_type=jnp.float32)
    hidden = (gate_vals / (1.0 + jnp.exp(-gate_vals)) * up_vals).astype(jnp.bfloat16)
    produced = jnp.dot(hidden, down_ref[0], preferred_element_type=jnp.float32)
    term = gates_ref[0] * produced.astype(jnp.bfloat16).astype(jnp.float32)

    @pl.when(expert == 0)
    def _():
        acc_ref[...] = term

    @pl.when(expert > 0)
    def _():
        acc_ref[...] += term

    @pl.when(expert == pl.num_programs(1) - 1)
    def _():
        o_ref[...] = acc_ref[...].astype(jnp.bfloat16)


def expert_sums(x, gates, gate_proj, up_proj, down_proj):
    rows, width = x.shape
    experts, _, hidden = gate_proj.shape
    block = min(512, rows)
    return pl.pallas_call(
        expert_kernel,
        out_shape=jax.ShapeDtypeStruct((rows, width), jnp.bfloat16),
        grid=(rows // block, experts),
        in_specs=[
            pl.BlockSpec((block, width), lambda i, e: (i, 0)),
            pl.BlockSpec((1, block, 1), lambda i, e: (e, i, 0)),
            pl.BlockSpec((1, width, hidden), lambda i, e: (e, 0, 0)),
            pl.BlockSpec((1, width, hidden), lambda i, e: (e, 0, 0)),
            pl.BlockSpec((1, hidden, width), lambda i, e: (e, 0, 0)),
        ],
        out_specs=pl.BlockSpec((block, width), lambda i, e: (i, 0)),
        scratch_shapes=[pltpu.VMEM((block, width), jnp.float32)],
        compiler_params=pltpu.CompilerParams(vmem_limit_bytes=56 << 20),
    )(x, gates, gate_proj, up_proj, down_proj)


def route(ids_ref, gates_ref, out):
    ids = ids_ref[...].astype(jnp.float32)
    gates = gates_ref[...]
    devices = out.shape[0]
    local = EXPERTS // devices
    rows = ids.shape[1]
    expert = lax.broadcasted_iota(jnp.int32, (EXPERTS, rows), 0).astype(jnp.float32)
    chosen = jnp.zeros((EXPERTS, rows), jnp.float32)
    gate = jnp.zeros((EXPERTS, rows), jnp.float32)
    for k in range(ids.shape[0]):
        hit = expert == ids[k : k + 1, :]
        chosen = jnp.where(hit, 1.0, chosen)
        gate = jnp.where(hit, gates[k : k + 1, :], gate)
    row = lax.broadcasted_iota(jnp.int32, (rows, rows), 0)
    column = lax.broadcasted_iota(jnp.int32, (rows, rows), 1)
    before = jnp.where(row < column, 1.0, 0.0).astype(jnp.bfloat16)
    slot = jnp.dot(chosen.astype(jnp.bfloat16), before, preferred_element_type=jnp.float32)
    slot = jnp.where(chosen > 0.5, slot, -1.0)
    high = gate.astype(jnp.bfloat16).astype(jnp.float32)
    rest = gate - high
    for device in range(devices):
        span = slice(device * local, (device + 1) * local)
        out[device] = jnp.concatenate(
            [slot[span], high[span], rest[span], jnp.zeros((16 - 3 * local, rows), jnp.float32)],
            axis=0,
        ).astype(jnp.bfloat16)


def layer_kernel(
    q_ref,
    suffix_ref,
    pool_ref,
    frequency_ref,
    table_ref,
    segment_ref,
    packed_ref,
    stream_ref,
    gain_ref,
    ids_ref,
    gates_ref,
    proj_hbm,
    wg_hbm,
    wu_hbm,
    wd_hbm,
    o_ref,
    mid_ref,
    cos_ref,
    sin_ref,
    proj,
    c_out,
    c_in,
    q_out,
    q_in,
    q_all,
    p_out,
    p_in,
    s_out,
    s_in,
    vx,
    bounds,
    best,
    acc,
    o_out,
    o_in,
    attended,
    proj_sem,
    qs_sem,
    qr_sem,
    ps_sem,
    pr_sem,
    ss_sem,
    sr_sem,
    os_sem,
    or_sem,
    cs_sem,
    cr_sem,
    wg,
    wu,
    wd,
    buf,
    part_sums,
    picked,
    produced,
    spread,
    sendx,
    recvx,
    stage,
    recv_out,
    recv_in,
    sendf,
    recvf,
    w_sem,
    ag_send,
    ag_recv,
    sx_sem,
    rx_sem,
    st_sem,
    ro_sem,
    ri_sem,
    f_sem,
):
    me = lax.axis_index("tok")
    z = me // 2
    x = me % 2
    partner = z * 2 + 1 - x
    rows = q_ref.shape[0]
    half = rows // 2
    page_rows = pool_ref.shape[0]
    kv_width = KVH * HD
    f32, bf16 = jnp.float32, jnp.bfloat16

    proj_copy = pltpu.make_async_copy(proj_hbm, proj, proj_sem)
    proj_copy.start()

    barrier = pltpu.get_barrier_semaphore()
    chunks = [z, 1 + z % 2, (2 + 3 * z) % 5, 3 - 3 * (z // 2)]
    near = [partner]
    for c in chunks[1:]:
        near += [2 * c + x, 2 * c + 1 - x]
    far = near[::-1]
    for peer in near:
        pl.semaphore_signal(
            barrier, inc=1, device_id={"tok": peer}, device_id_type=pl.DeviceIdType.MESH
        )

    def send(src, dst, send_sem, recv_sem, device):
        return pltpu.make_async_remote_copy(
            src_ref=src,
            dst_ref=dst,
            send_sem=send_sem,
            recv_sem=recv_sem,
            device_id={"tok": device},
            device_id_type=pl.DeviceIdType.MESH,
        )

    def exchange(out, into, send_sem, recv_sem):
        def to(peer):
            return send(out.at[peer], into.at[me], send_sem.at[peer], recv_sem.at[me], peer)

        def came(peer):
            return send(out.at[peer], into.at[peer], send_sem.at[peer], recv_sem.at[peer], peer)

        return to, came

    q_to, q_from = exchange(q_out, q_in, qs_sem, qr_sem)
    p_to, p_from = exchange(p_out, p_in, ps_sem, pr_sem)
    s_to, s_from = exchange(s_out, s_in, ss_sem, sr_sem)
    o_to, o_from = exchange(o_out, o_in, os_sem, or_sem)
    c_to, c_from = exchange(c_out, c_in, cs_sem, cr_sem)

    def lanes(shape):
        return lax.broadcasted_iota(jnp.int32, shape, 1)

    def turn(v, cosine, sine):
        first = lanes(v.shape) % HD < HD // 2
        swapped = jnp.where(first, pltpu.roll(v, 128 - HD // 2, 1), pltpu.roll(v, HD // 2, 1))
        return (v * cosine + swapped * sine).astype(bf16).astype(f32)

    def mix(left, right):
        return jnp.where(lanes(left.shape) < HD, left, right)

    def flip(v):
        return pltpu.roll(v, HD, 1)

    pages = page_rows // 128
    split = [slice(first, first + rows) for first in range(0, 8 * rows, rows)]
    dealt = jnp.concatenate([packed_ref[:, span] for span in split], axis=0).astype(f32)
    owner = jnp.concatenate([segment_ref[:, span] for span in split], axis=0).astype(f32)
    start = jnp.zeros_like(dealt)
    for request in range(REQS):
        earlier = jnp.where(owner < request, 1.0, 0.0)
        earlier = jnp.sum(jnp.sum(earlier, axis=1, keepdims=True), axis=0, keepdims=True)
        start = jnp.where(earlier <= dealt, jnp.maximum(start, earlier), start)
    bounds[0] = start.T
    bounds[1] = dealt.T

    def column(which, r):
        v = bounds[which]
        return jnp.sum(jnp.where(lanes(v.shape) == r, v, 0.0), axis=1, keepdims=True)

    prefix_len = table_ref.shape[1] * 128
    second = lanes((rows, 128)) % HD >= HD // 2
    angles = (column(1, me) - column(0, me) + prefix_len) * frequency_ref[...]
    cos_ref[page_rows:, :] = jnp.cos(angles)
    sine = jnp.sin(angles)
    sin_ref[page_rows:, :] = jnp.where(second, sine, -sine)

    def tables():
        table = table_ref[...]
        at = lax.broadcasted_iota(jnp.int32, table.shape, 1)
        lane = lanes((128, 128))
        logical = jnp.zeros((128, 128), f32)
        for i in range(pages):
            page = jnp.sum(
                jnp.where(table == me * pages + i, at, 0).astype(f32), axis=1, keepdims=True
            )
            logical = jnp.where(lane // (HD // 2) == i, page, logical)
        row = lax.broadcasted_iota(jnp.int32, (128, 128), 0).astype(f32)
        angles = (logical * 128.0 + row) * frequency_ref[...]
        for ref, every in ((cos_ref, jnp.cos(angles)), (sin_ref, jnp.sin(angles))):
            for i in range(pages):
                v = pltpu.roll(every, (4 - i) * (HD // 2) % 128, 1) if i else every
                v = jnp.where(lane < HD // 2, v, pltpu.roll(v, HD // 2, 1))
                v = jnp.where(lane < HD, v, pltpu.roll(v, HD, 1))
                if ref is sin_ref:
                    v = jnp.where(second, v, -v)
                ref[128 * i : 128 * i + 128, :] = v

    cosine, sine = cos_ref[page_rows:, :], sin_ref[page_rows:, :]
    for pair in range(QH // 2):
        v = q_ref[:, 128 * pair : 128 * pair + 128].astype(f32)
        v = turn(v, cosine, sine) * (HD**-0.5)
        top, low = v[:half], v[half:]
        for n, packed in ((2 * pair, mix(top, flip(low))), (2 * pair + 1, mix(flip(top), low))):
            q_out[n // RATIO, n % RATIO] = packed.astype(bf16)
    pl.semaphore_wait(barrier, 7)
    for peer in far:
        q_to(peer).start()

    def caches(src, first, table, out, at):
        span = pl.ds(first, 128)
        cosine, sine = cos_ref[pl.ds(table, 128), :], sin_ref[pl.ds(table, 128), :]
        for pair in range(KVH // 2):
            k = src[span, 128 * pair : 128 * pair + 128].astype(f32)
            k = turn(k, cosine, sine)
            v = src[span, kv_width + 128 * pair : kv_width + 128 * pair + 128].astype(f32)
            out[2 * pair, span, :] = mix(k, flip(v)).astype(bf16)
            out[2 * pair + 1, span, :] = mix(flip(k), v).astype(bf16)

    caches(suffix_ref, 0, page_rows, s_out, 0)
    for peer in far:
        s_to(peer).start()

    tables()

    def prepare(i, carry):
        first = pl.multiple_of(i * 128, 128)
        caches(pool_ref, first, first, p_out, 0)
        return carry

    lax.fori_loop(0, page_rows // 128, prepare, 0)
    for peer in near:
        p_to(peer).start()

    def weight_copies(e):
        return [
            pltpu.make_async_copy(src.at[e], dst.at[e], w_sem.at[e, i])
            for i, (src, dst) in enumerate([(wg_hbm, wg), (wu_hbm, wu), (wd_hbm, wd)])
        ]

    for e in range(wg.shape[0]):
        for copy in weight_copies(e):
            copy.start()

    route(ids_ref, gates_ref, c_out)
    for peer in near:
        c_to(peer).start()
    c_in[me] = c_out[me]
    q_in[me] = q_out[me]
    s_in[me] = s_out[me]

    def values(keys):
        return jnp.where(lanes(keys.shape) < HD, jnp.ones_like(keys), keys)

    def unpack(r):
        for j in range(RATIO):
            v = q_in[r, j].astype(f32)
            zero = jnp.zeros_like(v)
            q_all[r, pl.ds(j * rows, half), :] = mix(v, zero).astype(bf16)
            q_all[r, pl.ds(j * rows + half, half), :] = mix(flip(v), zero).astype(bf16)

    def scored(r, keys, count, masked):
        s = lax.dot_general(
            q_all[r], keys, (((1,), (1,)), ((), ())), preferred_element_type=f32
        )
        if masked:
            at = packed_ref[...].astype(f32)
            seen = (at >= column(0, r)) & (at <= column(1, r))
            bias = jnp.where(seen, 0.0, NEG_FILL)
            s = (s.reshape(RATIO, rows, count) + bias[None]).reshape(RATIO * rows, count)
        return s

    def blocks(rs, keys, count, masked=False, first=False):
        olds = [None if first else best[r][:, :1] for r in rs]
        sums = [None if first else acc[r] for r in rs]
        scores = [scored(r, keys, count, masked) for r in rs]
        tops, totals = [], []
        for s, old, before in zip(scores, olds, sums):
            top = jnp.max(s, axis=-1, keepdims=True)
            if not first:
                top = jnp.maximum(old, top)
            weights = jnp.exp(s - top).astype(bf16)
            total = jnp.dot(weights, vx[:count], preferred_element_type=f32)
            if not first:
                total = before * jnp.exp(old - top) + total
            tops.append(top)
            totals.append(total)
        for r, top, total in zip(rs, tops, totals):
            acc[r] = total
            best[r] = jnp.broadcast_to(top, (RATIO * rows, 128))

    def step(keys_ref, count, masked=False, first=False, last=False):
        vx[:count] = values(keys_ref())

        def body(i, carry):
            c = lax.rem(z + 1 + i, 4) if last else lax.rem(z + i, 4)
            for side in range(2):
                r = 2 * c + side
                if first:
                    pl.when(r != me)(lambda r=r: q_from(r).wait_recv())
                    unpack(r)
            blocks([2 * c, 2 * c + 1], keys_ref(), count, masked, first)
            if last:
                for side in range(2):
                    r = 2 * c + side
                    for j in range(RATIO):
                        v = acc[r, pl.ds(j * rows, rows), :]
                        v = v / flip(v)
                        o_out[r, j] = mix(flip(v[:half]), v[half:]).astype(bf16)
                    pl.when(r != me)(lambda r=r: o_to(r).start())
            return carry

        lax.fori_loop(0, 4, body, 0)

    step(lambda: p_out[me], page_rows, first=True)
    for peer in near:
        s_from(peer).wait_recv()
    step(lambda: s_in[...].reshape(8 * rows, 128), 8 * rows, masked=True)
    p_from(partner).wait_recv()
    step(lambda: p_in[partner], page_rows)
    for i in range(1, 4):
        c = chunks[i]
        p_from(2 * c + x).wait_recv()
        p_from(2 * c + 1 - x).wait_recv()
        step(
            lambda c=c: p_in[pl.ds(2 * c, 2)].reshape(2 * page_rows, 128),
            2 * page_rows,
            last=i == 3,
        )
    o_in[me] = o_out[me]
    for peer in far:
        o_from(peer).wait_recv()
    for pair in range(QH // 2):
        n, m = 2 * pair, 2 * pair + 1
        one = o_in[n // RATIO, n % RATIO].astype(f32)
        two = o_in[m // RATIO, m % RATIO].astype(f32)
        span = slice(128 * pair, 128 * pair + 128)
        attended[:half, span] = mix(one, flip(two)).astype(bf16)
        attended[half:, span] = mix(flip(one), two).astype(bf16)
    proj_copy.wait()
    for first in range(0, proj.shape[1], 512):
        span = slice(first, first + 512)
        mid_ref[:, span] = (
            stream_ref[:, span].astype(f32)
            + jnp.dot(attended[...], proj[:, span], preferred_element_type=f32)
        ).astype(bf16)
    mid = mid_ref[...].astype(f32)
    buf[me] = (
        mid * lax.rsqrt(jnp.mean(mid * mid, axis=-1, keepdims=True) + 1e-05) * gain_ref[...].reshape(1, -1)
    ).astype(bf16)
    for peer in near:
        c_from(peer).wait_recv()
    width = mid_ref.shape[1]
    local = wg.shape[0]
    cut = sendx.shape[1]
    tail = rows - cut
    parts = [pl.ds(0, cut), pl.ds(cut, tail)]
    inner = (z + 1) // 2 % 2 == 1
    outer = (z + 1) // 2 % 2 == 0
    toward = me + 2 - 4 * (z // 2)
    outside = me - 2 + 4 * (z // 2)

    def token_copy(shard, part, way):
        return send(
            buf.at[shard, parts[part]],
            buf.at[shard, parts[part]],
            ag_send.at[shard, part, way],
            ag_recv.at[shard, part],
            partner,
        )

    def to_partner(shard, part):
        token_copy(shard, part, 0).start()

    def way_copy(shard, part, device, way):
        return send(
            buf.at[shard, parts[part]],
            buf.at[shard, parts[part]],
            ag_send.at[shard, part, way],
            ag_recv.at[shard, part],
            device,
        )

    def to_center(shard, part):
        way_copy(shard, part, toward, 1).start()

    def to_outside(shard, part):
        way_copy(shard, part, outside, 2).start()

    def arrived(shard, part):
        token_copy(shard, part, 0).wait_recv()

    slots = picked.shape[0] // local

    def compute(c, first):
        tokens = buf[pl.ds(2 * c, 2)].reshape(2 * rows, width)
        code = c_in[pl.ds(2 * c, 2)].astype(f32)
        code = jnp.concatenate([code[0], code[1]], axis=1)
        shape = (slots, 2 * rows)
        row = lax.broadcasted_iota(jnp.int32, shape, 0).astype(f32)
        second = lax.broadcasted_iota(jnp.int32, (1, 2 * rows), 1) >= rows
        chosen = []
        for e in range(local):
            slot = code[e : e + 1, :]
            place = jnp.where(slot < 0.0, -1.0, jnp.where(second, slot + slots // 2, slot))
            hit = row == place
            chosen.append(jnp.where(hit, 1.0, 0.0).astype(bf16))
            for i in range(2):
                gate = code[(i + 1) * local + e : (i + 1) * local + e + 1, :]
                spread[i, e * slots : (e + 1) * slots, :] = jnp.where(hit, gate, 0.0).astype(bf16)
        picked[...] = jnp.dot(
            jnp.concatenate(chosen, axis=0), tokens, preferred_element_type=f32
        ).astype(bf16)

        def one(e, carry):
            if first:
                for copy in weight_copies(e):
                    copy.wait()
            span = pl.ds(pl.multiple_of(e * slots, 16), slots)
            some = picked[span, :]
            gate_vals = jnp.dot(some, wg[e], preferred_element_type=f32)
            up_vals = jnp.dot(some, wu[e], preferred_element_type=f32)
            hidden = (gate_vals / (1.0 + jnp.exp(-gate_vals)) * up_vals).astype(bf16)
            produced[span, :] = jnp.dot(hidden, wd[e], preferred_element_type=f32).astype(bf16)
            return carry

        lax.fori_loop(0, local, one, 0)
        total = sum(
            lax.dot_general(
                spread[i], produced[...], (((0,), (0,)), ((), ())), preferred_element_type=f32
            )
            for i in range(2)
        )
        part_sums[pl.ds(2 * c, 2)] = total.reshape(2, rows, width)
        sendx[c] = part_sums[2 * c + 1 - x, parts[0]].astype(bf16)
        across(c).start()

    def across(c):
        return send(sendx.at[c], recvx.at[c], sx_sem.at[c], rx_sem.at[c], partner)

    def add_across(c):
        across(c).wait()
        part_sums[2 * c + x, parts[0]] += recvx[c].astype(f32)

    def place(c, piece):
        if piece == 0:
            return part_sums.at[2 * c + x, parts[0]], pl.ds(0, cut)
        return part_sums.at[2 * c + piece - 1, parts[1]], pl.ds(cut + (piece - 1) * tail, tail)

    def hop(c, piece, into, sem, device):
        span = place(c, piece)[1]
        return send(
            stage.at[c, span], into.at[c, span], st_sem.at[c, piece], sem.at[c, piece], device
        )

    def outward_hop(c, piece):
        return hop(c, piece, recv_out, ro_sem, toward)

    def center_hop(c, piece):
        return hop(c, piece, recv_in, ri_sem, toward)

    def back_hop(c, piece):
        return hop(c, piece, recv_in, ri_sem, outside)

    def emit(c, piece, hop_of):
        part, span = place(c, piece)
        stage[c, span] = part[...].astype(bf16)
        hop_of(c, piece).start()

    def fold(c, piece, hop_of, ref):
        hop_of(c, piece).wait_recv()
        part, span = place(c, piece)
        part[...] += ref[c, span].astype(f32)

    def relay(c, pieces, came, ref, hop_of):
        for piece in pieces:
            if piece == 0:
                add_across(c)
            fold(c, piece, came, ref)
            emit(c, piece, hop_of)

    def early(c):
        emit(c, 1, outward_hop)
        emit(c, 2, outward_hop)

    def late(c):
        add_across(c)
        emit(c, 0, outward_hop)

    upper = z // 2
    is_inner = (z + 1) // 2 % 2

    def mirrored(c):
        return c + upper * (3 - 2 * c)

    turns = [mirrored(c) for c in (0 * z, 1 + 2 * is_inner, 3 - is_inner, 2 - is_inner)]
    near_c, far_c, mid_c = mirrored(1), mirrored(3), mirrored(2)
    out_c = mirrored(0)

    def pair(c):
        return 2 * c + x, 2 * c + 1 - x

    to_partner(me, 1)

    @pl.when(outer)
    def _():
        same, other = pair(near_c)
        to_center(me, 1)
        to_partner(me, 0)
        to_center(me, 0)
        arrived(partner, 1)
        to_center(partner, 1)
        arrived(partner, 0)
        arrived(same, 1)
        arrived(same, 0)
        to_partner(same, 0)

    @pl.when(inner)
    def _():
        same, other = pair(out_c)
        far_same, far_other = pair(far_c)
        to_outside(me, 1)
        to_center(me, 1)
        to_partner(me, 0)
        to_outside(me, 0)
        arrived(same, 1)
        to_center(same, 1)
        arrived(partner, 1)
        to_outside(partner, 1)
        to_center(partner, 1)
        arrived(same, 0)
        to_center(same, 0)
        to_partner(same, 0)
        arrived(other, 1)
        to_center(other, 1)
        to_center(me, 0)
        arrived(partner, 0)
        arrived(far_same, 1)
        to_outside(far_same, 1)
        in_same, in_other = pair(mid_c)
        arrived(in_same, 1)
        to_outside(in_same, 1)
        arrived(other, 0)

    compute(turns[0], True)

    @pl.when(outer)
    def _():
        same, other = pair(near_c)
        arrived(other, 1)
        arrived(other, 0)

    @pl.when(inner)
    def _():
        far_same, far_other = pair(far_c)
        in_same, in_other = pair(mid_c)
        arrived(far_same, 0)
        to_outside(far_same, 0)
        to_partner(far_same, 0)
        arrived(far_other, 1)
        to_outside(far_other, 1)
        arrived(in_same, 0)
        to_outside(in_same, 0)
        to_partner(in_same, 0)
        arrived(in_other, 1)
        to_outside(in_other, 1)
        arrived(far_other, 0)

    compute(turns[1], False)

    @pl.when(outer)
    def _():
        far_same, far_other = pair(far_c)
        early(near_c)
        arrived(far_same, 1)
        arrived(far_same, 0)
        to_partner(far_same, 0)
        late(near_c)
        arrived(far_other, 1)
        arrived(far_other, 0)

    @pl.when(inner)
    def _():
        arrived(pair(mid_c)[1], 0)

    compute(turns[2], False)

    @pl.when(outer)
    def _():
        in_same, in_other = pair(mid_c)
        early(far_c)
        arrived(in_same, 1)
        arrived(in_same, 0)
        to_partner(in_same, 0)
        late(far_c)
        arrived(in_other, 1)
        arrived(in_other, 0)

    @pl.when(inner)
    def _():
        relay(far_c, (1, 2), outward_hop, recv_out, center_hop)

    compute(turns[3], False)

    @pl.when(outer)
    def _():
        early(mid_c)
        late(mid_c)

    @pl.when(inner)
    def _():
        relay(far_c, (0,), outward_hop, recv_out, center_hop)
        relay(out_c, (1, 2, 0), center_hop, recv_in, back_hop)
        relay(mid_c, (1, 2, 0), outward_hop, recv_out, center_hop)

    add_across(z)
    for piece in (1, 2, 0):
        pl.when(inner)(lambda piece=piece: fold(z, piece, outward_hop, recv_out))
        fold(z, piece, center_hop, recv_in)
        if piece == 2:
            sendf[...] = part_sums[partner, parts[1]].astype(bf16)
            last = send(sendf, recvf, f_sem.at[0], f_sem.at[1], partner)
            last.start()
    o_ref[:cut, :] = (mid_ref[:cut, :].astype(f32) + part_sums[me, parts[0]]).astype(bf16)
    last.wait()
    o_ref[cut:, :] = (
        mid_ref[cut:, :].astype(f32) + (part_sums[me, parts[1]] + recvf[...].astype(f32))
    ).astype(bf16)

    for c in chunks[1:]:
        for piece in range(3):
            center_hop(c, piece).wait_send()

    for shard, part in [(me, 0), (me, 1)] + [(2 * c + x, 0) for c in chunks[1:]]:
        token_copy(shard, part, 0).wait_send()
    for shard, part in ((me, 0), (me, 1), (partner, 1)):
        way_copy(shard, part, toward, 1).wait_send()

    @pl.when(inner)
    def _():
        for way, cs in ((1, (out_c,)), (2, (z, mid_c, far_c))):
            for c in cs:
                same, other = pair(c)
                for shard, part in ((same, 0), (same, 1), (other, 1)):
                    way_copy(shard, part, toward, way).wait_send()
    for to in (q_to, s_to, p_to, o_to, c_to):
        for peer in near:
            to(peer).wait_send()


def layer(
    q, suffix, pool, table, segments, packed, stream, gain, ids, gates, proj, gate_proj, up_proj, down_proj
):
    rows = q.shape[0]
    half_dim = HD // 2
    frequency = np.tile(ROPE_BASE ** (-np.arange(half_dim) / half_dim), 4)
    frequency = jnp.asarray(frequency.astype(np.float32).reshape(1, 128))
    page_rows = pool.shape[0]
    width = stream.shape[1]
    local, _, hidden = gate_proj.shape
    cut = 5 * rows // 8
    legs = 2 * rows - cut
    vmem = pl.BlockSpec(memory_space=pltpu.VMEM)
    anywhere = pl.BlockSpec(memory_space=pl.ANY)
    bf16, f32 = jnp.bfloat16, jnp.float32
    dma = pltpu.SemaphoreType.DMA
    return pl.pallas_call(
        layer_kernel,
        out_shape=jax.ShapeDtypeStruct(stream.shape, bf16),
        in_specs=[vmem] * 11 + [anywhere] * 4,
        out_specs=vmem,
        scratch_shapes=[
            pltpu.VMEM(stream.shape, bf16),
            pltpu.VMEM((page_rows + rows, 128), f32),
            pltpu.VMEM((page_rows + rows, 128), f32),
            pltpu.VMEM(proj.shape, bf16),
            pltpu.VMEM((8, 16, rows), bf16),
            pltpu.VMEM((8, 16, rows), bf16),
            pltpu.VMEM((8, RATIO, rows // 2, 128), bf16),
            pltpu.VMEM((8, RATIO, rows // 2, 128), bf16),
            pltpu.VMEM((8, RATIO * rows, 128), bf16),
            pltpu.VMEM((8, page_rows, 128), bf16),
            pltpu.VMEM((8, page_rows, 128), bf16),
            pltpu.VMEM((8, rows, 128), bf16),
            pltpu.VMEM((8, rows, 128), bf16),
            pltpu.VMEM((2 * page_rows, 128), bf16),
            pltpu.VMEM((2, rows, 8), f32),
            pltpu.VMEM((8, RATIO * rows, 128), f32),
            pltpu.VMEM((8, RATIO * rows, 128), f32),
            pltpu.VMEM((8, RATIO, rows // 2, 128), bf16),
            pltpu.VMEM((8, RATIO, rows // 2, 128), bf16),
            pltpu.VMEM(q.shape, bf16),
            dma(()),
        ]
        + [dma((8,))] * 10
        + [
            pltpu.VMEM((local, width, hidden), bf16),
            pltpu.VMEM((local, width, hidden), bf16),
            pltpu.VMEM((local, hidden, width), bf16),
            pltpu.VMEM((8, rows, width), bf16),
            pltpu.VMEM((8, rows, width), f32),
            pltpu.VMEM((local * 2 * CAP, width), bf16),
            pltpu.VMEM((local * 2 * CAP, width), bf16),
            pltpu.VMEM((2, local * 2 * CAP, 2 * rows), bf16),
            pltpu.VMEM((4, cut, width), bf16),
            pltpu.VMEM((4, cut, width), bf16),
            pltpu.VMEM((4, legs, width), bf16),
            pltpu.VMEM((4, legs, width), bf16),
            pltpu.VMEM((4, legs, width), bf16),
            pltpu.VMEM((rows - cut, width), bf16),
            pltpu.VMEM((rows - cut, width), bf16),
            dma((local, 3)),
            dma((8, 2, 3)),
            dma((8, 2)),
            dma((4,)),
            dma((4,)),
            dma((4, 3)),
            dma((4, 3)),
            dma((4, 3)),
            dma((2,)),
        ],
        compiler_params=pltpu.CompilerParams(
            collective_id=1, has_side_effects=True, vmem_limit_bytes=60 << 20
        ),
    )(
        q,
        suffix,
        pool,
        frequency,
        table,
        segments,
        packed,
        stream,
        gain,
        ids,
        gates,
        proj,
        gate_proj,
        up_proj,
        down_proj,
    )


def shards(
    queries,
    suffix_cache,
    stream_in,
    page_pool,
    page_table,
    segment_ids,
    dealing,
    out_proj,
    norm_gain,
    expert_ids,
    expert_gates,
    gate_proj,
    up_proj,
    down_proj,
):
    tok_count = lax.axis_size("tok")
    tok_index = lax.axis_index("tok")
    rows_dev = queries.shape[1]
    width = KVH * HD
    table = page_table[0]
    pages_all = table.shape[0]
    pages_dev = page_pool.shape[1]
    page_len = page_pool.shape[2]
    pool_rows = pages_dev * page_len
    prefix_len = pages_all * page_len
    repeats = tok_count // KVH
    head_groups = [[r * KVH + h for h in range(KVH)] for r in range(repeats)]
    same_head = [[r * KVH + h for r in range(repeats)] for h in range(KVH)]
    sub = dict(axis_index_groups=head_groups) if repeats > 1 else {}

    gate_dense = jnp.sum(
        jnp.where(
            expert_ids[0][:, :, None] == jnp.arange(EXPERTS, dtype=jnp.int32)[None, None, :],
            expert_gates[0][:, :, None],
            0.0,
        ),
        axis=1,
    )

    my_slots = tok_index * pages_dev + jnp.arange(pages_dev, dtype=jnp.int32)
    logical_page = jnp.sum(
        jnp.where(
            table[:, None] == my_slots[None, :],
            jnp.arange(pages_all, dtype=jnp.int32)[:, None],
            0,
        ),
        axis=0,
    )
    pool_positions = (
        logical_page[:, None] * page_len + jnp.arange(page_len, dtype=jnp.int32)[None, :]
    ).reshape(-1)
    dealt = dealing[0]
    requests = jnp.arange(REQS, dtype=jnp.int32)
    starts = jnp.sum((segment_ids[0][:, None] < requests[None, :]).astype(jnp.int32), axis=0)
    low_all = jnp.max(
        jnp.where(starts[None, :] <= dealt[:, None], starts[None, :], 0), axis=1
    )
    my_start = tok_index * rows_dev
    my_dealt = lax.dynamic_slice_in_dim(dealt, my_start, rows_dev)
    my_low = lax.dynamic_slice_in_dim(low_all, my_start, rows_dev)
    my_positions = prefix_len + my_dealt - my_low

    if tok_count == 8:
        return layer(
            queries[0],
            suffix_cache[0],
            page_pool.reshape(pool_rows, 2 * width),
            page_table,
            segment_ids,
            dealing,
            stream_in[0],
            norm_gain,
            expert_ids[0].T,
            expert_gates[0].T,
            out_proj,
            gate_proj,
            up_proj,
            down_proj,
        )[None]

    cache = jnp.concatenate([page_pool.reshape(pool_rows, 2 * width), suffix_cache[0]], axis=0)
    positions = jnp.concatenate([pool_positions, my_positions])
    count = pool_rows + rows_dev
    keys = rotate(cache[:, :width].reshape(count, KVH, HD), positions)
    values = cache[:, width:].reshape(count, KVH, HD)
    outgoing = jnp.concatenate([keys, values], axis=-1).transpose(1, 0, 2)
    arrived = lax.all_to_all(outgoing, "tok", split_axis=0, concat_axis=0, tiled=True, **sub)
    if repeats > 1:
        arrived = lax.all_gather(
            arrived, "tok", axis=0, tiled=True, axis_index_groups=same_head
        )
    kv = jnp.concatenate(
        [
            arrived[:, :pool_rows].reshape(-1, 2 * HD),
            arrived[:, pool_rows:].reshape(-1, 2 * HD),
        ],
        axis=0,
    )

    half = rows_dev // 2
    roped = rotate(queries[0].reshape(rows_dev, QH, HD), my_positions)
    packed_q = (
        roped.reshape(2, half, KVH, RATIO, HD)
        .transpose(2, 3, 1, 0, 4)
        .reshape(KVH, RATIO, half, 2 * HD)
    )
    got_q = lax.all_to_all(packed_q, "tok", split_axis=0, concat_axis=0, tiled=True, **sub)
    got_q = jnp.concatenate([got_q[..., :HD], got_q[..., HD:]], axis=2)
    got_q = jnp.pad(got_q, ((0, 0), (0, 0), (0, 0), (0, HD)))
    row_count = KVH * rows_dev
    first_row = (tok_index // KVH) * row_count
    low_q = lax.dynamic_slice_in_dim(low_all, first_row, row_count)
    high_q = lax.dynamic_slice_in_dim(dealt, first_row, row_count)
    out = attention(got_q, kv, low_q, high_q, dealt, prefix_len)
    back = lax.all_to_all(out, "tok", split_axis=0, concat_axis=0, tiled=True, **sub)
    attended = (
        back.reshape(KVH, RATIO, half, 2, HD)
        .transpose(3, 2, 0, 1, 4)
        .reshape(rows_dev, QH * HD)
    )

    mid_round = lax.optimization_barrier(
        (
            stream_in[0].astype(jnp.float32)
            + jnp.dot(attended, out_proj, preferred_element_type=jnp.float32)
        ).astype(jnp.bfloat16)
    )
    mid_float = mid_round.astype(jnp.float32)
    normed = (
        mid_float
        * lax.rsqrt(jnp.mean(mid_float * mid_float, axis=-1, keepdims=True) + 1e-05)
        * norm_gain
    ).astype(jnp.bfloat16)

    local = gate_proj.shape[0]
    gates_all = lax.all_gather(gate_dense, "tok", axis=0, tiled=True)
    gates_mine = lax.dynamic_slice_in_dim(gates_all, tok_index * local, local, axis=1)
    gates_mine = gates_mine.T.reshape(local, tok_count * rows_dev, 1)
    tokens = lax.all_gather(normed, "tok", axis=0, tiled=True)
    sums = expert_sums(tokens, gates_mine, gate_proj, up_proj, down_proj)
    mixed = lax.psum_scatter(sums, "tok", scatter_dimension=0, tiled=True)
    return (mid_float + mixed.astype(jnp.float32)).astype(jnp.bfloat16)[None]


def solution(mesh):
    placed = (
        P("group", "tok", None),
        P("group", "tok", None),
        P("group", "tok", None),
        P("group", "tok", None, None),
        P("group", None),
        P("group", None),
        P("group", None),
        P(),
        P(),
        P("group", "tok", None),
        P("group", "tok", None),
        P("tok", None, None),
        P("tok", None, None),
        P("tok", None, None),
    )
    return jax.shard_map(
        shards, mesh=mesh, in_specs=placed, out_specs=P("group", "tok", None), check_vma=False
    )
```

```python
import functools

import jax
import jax.numpy as jnp
import numpy as np
from jax import lax
from jax.experimental import pallas as pl
from jax.experimental.pallas import tpu as pltpu
from jax.sharding import PartitionSpec as P

QH = 24
KVH = 8
HD = 64
RATIO = QH // KVH
EXPERTS = 32
REQS = 16
CAP = 40
ROPE_BASE = 10000.0
NEG_FILL = -1e30
KEY_CHUNK = 1024


def rotate(vectors, positions):
    half_dim = vectors.shape[-1] // 2
    frequency = ROPE_BASE ** (-jnp.arange(half_dim, dtype=jnp.float32) / half_dim)
    angles = positions.astype(jnp.float32)[:, None] * frequency[None, :]
    cosine = jnp.cos(angles)[:, None, :]
    sine_part = jnp.sin(angles)[:, None, :]
    first_half = vectors[..., :half_dim].astype(jnp.float32)
    second = vectors[..., half_dim:].astype(jnp.float32)
    joined = jnp.concatenate(
        [first_half * cosine - second * sine_part, first_half * sine_part + second * cosine],
        axis=-1,
    )
    return joined.astype(jnp.bfloat16)


def attention_kernel(prefix_len, q_ref, kv_ref, lo_ref, hi_ref, pk_ref, o_ref, vx_ref):
    keys = kv_ref.shape[0]
    rows = q_ref.shape[2]

    @pl.when(pl.program_id(0) == 0)
    def _():
        lane = lax.broadcasted_iota(jnp.int32, kv_ref.shape, 1)
        vx_ref[...] = jnp.where(lane < HD, jnp.ones_like(kv_ref), kv_ref[...])

    q = q_ref[0].reshape(RATIO * rows, 2 * HD)
    best = jnp.full((RATIO * rows, 1), NEG_FILL, jnp.float32)
    accum = jnp.zeros((RATIO * rows, 2 * HD), jnp.float32)
    scale = HD ** (-0.5)
    for first in range(0, keys, KEY_CHUNK):
        part = slice(first, first + KEY_CHUNK)
        scores = (
            lax.dot_general(
                q, kv_ref[part, :], (((1,), (1,)), ((), ())), preferred_element_type=jnp.float32
            )
            * scale
        )
        if first >= prefix_len:
            pk = pk_ref[:, first - prefix_len : first - prefix_len + KEY_CHUNK]
            seen = (pk >= lo_ref[0]) & (pk <= hi_ref[0])
            seen = jnp.concatenate([seen.astype(jnp.float32)] * RATIO, axis=0) > 0.5
            scores = jnp.where(seen, scores, NEG_FILL)
        new_best = jnp.maximum(best, jnp.max(scores, axis=-1, keepdims=True))
        weights = jnp.exp(scores - new_best).astype(jnp.bfloat16)
        factor = jnp.exp(best - new_best)
        accum = accum * factor + jnp.dot(
            weights, vx_ref[part, :], preferred_element_type=jnp.float32
        )
        best = new_best
    out = (accum[:, HD:] / accum[:, :HD]).astype(jnp.bfloat16).reshape(RATIO, rows, HD)
    o_ref[0] = jnp.concatenate([out[:, : rows // 2], out[:, rows // 2 :]], axis=-1)


def attention(q, kv, low, high, packed, prefix_len):
    sources, _, rows, _ = q.shape
    keys = kv.shape[0]
    suffix = keys - prefix_len
    return pl.pallas_call(
        functools.partial(attention_kernel, prefix_len),
        out_shape=jax.ShapeDtypeStruct((sources, RATIO, rows // 2, 2 * HD), jnp.bfloat16),
        grid=(sources,),
        in_specs=[
            pl.BlockSpec((1, RATIO, rows, 2 * HD), lambda i: (i, 0, 0, 0)),
            pl.BlockSpec((keys, 2 * HD), lambda i: (0, 0)),
            pl.BlockSpec((1, rows, 1), lambda i: (i, 0, 0)),
            pl.BlockSpec((1, rows, 1), lambda i: (i, 0, 0)),
            pl.BlockSpec((1, suffix), lambda i: (0, 0)),
        ],
        out_specs=pl.BlockSpec((1, RATIO, rows // 2, 2 * HD), lambda i: (i, 0, 0, 0)),
        scratch_shapes=[pltpu.VMEM((keys, 2 * HD), jnp.bfloat16)],
        compiler_params=pltpu.CompilerParams(vmem_limit_bytes=48 << 20),
    )(q, kv, low.reshape(sources, rows, 1), high.reshape(sources, rows, 1), packed.reshape(1, suffix))


def expert_kernel(x_ref, gates_ref, gate_ref, up_ref, down_ref, o_ref, acc_ref):
    expert = pl.program_id(1)
    x = x_ref[...]
    gate_vals = jnp.dot(x, gate_ref[0], preferred_element_type=jnp.float32)
    up_vals = jnp.dot(x, up_ref[0], preferred_element_type=jnp.float32)
    hidden = (gate_vals / (1.0 + jnp.exp(-gate_vals)) * up_vals).astype(jnp.bfloat16)
    produced = jnp.dot(hidden, down_ref[0], preferred_element_type=jnp.float32)
    term = gates_ref[0] * produced.astype(jnp.bfloat16).astype(jnp.float32)

    @pl.when(expert == 0)
    def _():
        acc_ref[...] = term

    @pl.when(expert > 0)
    def _():
        acc_ref[...] += term

    @pl.when(expert == pl.num_programs(1) - 1)
    def _():
        o_ref[...] = acc_ref[...].astype(jnp.bfloat16)


def expert_sums(x, gates, gate_proj, up_proj, down_proj):
    rows, width = x.shape
    experts, _, hidden = gate_proj.shape
    block = min(512, rows)
    return pl.pallas_call(
        expert_kernel,
        out_shape=jax.ShapeDtypeStruct((rows, width), jnp.bfloat16),
        grid=(rows // block, experts),
        in_specs=[
            pl.BlockSpec((block, width), lambda i, e: (i, 0)),
            pl.BlockSpec((1, block, 1), lambda i, e: (e, i, 0)),
            pl.BlockSpec((1, width, hidden), lambda i, e: (e, 0, 0)),
            pl.BlockSpec((1, width, hidden), lambda i, e: (e, 0, 0)),
            pl.BlockSpec((1, hidden, width), lambda i, e: (e, 0, 0)),
        ],
        out_specs=pl.BlockSpec((block, width), lambda i, e: (i, 0)),
        scratch_shapes=[pltpu.VMEM((block, width), jnp.float32)],
        compiler_params=pltpu.CompilerParams(vmem_limit_bytes=56 << 20),
    )(x, gates, gate_proj, up_proj, down_proj)


def route(ids_ref, gates_ref, out):
    ids = ids_ref[...].astype(jnp.float32)
    gates = gates_ref[...]
    devices = out.shape[0]
    local = EXPERTS // devices
    rows = ids.shape[1]
    expert = lax.broadcasted_iota(jnp.int32, (EXPERTS, rows), 0).astype(jnp.float32)
    chosen = jnp.zeros((EXPERTS, rows), jnp.float32)
    gate = jnp.zeros((EXPERTS, rows), jnp.float32)
    for k in range(ids.shape[0]):
        hit = expert == ids[k : k + 1, :]
        chosen = jnp.where(hit, 1.0, chosen)
        gate = jnp.where(hit, gates[k : k + 1, :], gate)
    row = lax.broadcasted_iota(jnp.int32, (rows, rows), 0)
    column = lax.broadcasted_iota(jnp.int32, (rows, rows), 1)
    before = jnp.where(row < column, 1.0, 0.0).astype(jnp.bfloat16)
    slot = jnp.dot(chosen.astype(jnp.bfloat16), before, preferred_element_type=jnp.float32)
    slot = jnp.where(chosen > 0.5, slot, -1.0)
    high = gate.astype(jnp.bfloat16).astype(jnp.float32)
    rest = gate - high
    for device in range(devices):
        span = slice(device * local, (device + 1) * local)
        out[device] = jnp.concatenate(
            [slot[span], high[span], rest[span], jnp.zeros((16 - 3 * local, rows), jnp.float32)],
            axis=0,
        ).astype(jnp.bfloat16)


def layer_kernel(
    q_ref,
    suffix_ref,
    pool_ref,
    frequency_ref,
    table_ref,
    segment_ref,
    packed_ref,
    stream_ref,
    gain_ref,
    ids_ref,
    gates_ref,
    proj_hbm,
    wg_hbm,
    wu_hbm,
    wd_hbm,
    o_ref,
    mid_ref,
    cos_ref,
    sin_ref,
    proj,
    c_out,
    c_in,
    q_out,
    q_in,
    q_all,
    p_out,
    p_in,
    s_out,
    s_in,
    vx,
    bounds,
    best,
    acc,
    o_out,
    o_in,
    attended,
    proj_sem,
    qs_sem,
    qr_sem,
    ps_sem,
    pr_sem,
    ss_sem,
    sr_sem,
    os_sem,
    or_sem,
    cs_sem,
    cr_sem,
    wg,
    wu,
    wd,
    buf,
    part_sums,
    picked,
    produced,
    spread,
    sendx,
    recvx,
    stage,
    recv_out,
    recv_in,
    sendf,
    recvf,
    w_sem,
    ag_send,
    ag_recv,
    sx_sem,
    rx_sem,
    st_sem,
    ro_sem,
    ri_sem,
    f_sem,
):
    me = lax.axis_index("tok")
    z = me // 2
    x = me % 2
    partner = z * 2 + 1 - x
    rows = q_ref.shape[0]
    half = rows // 2
    page_rows = pool_ref.shape[0]
    kv_width = KVH * HD
    f32, bf16 = jnp.float32, jnp.bfloat16

    proj_copy = pltpu.make_async_copy(proj_hbm, proj, proj_sem)
    proj_copy.start()

    barrier = pltpu.get_barrier_semaphore()
    chunks = [z, 1 + z % 2, (2 + 3 * z) % 5, 3 - 3 * (z // 2)]
    near = [partner]
    for c in chunks[1:]:
        near += [2 * c + x, 2 * c + 1 - x]
    far = near[::-1]
    for peer in near:
        pl.semaphore_signal(
            barrier, inc=1, device_id={"tok": peer}, device_id_type=pl.DeviceIdType.MESH
        )

    def send(src, dst, send_sem, recv_sem, device):
        return pltpu.make_async_remote_copy(
            src_ref=src,
            dst_ref=dst,
            send_sem=send_sem,
            recv_sem=recv_sem,
            device_id={"tok": device},
            device_id_type=pl.DeviceIdType.MESH,
        )

    def exchange(out, into, send_sem, recv_sem):
        def to(peer):
            return send(out.at[peer], into.at[me], send_sem.at[peer], recv_sem.at[me], peer)

        def came(peer):
            return send(out.at[peer], into.at[peer], send_sem.at[peer], recv_sem.at[peer], peer)

        return to, came

    q_to, q_from = exchange(q_out, q_in, qs_sem, qr_sem)
    p_to, p_from = exchange(p_out, p_in, ps_sem, pr_sem)
    s_to, s_from = exchange(s_out, s_in, ss_sem, sr_sem)
    o_to, o_from = exchange(o_out, o_in, os_sem, or_sem)
    c_to, c_from = exchange(c_out, c_in, cs_sem, cr_sem)

    def lanes(shape):
        return lax.broadcasted_iota(jnp.int32, shape, 1)

    def turn(v, cosine, sine):
        first = lanes(v.shape) % HD < HD // 2
        swapped = jnp.where(first, pltpu.roll(v, 128 - HD // 2, 1), pltpu.roll(v, HD // 2, 1))
        return (v * cosine + swapped * sine).astype(bf16).astype(f32)

    def mix(left, right):
        return jnp.where(lanes(left.shape) < HD, left, right)

    def flip(v):
        return pltpu.roll(v, HD, 1)

    pages = page_rows // 128
    split = [slice(first, first + rows) for first in range(0, 8 * rows, rows)]
    dealt = jnp.concatenate([packed_ref[:, span] for span in split], axis=0).astype(f32)
    owner = jnp.concatenate([segment_ref[:, span] for span in split], axis=0).astype(f32)
    start = jnp.zeros_like(dealt)
    for request in range(REQS):
        earlier = jnp.where(owner < request, 1.0, 0.0)
        earlier = jnp.sum(jnp.sum(earlier, axis=1, keepdims=True), axis=0, keepdims=True)
        start = jnp.where(earlier <= dealt, jnp.maximum(start, earlier), start)
    bounds[0] = start.T
    bounds[1] = dealt.T

    def column(which, r):
        v = bounds[which]
        return jnp.sum(jnp.where(lanes(v.shape) == r, v, 0.0), axis=1, keepdims=True)

    prefix_len = table_ref.shape[1] * 128
    second = lanes((rows, 128)) % HD >= HD // 2
    angles = (column(1, me) - column(0, me) + prefix_len) * frequency_ref[...]
    cos_ref[page_rows:, :] = jnp.cos(angles)
    sine = jnp.sin(angles)
    sin_ref[page_rows:, :] = jnp.where(second, sine, -sine)

    def tables():
        table = table_ref[...]
        at = lax.broadcasted_iota(jnp.int32, table.shape, 1)
        lane = lanes((128, 128))
        logical = jnp.zeros((128, 128), f32)
        for i in range(pages):
            page = jnp.sum(
                jnp.where(table == me * pages + i, at, 0).astype(f32), axis=1, keepdims=True
            )
            logical = jnp.where(lane // (HD // 2) == i, page, logical)
        row = lax.broadcasted_iota(jnp.int32, (128, 128), 0).astype(f32)
        angles = (logical * 128.0 + row) * frequency_ref[...]
        for ref, every in ((cos_ref, jnp.cos(angles)), (sin_ref, jnp.sin(angles))):
            for i in range(pages):
                v = pltpu.roll(every, (4 - i) * (HD // 2) % 128, 1) if i else every
                v = jnp.where(lane < HD // 2, v, pltpu.roll(v, HD // 2, 1))
                v = jnp.where(lane < HD, v, pltpu.roll(v, HD, 1))
                if ref is sin_ref:
                    v = jnp.where(second, v, -v)
                ref[128 * i : 128 * i + 128, :] = v

    cosine, sine = cos_ref[page_rows:, :], sin_ref[page_rows:, :]
    for pair in range(QH // 2):
        v = q_ref[:, 128 * pair : 128 * pair + 128].astype(f32)
        v = turn(v, cosine, sine) * (HD**-0.5)
        top, low = v[:half], v[half:]
        for n, packed in ((2 * pair, mix(top, flip(low))), (2 * pair + 1, mix(flip(top), low))):
            q_out[n // RATIO, n % RATIO] = packed.astype(bf16)
    pl.semaphore_wait(barrier, 7)
    for peer in near:
        q_to(peer).start()

    def caches(src, first, table, out, at):
        span = pl.ds(first, 128)
        cosine, sine = cos_ref[pl.ds(table, 128), :], sin_ref[pl.ds(table, 128), :]
        for pair in range(KVH // 2):
            k = src[span, 128 * pair : 128 * pair + 128].astype(f32)
            k = turn(k, cosine, sine)
            v = src[span, kv_width + 128 * pair : kv_width + 128 * pair + 128].astype(f32)
            out[2 * pair, span, :] = mix(k, flip(v)).astype(bf16)
            out[2 * pair + 1, span, :] = mix(flip(k), v).astype(bf16)

    caches(suffix_ref, 0, page_rows, s_out, 0)
    for peer in near:
        s_to(peer).start()

    tables()

    def prepare(i, carry):
        first = pl.multiple_of(i * 128, 128)
        caches(pool_ref, first, first, p_out, 0)
        return carry

    lax.fori_loop(0, page_rows // 128, prepare, 0)
    for peer in near:
        p_to(peer).start()

    def weight_copies(e):
        return [
            pltpu.make_async_copy(src.at[e], dst.at[e], w_sem.at[e, i])
            for i, (src, dst) in enumerate([(wg_hbm, wg), (wu_hbm, wu), (wd_hbm, wd)])
        ]

    for e in range(wg.shape[0]):
        for copy in weight_copies(e):
            copy.start()

    route(ids_ref, gates_ref, c_out)
    for peer in near:
        c_to(peer).start()
    c_in[me] = c_out[me]
    q_in[me] = q_out[me]
    s_in[me] = s_out[me]

    def values(keys):
        return jnp.where(lanes(keys.shape) < HD, jnp.ones_like(keys), keys)

    def unpack(r):
        for j in range(RATIO):
            v = q_in[r, j].astype(f32)
            zero = jnp.zeros_like(v)
            q_all[r, pl.ds(j * rows, half), :] = mix(v, zero).astype(bf16)
            q_all[r, pl.ds(j * rows + half, half), :] = mix(flip(v), zero).astype(bf16)

    def scored(r, keys, count, masked):
        s = lax.dot_general(
            q_all[r], keys, (((1,), (1,)), ((), ())), preferred_element_type=f32
        )
        if masked:
            at = packed_ref[...].astype(f32)
            seen = (at >= column(0, r)) & (at <= column(1, r))
            bias = jnp.where(seen, 0.0, NEG_FILL)
            s = (s.reshape(RATIO, rows, count) + bias[None]).reshape(RATIO * rows, count)
        return s

    def blocks(rs, keys, count, masked=False, first=False):
        olds = [None if first else best[r] for r in rs]
        sums = [None if first else acc[r] for r in rs]
        scores = [scored(r, keys, count, masked) for r in rs]
        tops, totals = [], []
        for s, old, before in zip(scores, olds, sums):
            top = jnp.broadcast_to(jnp.max(s, axis=-1, keepdims=True), (RATIO * rows, 128))
            if not first:
                top = jnp.maximum(old, top)
            weights = jnp.exp(s - jnp.concatenate([top] * (count // 128), axis=1)).astype(bf16)
            total = jnp.dot(weights, vx[:count], preferred_element_type=f32)
            if not first:
                total = before * jnp.exp(old - top) + total
            tops.append(top)
            totals.append(total)
        for r, top, total in zip(rs, tops, totals):
            acc[r] = total
            best[r] = top

    def step(keys_ref, count, masked=False, first=False, last=False):
        vx[:count] = values(keys_ref())

        def body(i, carry):
            c = lax.rem(z + 1 + i, 4) if last else lax.rem(z + i, 4)
            for side in range(2):
                r = 2 * c + side
                if first:
                    pl.when(r != me)(lambda r=r: q_from(r).wait_recv())
                    unpack(r)
            blocks([2 * c, 2 * c + 1], keys_ref(), count, masked, first)
            if last:
                for side in range(2):
                    r = 2 * c + side
                    for j in range(RATIO):
                        v = acc[r, pl.ds(j * rows, rows), :]
                        v = v / flip(v)
                        o_out[r, j] = mix(flip(v[:half]), v[half:]).astype(bf16)
                    pl.when(r != me)(lambda r=r: o_to(r).start())
            return carry

        lax.fori_loop(0, 4, body, 0)

    step(lambda: p_out[me], page_rows, first=True)
    for peer in near:
        s_from(peer).wait_recv()
    step(lambda: s_in[...].reshape(8 * rows, 128), 8 * rows, masked=True)
    p_from(partner).wait_recv()
    step(lambda: p_in[partner], page_rows)
    for i in range(1, 4):
        c = chunks[i]
        p_from(2 * c + x).wait_recv()
        p_from(2 * c + 1 - x).wait_recv()
        step(
            lambda c=c: p_in[pl.ds(2 * c, 2)].reshape(2 * page_rows, 128),
            2 * page_rows,
            last=i == 3,
        )
    o_in[me] = o_out[me]
    for peer in far:
        o_from(peer).wait_recv()
    for pair in range(QH // 2):
        n, m = 2 * pair, 2 * pair + 1
        one = o_in[n // RATIO, n % RATIO].astype(f32)
        two = o_in[m // RATIO, m % RATIO].astype(f32)
        span = slice(128 * pair, 128 * pair + 128)
        attended[:half, span] = mix(one, flip(two)).astype(bf16)
        attended[half:, span] = mix(flip(one), two).astype(bf16)
    proj_copy.wait()
    for first in range(0, proj.shape[1], 512):
        span = slice(first, first + 512)
        mid_ref[:, span] = (
            stream_ref[:, span].astype(f32)
            + jnp.dot(attended[...], proj[:, span], preferred_element_type=f32)
        ).astype(bf16)
    mid = mid_ref[...].astype(f32)
    buf[me] = (
        mid * lax.rsqrt(jnp.mean(mid * mid, axis=-1, keepdims=True) + 1e-05) * gain_ref[...].reshape(1, -1)
    ).astype(bf16)
    for peer in near:
        c_from(peer).wait_recv()
    width = mid_ref.shape[1]
    local = wg.shape[0]
    cut = sendx.shape[1]
    tail = rows - cut
    parts = [pl.ds(0, cut), pl.ds(cut, tail)]
    inner = (z + 1) // 2 % 2 == 1
    outer = (z + 1) // 2 % 2 == 0
    toward = me + 2 - 4 * (z // 2)
    outside = me - 2 + 4 * (z // 2)

    def token_copy(shard, part, way):
        return send(
            buf.at[shard, parts[part]],
            buf.at[shard, parts[part]],
            ag_send.at[shard, part, way],
            ag_recv.at[shard, part],
            partner,
        )

    def to_partner(shard, part):
        token_copy(shard, part, 0).start()

    def way_copy(shard, part, device, way):
        return send(
            buf.at[shard, parts[part]],
            buf.at[shard, parts[part]],
            ag_send.at[shard, part, way],
            ag_recv.at[shard, part],
            device,
        )

    def to_center(shard, part):
        way_copy(shard, part, toward, 1).start()

    def to_outside(shard, part):
        way_copy(shard, part, outside, 2).start()

    def arrived(shard, part):
        token_copy(shard, part, 0).wait_recv()

    slots = picked.shape[0] // local

    def compute(c, first):
        tokens = buf[pl.ds(2 * c, 2)].reshape(2 * rows, width)
        code = c_in[pl.ds(2 * c, 2)].astype(f32)
        code = jnp.concatenate([code[0], code[1]], axis=1)
        shape = (slots, 2 * rows)
        row = lax.broadcasted_iota(jnp.int32, shape, 0).astype(f32)
        second = lax.broadcasted_iota(jnp.int32, (1, 2 * rows), 1) >= rows
        chosen = []
        for e in range(local):
            slot = code[e : e + 1, :]
            place = jnp.where(slot < 0.0, -1.0, jnp.where(second, slot + slots // 2, slot))
            hit = row == place
            chosen.append(jnp.where(hit, 1.0, 0.0).astype(bf16))
            for i in range(2):
                gate = code[(i + 1) * local + e : (i + 1) * local + e + 1, :]
                spread[i, e * slots : (e + 1) * slots, :] = jnp.where(hit, gate, 0.0).astype(bf16)
        picked[...] = jnp.dot(
            jnp.concatenate(chosen, axis=0), tokens, preferred_element_type=f32
        ).astype(bf16)

        def one(e, carry):
            if first:
                for copy in weight_copies(e):
                    copy.wait()
            span = pl.ds(pl.multiple_of(e * slots, 16), slots)
            some = picked[span, :]
            gate_vals = jnp.dot(some, wg[e], preferred_element_type=f32)
            up_vals = jnp.dot(some, wu[e], preferred_element_type=f32)
            hidden = (gate_vals / (1.0 + jnp.exp(-gate_vals)) * up_vals).astype(bf16)
            produced[span, :] = jnp.dot(hidden, wd[e], preferred_element_type=f32).astype(bf16)
            return carry

        lax.fori_loop(0, local, one, 0, unroll=2)
        total = sum(
            lax.dot_general(
                spread[i], produced[...], (((0,), (0,)), ((), ())), preferred_element_type=f32
            )
            for i in range(2)
        )
        part_sums[pl.ds(2 * c, 2)] = total.reshape(2, rows, width)
        sendx[c] = part_sums[2 * c + 1 - x, parts[0]].astype(bf16)
        across(c).start()

    def across(c):
        return send(sendx.at[c], recvx.at[c], sx_sem.at[c], rx_sem.at[c], partner)

    def add_across(c):
        across(c).wait()
        part_sums[2 * c + x, parts[0]] += recvx[c].astype(f32)

    def place(c, piece):
        if piece == 0:
            return part_sums.at[2 * c + x, parts[0]], pl.ds(0, cut)
        return part_sums.at[2 * c + piece - 1, parts[1]], pl.ds(cut + (piece - 1) * tail, tail)

    def hop(c, piece, into, sem, device):
        span = place(c, piece)[1]
        return send(
            stage.at[c, span], into.at[c, span], st_sem.at[c, piece], sem.at[c, piece], device
        )

    def outward_hop(c, piece):
        return hop(c, piece, recv_out, ro_sem, toward)

    def center_hop(c, piece):
        return hop(c, piece, recv_in, ri_sem, toward)

    def back_hop(c, piece):
        return hop(c, piece, recv_in, ri_sem, outside)

    def emit(c, piece, hop_of):
        part, span = place(c, piece)
        stage[c, span] = part[...].astype(bf16)
        hop_of(c, piece).start()

    def fold(c, piece, hop_of, ref):
        hop_of(c, piece).wait_recv()
        part, span = place(c, piece)
        part[...] += ref[c, span].astype(f32)

    def relay(c, pieces, came, ref, hop_of):
        for piece in pieces:
            if piece == 0:
                add_across(c)
            fold(c, piece, came, ref)
            emit(c, piece, hop_of)

    def early(c):
        emit(c, 1, outward_hop)
        emit(c, 2, outward_hop)

    def late(c):
        add_across(c)
        emit(c, 0, outward_hop)

    upper = z // 2
    is_inner = (z + 1) // 2 % 2

    def mirrored(c):
        return c + upper * (3 - 2 * c)

    turns = [mirrored(c) for c in (0 * z, 1 + 2 * is_inner, 3 - is_inner, 2 - is_inner)]
    near_c, far_c, mid_c = mirrored(1), mirrored(3), mirrored(2)
    out_c = mirrored(0)

    def pair(c):
        return 2 * c + x, 2 * c + 1 - x

    to_partner(me, 1)

    @pl.when(outer)
    def _():
        same, other = pair(near_c)
        to_center(me, 1)
        to_partner(me, 0)
        to_center(me, 0)
        arrived(partner, 1)
        to_center(partner, 1)
        arrived(partner, 0)
        arrived(same, 1)
        arrived(same, 0)
        to_partner(same, 0)

    @pl.when(inner)
    def _():
        same, other = pair(out_c)
        far_same, far_other = pair(far_c)
        to_outside(me, 1)
        to_center(me, 1)
        to_partner(me, 0)
        to_outside(me, 0)
        arrived(same, 1)
        to_center(same, 1)
        arrived(partner, 1)
        to_outside(partner, 1)
        to_center(partner, 1)
        arrived(same, 0)
        to_center(same, 0)
        to_partner(same, 0)
        arrived(other, 1)
        to_center(other, 1)
        to_center(me, 0)
        arrived(partner, 0)
        arrived(far_same, 1)
        to_outside(far_same, 1)
        in_same, in_other = pair(mid_c)
        arrived(in_same, 1)
        to_outside(in_same, 1)
        arrived(other, 0)

    compute(turns[0], True)

    @pl.when(outer)
    def _():
        same, other = pair(near_c)
        arrived(other, 1)
        arrived(other, 0)

    @pl.when(inner)
    def _():
        far_same, far_other = pair(far_c)
        in_same, in_other = pair(mid_c)
        arrived(far_same, 0)
        to_outside(far_same, 0)
        to_partner(far_same, 0)
        arrived(far_other, 1)
        to_outside(far_other, 1)
        arrived(in_same, 0)
        to_outside(in_same, 0)
        to_partner(in_same, 0)
        arrived(in_other, 1)
        to_outside(in_other, 1)
        arrived(far_other, 0)

    compute(turns[1], False)

    @pl.when(outer)
    def _():
        far_same, far_other = pair(far_c)
        early(near_c)
        arrived(far_same, 1)
        arrived(far_same, 0)
        to_partner(far_same, 0)
        late(near_c)
        arrived(far_other, 1)
        arrived(far_other, 0)

    @pl.when(inner)
    def _():
        arrived(pair(mid_c)[1], 0)

    compute(turns[2], False)

    @pl.when(outer)
    def _():
        in_same, in_other = pair(mid_c)
        early(far_c)
        arrived(in_same, 1)
        arrived(in_same, 0)
        to_partner(in_same, 0)
        late(far_c)
        arrived(in_other, 1)
        arrived(in_other, 0)

    compute(turns[3], False)

    @pl.when(outer)
    def _():
        early(mid_c)
        late(mid_c)

    @pl.when(inner)
    def _():
        relay(far_c, (1, 2, 0), outward_hop, recv_out, center_hop)
        relay(out_c, (1, 2), center_hop, recv_in, back_hop)
        relay(mid_c, (1, 2), outward_hop, recv_out, center_hop)
        relay(out_c, (0,), center_hop, recv_in, back_hop)
        relay(mid_c, (0,), outward_hop, recv_out, center_hop)

    add_across(z)
    for piece in (1, 2, 0):
        pl.when(inner)(lambda piece=piece: fold(z, piece, outward_hop, recv_out))
        fold(z, piece, center_hop, recv_in)
        if piece == 2:
            sendf[...] = part_sums[partner, parts[1]].astype(bf16)
            last = send(sendf, recvf, f_sem.at[0], f_sem.at[1], partner)
            last.start()
    o_ref[:cut, :] = (mid_ref[:cut, :].astype(f32) + part_sums[me, parts[0]]).astype(bf16)
    last.wait()
    o_ref[cut:, :] = (
        mid_ref[cut:, :].astype(f32) + (part_sums[me, parts[1]] + recvf[...].astype(f32))
    ).astype(bf16)

    for c in chunks[1:]:
        for piece in range(3):
            center_hop(c, piece).wait_send()

    for shard, part in [(me, 0), (me, 1)] + [(2 * c + x, 0) for c in chunks[1:]]:
        token_copy(shard, part, 0).wait_send()
    for shard, part in ((me, 0), (me, 1), (partner, 1)):
        way_copy(shard, part, toward, 1).wait_send()

    @pl.when(inner)
    def _():
        for way, cs in ((1, (out_c,)), (2, (z, mid_c, far_c))):
            for c in cs:
                same, other = pair(c)
                for shard, part in ((same, 0), (same, 1), (other, 1)):
                    way_copy(shard, part, toward, way).wait_send()
    for to in (q_to, s_to, p_to, o_to, c_to):
        for peer in near:
            to(peer).wait_send()


def layer(
    q, suffix, pool, table, segments, packed, stream, gain, ids, gates, proj, gate_proj, up_proj, down_proj
):
    rows = q.shape[0]
    half_dim = HD // 2
    frequency = np.tile(ROPE_BASE ** (-np.arange(half_dim) / half_dim), 4)
    frequency = jnp.asarray(frequency.astype(np.float32).reshape(1, 128))
    page_rows = pool.shape[0]
    width = stream.shape[1]
    local, _, hidden = gate_proj.shape
    cut = 5 * rows // 8
    legs = 2 * rows - cut
    vmem = pl.BlockSpec(memory_space=pltpu.VMEM)
    anywhere = pl.BlockSpec(memory_space=pl.ANY)
    bf16, f32 = jnp.bfloat16, jnp.float32
    dma = pltpu.SemaphoreType.DMA
    return pl.pallas_call(
        layer_kernel,
        out_shape=jax.ShapeDtypeStruct(stream.shape, bf16),
        in_specs=[vmem] * 11 + [anywhere] * 4,
        out_specs=vmem,
        scratch_shapes=[
            pltpu.VMEM(stream.shape, bf16),
            pltpu.VMEM((page_rows + rows, 128), f32),
            pltpu.VMEM((page_rows + rows, 128), f32),
            pltpu.VMEM(proj.shape, bf16),
            pltpu.VMEM((8, 16, rows), bf16),
            pltpu.VMEM((8, 16, rows), bf16),
            pltpu.VMEM((8, RATIO, rows // 2, 128), bf16),
            pltpu.VMEM((8, RATIO, rows // 2, 128), bf16),
            pltpu.VMEM((8, RATIO * rows, 128), bf16),
            pltpu.VMEM((8, page_rows, 128), bf16),
            pltpu.VMEM((8, page_rows, 128), bf16),
            pltpu.VMEM((8, rows, 128), bf16),
            pltpu.VMEM((8, rows, 128), bf16),
            pltpu.VMEM((2 * page_rows, 128), bf16),
            pltpu.VMEM((2, rows, 8), f32),
            pltpu.VMEM((8, RATIO * rows, 128), f32),
            pltpu.VMEM((8, RATIO * rows, 128), f32),
            pltpu.VMEM((8, RATIO, rows // 2, 128), bf16),
            pltpu.VMEM((8, RATIO, rows // 2, 128), bf16),
            pltpu.VMEM(q.shape, bf16),
            dma(()),
        ]
        + [dma((8,))] * 10
        + [
            pltpu.VMEM((local, width, hidden), bf16),
            pltpu.VMEM((local, width, hidden), bf16),
            pltpu.VMEM((local, hidden, width), bf16),
            pltpu.VMEM((8, rows, width), bf16),
            pltpu.VMEM((8, rows, width), f32),
            pltpu.VMEM((local * 2 * CAP, width), bf16),
            pltpu.VMEM((local * 2 * CAP, width), bf16),
            pltpu.VMEM((2, local * 2 * CAP, 2 * rows), bf16),
            pltpu.VMEM((4, cut, width), bf16),
            pltpu.VMEM((4, cut, width), bf16),
            pltpu.VMEM((4, legs, width), bf16),
            pltpu.VMEM((4, legs, width), bf16),
            pltpu.VMEM((4, legs, width), bf16),
            pltpu.VMEM((rows - cut, width), bf16),
            pltpu.VMEM((rows - cut, width), bf16),
            dma((local, 3)),
            dma((8, 2, 3)),
            dma((8, 2)),
            dma((4,)),
            dma((4,)),
            dma((4, 3)),
            dma((4, 3)),
            dma((4, 3)),
            dma((2,)),
        ],
        compiler_params=pltpu.CompilerParams(
            collective_id=1, has_side_effects=True, vmem_limit_bytes=60 << 20
        ),
    )(
        q,
        suffix,
        pool,
        frequency,
        table,
        segments,
        packed,
        stream,
        gain,
        ids,
        gates,
        proj,
        gate_proj,
        up_proj,
        down_proj,
    )


def shards(
    queries,
    suffix_cache,
    stream_in,
    page_pool,
    page_table,
    segment_ids,
    dealing,
    out_proj,
    norm_gain,
    expert_ids,
    expert_gates,
    gate_proj,
    up_proj,
    down_proj,
):
    tok_count = lax.axis_size("tok")
    tok_index = lax.axis_index("tok")
    rows_dev = queries.shape[1]
    width = KVH * HD
    table = page_table[0]
    pages_all = table.shape[0]
    pages_dev = page_pool.shape[1]
    page_len = page_pool.shape[2]
    pool_rows = pages_dev * page_len
    prefix_len = pages_all * page_len
    repeats = tok_count // KVH
    head_groups = [[r * KVH + h for h in range(KVH)] for r in range(repeats)]
    same_head = [[r * KVH + h for r in range(repeats)] for h in range(KVH)]
    sub = dict(axis_index_groups=head_groups) if repeats > 1 else {}

    gate_dense = jnp.sum(
        jnp.where(
            expert_ids[0][:, :, None] == jnp.arange(EXPERTS, dtype=jnp.int32)[None, None, :],
            expert_gates[0][:, :, None],
            0.0,
        ),
        axis=1,
    )

    my_slots = tok_index * pages_dev + jnp.arange(pages_dev, dtype=jnp.int32)
    logical_page = jnp.sum(
        jnp.where(
            table[:, None] == my_slots[None, :],
            jnp.arange(pages_all, dtype=jnp.int32)[:, None],
            0,
        ),
        axis=0,
    )
    pool_positions = (
        logical_page[:, None] * page_len + jnp.arange(page_len, dtype=jnp.int32)[None, :]
    ).reshape(-1)
    dealt = dealing[0]
    requests = jnp.arange(REQS, dtype=jnp.int32)
    starts = jnp.sum((segment_ids[0][:, None] < requests[None, :]).astype(jnp.int32), axis=0)
    low_all = jnp.max(
        jnp.where(starts[None, :] <= dealt[:, None], starts[None, :], 0), axis=1
    )
    my_start = tok_index * rows_dev
    my_dealt = lax.dynamic_slice_in_dim(dealt, my_start, rows_dev)
    my_low = lax.dynamic_slice_in_dim(low_all, my_start, rows_dev)
    my_positions = prefix_len + my_dealt - my_low

    if tok_count == 8:
        return layer(
            queries[0],
            suffix_cache[0],
            page_pool.reshape(pool_rows, 2 * width),
            page_table,
            segment_ids,
            dealing,
            stream_in[0],
            norm_gain,
            expert_ids[0].T,
            expert_gates[0].T,
            out_proj,
            gate_proj,
            up_proj,
            down_proj,
        )[None]

    cache = jnp.concatenate([page_pool.reshape(pool_rows, 2 * width), suffix_cache[0]], axis=0)
    positions = jnp.concatenate([pool_positions, my_positions])
    count = pool_rows + rows_dev
    keys = rotate(cache[:, :width].reshape(count, KVH, HD), positions)
    values = cache[:, width:].reshape(count, KVH, HD)
    outgoing = jnp.concatenate([keys, values], axis=-1).transpose(1, 0, 2)
    arrived = lax.all_to_all(outgoing, "tok", split_axis=0, concat_axis=0, tiled=True, **sub)
    if repeats > 1:
        arrived = lax.all_gather(
            arrived, "tok", axis=0, tiled=True, axis_index_groups=same_head
        )
    kv = jnp.concatenate(
        [
            arrived[:, :pool_rows].reshape(-1, 2 * HD),
            arrived[:, pool_rows:].reshape(-1, 2 * HD),
        ],
        axis=0,
    )

    half = rows_dev // 2
    roped = rotate(queries[0].reshape(rows_dev, QH, HD), my_positions)
    packed_q = (
        roped.reshape(2, half, KVH, RATIO, HD)
        .transpose(2, 3, 1, 0, 4)
        .reshape(KVH, RATIO, half, 2 * HD)
    )
    got_q = lax.all_to_all(packed_q, "tok", split_axis=0, concat_axis=0, tiled=True, **sub)
    got_q = jnp.concatenate([got_q[..., :HD], got_q[..., HD:]], axis=2)
    got_q = jnp.pad(got_q, ((0, 0), (0, 0), (0, 0), (0, HD)))
    row_count = KVH * rows_dev
    first_row = (tok_index // KVH) * row_count
    low_q = lax.dynamic_slice_in_dim(low_all, first_row, row_count)
    high_q = lax.dynamic_slice_in_dim(dealt, first_row, row_count)
    out = attention(got_q, kv, low_q, high_q, dealt, prefix_len)
    back = lax.all_to_all(out, "tok", split_axis=0, concat_axis=0, tiled=True, **sub)
    attended = (
        back.reshape(KVH, RATIO, half, 2, HD)
        .transpose(3, 2, 0, 1, 4)
        .reshape(rows_dev, QH * HD)
    )

    mid_round = lax.optimization_barrier(
        (
            stream_in[0].astype(jnp.float32)
            + jnp.dot(attended, out_proj, preferred_element_type=jnp.float32)
        ).astype(jnp.bfloat16)
    )
    mid_float = mid_round.astype(jnp.float32)
    normed = (
        mid_float
        * lax.rsqrt(jnp.mean(mid_float * mid_float, axis=-1, keepdims=True) + 1e-05)
        * norm_gain
    ).astype(jnp.bfloat16)

    local = gate_proj.shape[0]
    gates_all = lax.all_gather(gate_dense, "tok", axis=0, tiled=True)
    gates_mine = lax.dynamic_slice_in_dim(gates_all, tok_index * local, local, axis=1)
    gates_mine = gates_mine.T.reshape(local, tok_count * rows_dev, 1)
    tokens = lax.all_gather(normed, "tok", axis=0, tiled=True)
    sums = expert_sums(tokens, gates_mine, gate_proj, up_proj, down_proj)
    mixed = lax.psum_scatter(sums, "tok", scatter_dimension=0, tiled=True)
    return (mid_float + mixed.astype(jnp.float32)).astype(jnp.bfloat16)[None]


def solution(mesh):
    placed = (
        P("group", "tok", None),
        P("group", "tok", None),
        P("group", "tok", None),
        P("group", "tok", None, None),
        P("group", None),
        P("group", None),
        P("group", None),
        P(),
        P(),
        P("group", "tok", None),
        P("group", "tok", None),
        P("tok", None, None),
        P("tok", None, None),
        P("tok", None, None),
    )
    return jax.shard_map(
        shards, mesh=mesh, in_specs=placed, out_specs=P("group", "tok", None), check_vma=False
    )
```

```python
import functools

import jax
import jax.numpy as jnp
import numpy as np
from jax import lax
from jax.experimental import pallas as pl
from jax.experimental.pallas import tpu as pltpu
from jax.sharding import PartitionSpec as P

QH = 24
KVH = 8
HD = 64
RATIO = QH // KVH
EXPERTS = 32
REQS = 16
CAP = 40
ROPE_BASE = 10000.0
NEG_FILL = -1e30
KEY_CHUNK = 1024


def rotate(vectors, positions):
    half_dim = vectors.shape[-1] // 2
    frequency = ROPE_BASE ** (-jnp.arange(half_dim, dtype=jnp.float32) / half_dim)
    angles = positions.astype(jnp.float32)[:, None] * frequency[None, :]
    cosine = jnp.cos(angles)[:, None, :]
    sine_part = jnp.sin(angles)[:, None, :]
    first_half = vectors[..., :half_dim].astype(jnp.float32)
    second = vectors[..., half_dim:].astype(jnp.float32)
    joined = jnp.concatenate(
        [first_half * cosine - second * sine_part, first_half * sine_part + second * cosine],
        axis=-1,
    )
    return joined.astype(jnp.bfloat16)


def attention_kernel(prefix_len, q_ref, kv_ref, lo_ref, hi_ref, pk_ref, o_ref, vx_ref):
    keys = kv_ref.shape[0]
    rows = q_ref.shape[2]

    @pl.when(pl.program_id(0) == 0)
    def _():
        lane = lax.broadcasted_iota(jnp.int32, kv_ref.shape, 1)
        vx_ref[...] = jnp.where(lane < HD, jnp.ones_like(kv_ref), kv_ref[...])

    q = q_ref[0].reshape(RATIO * rows, 2 * HD)
    best = jnp.full((RATIO * rows, 1), NEG_FILL, jnp.float32)
    accum = jnp.zeros((RATIO * rows, 2 * HD), jnp.float32)
    scale = HD ** (-0.5)
    for first in range(0, keys, KEY_CHUNK):
        part = slice(first, first + KEY_CHUNK)
        scores = (
            lax.dot_general(
                q, kv_ref[part, :], (((1,), (1,)), ((), ())), preferred_element_type=jnp.float32
            )
            * scale
        )
        if first >= prefix_len:
            pk = pk_ref[:, first - prefix_len : first - prefix_len + KEY_CHUNK]
            seen = (pk >= lo_ref[0]) & (pk <= hi_ref[0])
            seen = jnp.concatenate([seen.astype(jnp.float32)] * RATIO, axis=0) > 0.5
            scores = jnp.where(seen, scores, NEG_FILL)
        new_best = jnp.maximum(best, jnp.max(scores, axis=-1, keepdims=True))
        weights = jnp.exp(scores - new_best).astype(jnp.bfloat16)
        factor = jnp.exp(best - new_best)
        accum = accum * factor + jnp.dot(
            weights, vx_ref[part, :], preferred_element_type=jnp.float32
        )
        best = new_best
    out = (accum[:, HD:] / accum[:, :HD]).astype(jnp.bfloat16).reshape(RATIO, rows, HD)
    o_ref[0] = jnp.concatenate([out[:, : rows // 2], out[:, rows // 2 :]], axis=-1)


def attention(q, kv, low, high, packed, prefix_len):
    sources, _, rows, _ = q.shape
    keys = kv.shape[0]
    suffix = keys - prefix_len
    return pl.pallas_call(
        functools.partial(attention_kernel, prefix_len),
        out_shape=jax.ShapeDtypeStruct((sources, RATIO, rows // 2, 2 * HD), jnp.bfloat16),
        grid=(sources,),
        in_specs=[
            pl.BlockSpec((1, RATIO, rows, 2 * HD), lambda i: (i, 0, 0, 0)),
            pl.BlockSpec((keys, 2 * HD), lambda i: (0, 0)),
            pl.BlockSpec((1, rows, 1), lambda i: (i, 0, 0)),
            pl.BlockSpec((1, rows, 1), lambda i: (i, 0, 0)),
            pl.BlockSpec((1, suffix), lambda i: (0, 0)),
        ],
        out_specs=pl.BlockSpec((1, RATIO, rows // 2, 2 * HD), lambda i: (i, 0, 0, 0)),
        scratch_shapes=[pltpu.VMEM((keys, 2 * HD), jnp.bfloat16)],
        compiler_params=pltpu.CompilerParams(vmem_limit_bytes=48 << 20),
    )(q, kv, low.reshape(sources, rows, 1), high.reshape(sources, rows, 1), packed.reshape(1, suffix))


def expert_kernel(x_ref, gates_ref, gate_ref, up_ref, down_ref, o_ref, acc_ref):
    expert = pl.program_id(1)
    x = x_ref[...]
    gate_vals = jnp.dot(x, gate_ref[0], preferred_element_type=jnp.float32)
    up_vals = jnp.dot(x, up_ref[0], preferred_element_type=jnp.float32)
    hidden = (gate_vals / (1.0 + jnp.exp(-gate_vals)) * up_vals).astype(jnp.bfloat16)
    produced = jnp.dot(hidden, down_ref[0], preferred_element_type=jnp.float32)
    term = gates_ref[0] * produced.astype(jnp.bfloat16).astype(jnp.float32)

    @pl.when(expert == 0)
    def _():
        acc_ref[...] = term

    @pl.when(expert > 0)
    def _():
        acc_ref[...] += term

    @pl.when(expert == pl.num_programs(1) - 1)
    def _():
        o_ref[...] = acc_ref[...].astype(jnp.bfloat16)


def expert_sums(x, gates, gate_proj, up_proj, down_proj):
    rows, width = x.shape
    experts, _, hidden = gate_proj.shape
    block = min(512, rows)
    return pl.pallas_call(
        expert_kernel,
        out_shape=jax.ShapeDtypeStruct((rows, width), jnp.bfloat16),
        grid=(rows // block, experts),
        in_specs=[
            pl.BlockSpec((block, width), lambda i, e: (i, 0)),
            pl.BlockSpec((1, block, 1), lambda i, e: (e, i, 0)),
            pl.BlockSpec((1, width, hidden), lambda i, e: (e, 0, 0)),
            pl.BlockSpec((1, width, hidden), lambda i, e: (e, 0, 0)),
            pl.BlockSpec((1, hidden, width), lambda i, e: (e, 0, 0)),
        ],
        out_specs=pl.BlockSpec((block, width), lambda i, e: (i, 0)),
        scratch_shapes=[pltpu.VMEM((block, width), jnp.float32)],
        compiler_params=pltpu.CompilerParams(vmem_limit_bytes=56 << 20),
    )(x, gates, gate_proj, up_proj, down_proj)


def route(ids_ref, gates_ref, out):
    ids = ids_ref[...].astype(jnp.float32)
    gates = gates_ref[...]
    devices = out.shape[0]
    local = EXPERTS // devices
    rows = ids.shape[1]
    expert = lax.broadcasted_iota(jnp.int32, (EXPERTS, rows), 0).astype(jnp.float32)
    chosen = jnp.zeros((EXPERTS, rows), jnp.float32)
    gate = jnp.zeros((EXPERTS, rows), jnp.float32)
    for k in range(ids.shape[0]):
        hit = expert == ids[k : k + 1, :]
        chosen = jnp.where(hit, 1.0, chosen)
        gate = jnp.where(hit, gates[k : k + 1, :], gate)
    row = lax.broadcasted_iota(jnp.int32, (rows, rows), 0)
    column = lax.broadcasted_iota(jnp.int32, (rows, rows), 1)
    before = jnp.where(row < column, 1.0, 0.0).astype(jnp.bfloat16)
    slot = jnp.dot(chosen.astype(jnp.bfloat16), before, preferred_element_type=jnp.float32)
    slot = jnp.where(chosen > 0.5, slot, -1.0)
    high = gate.astype(jnp.bfloat16).astype(jnp.float32)
    rest = gate - high
    for device in range(devices):
        span = slice(device * local, (device + 1) * local)
        out[device] = jnp.concatenate(
            [slot[span], high[span], rest[span], jnp.zeros((16 - 3 * local, rows), jnp.float32)],
            axis=0,
        ).astype(jnp.bfloat16)


def layer_kernel(
    q_ref,
    suffix_ref,
    pool_ref,
    frequency_ref,
    table_ref,
    segment_ref,
    packed_ref,
    stream_ref,
    gain_ref,
    ids_ref,
    gates_ref,
    proj_hbm,
    wg_hbm,
    wu_hbm,
    wd_hbm,
    o_ref,
    mid_ref,
    cos_ref,
    sin_ref,
    proj,
    c_out,
    c_in,
    q_out,
    q_in,
    q_all,
    p_out,
    p_in,
    s_out,
    s_in,
    vx,
    bounds,
    best,
    acc,
    o_out,
    o_in,
    attended,
    proj_sem,
    qs_sem,
    qr_sem,
    ps_sem,
    pr_sem,
    ss_sem,
    sr_sem,
    os_sem,
    or_sem,
    cs_sem,
    cr_sem,
    wg,
    wu,
    wd,
    buf,
    part_sums,
    picked,
    produced,
    spread,
    sendx,
    recvx,
    stage,
    recv_out,
    recv_in,
    sendf,
    recvf,
    w_sem,
    ag_send,
    ag_recv,
    sx_sem,
    rx_sem,
    st_sem,
    ro_sem,
    ri_sem,
    f_sem,
):
    me = lax.axis_index("tok")
    z = me // 2
    x = me % 2
    partner = z * 2 + 1 - x
    rows = q_ref.shape[0]
    half = rows // 2
    page_rows = pool_ref.shape[0]
    kv_width = KVH * HD
    f32, bf16 = jnp.float32, jnp.bfloat16

    proj_copy = pltpu.make_async_copy(proj_hbm, proj, proj_sem)
    proj_copy.start()

    barrier = pltpu.get_barrier_semaphore()
    chunks = [z, 1 + z % 2, (2 + 3 * z) % 5, 3 - 3 * (z // 2)]
    near = [partner]
    for c in chunks[1:]:
        near += [2 * c + x, 2 * c + 1 - x]
    far = near[::-1]
    for peer in near:
        pl.semaphore_signal(
            barrier, inc=1, device_id={"tok": peer}, device_id_type=pl.DeviceIdType.MESH
        )

    def send(src, dst, send_sem, recv_sem, device):
        return pltpu.make_async_remote_copy(
            src_ref=src,
            dst_ref=dst,
            send_sem=send_sem,
            recv_sem=recv_sem,
            device_id={"tok": device},
            device_id_type=pl.DeviceIdType.MESH,
        )

    def exchange(out, into, send_sem, recv_sem):
        def to(peer):
            return send(out.at[peer], into.at[me], send_sem.at[peer], recv_sem.at[me], peer)

        def came(peer):
            return send(out.at[peer], into.at[peer], send_sem.at[peer], recv_sem.at[peer], peer)

        return to, came

    q_to, q_from = exchange(q_out, q_in, qs_sem, qr_sem)
    p_to, p_from = exchange(p_out, p_in, ps_sem, pr_sem)
    s_to, s_from = exchange(s_out, s_in, ss_sem, sr_sem)
    returns = [
        exchange(o_out.at[h], o_in.at[h], os_sem.at[h], or_sem.at[h]) for h in range(2)
    ]
    c_to, c_from = exchange(c_out, c_in, cs_sem, cr_sem)

    def lanes(shape):
        return lax.broadcasted_iota(jnp.int32, shape, 1)

    def turn(v, cosine, sine):
        first = lanes(v.shape) % HD < HD // 2
        swapped = jnp.where(first, pltpu.roll(v, 128 - HD // 2, 1), pltpu.roll(v, HD // 2, 1))
        return (v * cosine + swapped * sine).astype(bf16).astype(f32)

    def mix(left, right):
        return jnp.where(lanes(left.shape) < HD, left, right)

    def flip(v):
        return pltpu.roll(v, HD, 1)

    pages = page_rows // 128
    split = [slice(first, first + rows) for first in range(0, 8 * rows, rows)]
    dealt = jnp.concatenate([packed_ref[:, span] for span in split], axis=0).astype(f32)
    owner = jnp.concatenate([segment_ref[:, span] for span in split], axis=0).astype(f32)
    start = jnp.zeros_like(dealt)
    for request in range(REQS):
        earlier = jnp.where(owner < request, 1.0, 0.0)
        earlier = jnp.sum(jnp.sum(earlier, axis=1, keepdims=True), axis=0, keepdims=True)
        start = jnp.where(earlier <= dealt, jnp.maximum(start, earlier), start)
    bounds[0] = start.T
    bounds[1] = dealt.T

    def column(which, r):
        v = bounds[which]
        return jnp.sum(jnp.where(lanes(v.shape) == r, v, 0.0), axis=1, keepdims=True)

    prefix_len = table_ref.shape[1] * 128
    second = lanes((rows, 128)) % HD >= HD // 2
    angles = (column(1, me) - column(0, me) + prefix_len) * frequency_ref[...]
    cos_ref[page_rows:, :] = jnp.cos(angles)
    sine = jnp.sin(angles)
    sin_ref[page_rows:, :] = jnp.where(second, sine, -sine)

    def tables():
        table = table_ref[...]
        at = lax.broadcasted_iota(jnp.int32, table.shape, 1)
        lane = lanes((128, 128))
        logical = jnp.zeros((128, 128), f32)
        for i in range(pages):
            page = jnp.sum(
                jnp.where(table == me * pages + i, at, 0).astype(f32), axis=1, keepdims=True
            )
            logical = jnp.where(lane // (HD // 2) == i, page, logical)
        row = lax.broadcasted_iota(jnp.int32, (128, 128), 0).astype(f32)
        angles = (logical * 128.0 + row) * frequency_ref[...]
        for ref, every in ((cos_ref, jnp.cos(angles)), (sin_ref, jnp.sin(angles))):
            for i in range(pages):
                v = pltpu.roll(every, (4 - i) * (HD // 2) % 128, 1) if i else every
                v = jnp.where(lane < HD // 2, v, pltpu.roll(v, HD // 2, 1))
                v = jnp.where(lane < HD, v, pltpu.roll(v, HD, 1))
                if ref is sin_ref:
                    v = jnp.where(second, v, -v)
                ref[128 * i : 128 * i + 128, :] = v

    cosine, sine = cos_ref[page_rows:, :], sin_ref[page_rows:, :]
    for pair in range(QH // 2):
        v = q_ref[:, 128 * pair : 128 * pair + 128].astype(f32)
        v = turn(v, cosine, sine) * (HD**-0.5)
        top, low = v[:half], v[half:]
        for n, packed in ((2 * pair, mix(top, flip(low))), (2 * pair + 1, mix(flip(top), low))):
            q_out[n // RATIO, n % RATIO] = packed.astype(bf16)
    pl.semaphore_wait(barrier, 7)
    for peer in near:
        q_to(peer).start()

    def caches(src, first, table, out, at):
        span = pl.ds(first, 128)
        cosine, sine = cos_ref[pl.ds(table, 128), :], sin_ref[pl.ds(table, 128), :]
        for pair in range(KVH // 2):
            k = src[span, 128 * pair : 128 * pair + 128].astype(f32)
            k = turn(k, cosine, sine)
            v = src[span, kv_width + 128 * pair : kv_width + 128 * pair + 128].astype(f32)
            out[2 * pair, span, :] = mix(k, flip(v)).astype(bf16)
            out[2 * pair + 1, span, :] = mix(flip(k), v).astype(bf16)

    caches(suffix_ref, 0, page_rows, s_out, 0)
    for peer in near:
        s_to(peer).start()

    tables()

    def prepare(i, carry):
        first = pl.multiple_of(i * 128, 128)
        caches(pool_ref, first, first, p_out, 0)
        return carry

    lax.fori_loop(0, page_rows // 128, prepare, 0)
    for peer in near:
        p_to(peer).start()

    def weight_copies(e):
        return [
            pltpu.make_async_copy(src.at[e], dst.at[e], w_sem.at[e, i])
            for i, (src, dst) in enumerate([(wg_hbm, wg), (wu_hbm, wu), (wd_hbm, wd)])
        ]

    for e in range(wg.shape[0]):
        for copy in weight_copies(e):
            copy.start()

    route(ids_ref, gates_ref, c_out)
    for peer in near:
        c_to(peer).start()
    c_in[me] = c_out[me]
    q_in[me] = q_out[me]
    s_in[me] = s_out[me]

    def values(keys):
        return jnp.where(lanes(keys.shape) < HD, jnp.ones_like(keys), keys)

    def unpack(r):
        for j in range(RATIO):
            v = q_in[r, j].astype(f32)
            zero = jnp.zeros_like(v)
            q_all[r, pl.ds(j * rows, half), :] = mix(v, zero).astype(bf16)
            q_all[r, pl.ds(j * rows + half, half), :] = mix(flip(v), zero).astype(bf16)

    def scored(r, keys, count, masked):
        s = lax.dot_general(
            q_all[r], keys, (((1,), (1,)), ((), ())), preferred_element_type=f32
        )
        if masked:
            at = packed_ref[...].astype(f32)
            seen = (at >= column(0, r)) & (at <= column(1, r))
            bias = jnp.where(seen, 0.0, NEG_FILL)
            s = (s.reshape(RATIO, rows, count) + bias[None]).reshape(RATIO * rows, count)
        return s

    def blocks(rs, keys, count, masked=False, first=False):
        olds = [None if first else best[r] for r in rs]
        sums = [None if first else acc[r] for r in rs]
        scores = [scored(r, keys, count, masked) for r in rs]
        tops, totals = [], []
        for s, old, before in zip(scores, olds, sums):
            top = jnp.broadcast_to(jnp.max(s, axis=-1, keepdims=True), (RATIO * rows, 128))
            if not first:
                top = jnp.maximum(old, top)
            weights = jnp.exp(s - jnp.concatenate([top] * (count // 128), axis=1)).astype(bf16)
            total = jnp.dot(weights, vx[:count], preferred_element_type=f32)
            if not first:
                total = before * jnp.exp(old - top) + total
            tops.append(top)
            totals.append(total)
        for r, top, total in zip(rs, tops, totals):
            acc[r] = total
            best[r] = top

    def finish(rs, h, keys, count):
        def taken(ref, r):
            spans = [pl.ds(j * rows + h * half, half) for j in range(RATIO)]
            return jnp.concatenate([ref[r, span, :] for span in spans], axis=0)

        olds = [taken(best, r) for r in rs]
        sums = [taken(acc, r) for r in rs]
        scores = [
            lax.dot_general(
                taken(q_all, r), keys, (((1,), (1,)), ((), ())), preferred_element_type=f32
            )
            for r in rs
        ]
        totals = []
        for s, old, before in zip(scores, olds, sums):
            top = jnp.broadcast_to(jnp.max(s, axis=-1, keepdims=True), old.shape)
            top = jnp.maximum(old, top)
            weights = jnp.exp(s - jnp.concatenate([top] * (count // 128), axis=1)).astype(bf16)
            total = jnp.dot(weights, vx[:count], preferred_element_type=f32)
            totals.append(before * jnp.exp(old - top) + total)
        for r, total in zip(rs, totals):
            v = total / flip(total)
            for j in range(RATIO):
                w = v[j * half : (j + 1) * half]
                o_out[h, r, j] = mix(flip(w[: half // 2]), w[half // 2 :]).astype(bf16)
            pl.when(r != me)(lambda r=r: returns[h][0](r).start())

    def last_step(keys_ref, count):
        vx[:count] = values(keys_ref())
        for h in (1, 0):

            def body(i, carry, h=h):
                c, d = lax.rem(z + 1 + 2 * i, 4), lax.rem(z + 2 + 2 * i, 4)
                finish([2 * c, 2 * c + 1, 2 * d, 2 * d + 1], h, keys_ref(), count)
                return carry

            lax.fori_loop(0, 2, body, 0)

    def step(keys_ref, count, masked=False, first=False):
        vx[:count] = values(keys_ref())

        def body(i, carry):
            c = lax.rem(z + i, 4)
            for side in range(2):
                r = 2 * c + side
                if first:
                    pl.when(r != me)(lambda r=r: q_from(r).wait_recv())
                    unpack(r)
            blocks([2 * c, 2 * c + 1], keys_ref(), count, masked, first)
            return carry

        lax.fori_loop(0, 4, body, 0)

    step(lambda: p_out[me], page_rows, first=True)
    for peer in near:
        s_from(peer).wait_recv()
    step(lambda: s_in[...].reshape(8 * rows, 128), 8 * rows, masked=True)
    p_from(partner).wait_recv()
    step(lambda: p_in[partner], page_rows)
    for i in range(1, 4):
        c = chunks[i]
        p_from(2 * c + x).wait_recv()
        p_from(2 * c + 1 - x).wait_recv()
        (last_step if i == 3 else step)(
            lambda c=c: p_in[pl.ds(2 * c, 2)].reshape(2 * page_rows, 128), 2 * page_rows
        )
    for peer in near:
        c_from(peer).wait_recv()
    width = mid_ref.shape[1]
    local = wg.shape[0]
    cut = sendx.shape[1]
    tail = rows - cut
    parts = [pl.ds(0, cut), pl.ds(cut, tail)]
    inner = (z + 1) // 2 % 2 == 1
    outer = (z + 1) // 2 % 2 == 0
    toward = me + 2 - 4 * (z // 2)
    outside = me - 2 + 4 * (z // 2)

    def token_copy(shard, part, way):
        return send(
            buf.at[shard, parts[part]],
            buf.at[shard, parts[part]],
            ag_send.at[shard, part, way],
            ag_recv.at[shard, part],
            partner,
        )

    def to_partner(shard, part):
        token_copy(shard, part, 0).start()

    def way_copy(shard, part, device, way):
        return send(
            buf.at[shard, parts[part]],
            buf.at[shard, parts[part]],
            ag_send.at[shard, part, way],
            ag_recv.at[shard, part],
            device,
        )

    def to_center(shard, part):
        way_copy(shard, part, toward, 1).start()

    def to_outside(shard, part):
        way_copy(shard, part, outside, 2).start()

    def arrived(shard, part):
        token_copy(shard, part, 0).wait_recv()

    slots = picked.shape[0] // local

    def compute(c, first):
        tokens = buf[pl.ds(2 * c, 2)].reshape(2 * rows, width)
        code = c_in[pl.ds(2 * c, 2)].astype(f32)
        code = jnp.concatenate([code[0], code[1]], axis=1)
        shape = (slots, 2 * rows)
        row = lax.broadcasted_iota(jnp.int32, shape, 0).astype(f32)
        second = lax.broadcasted_iota(jnp.int32, (1, 2 * rows), 1) >= rows
        chosen = []
        for e in range(local):
            slot = code[e : e + 1, :]
            place = jnp.where(slot < 0.0, -1.0, jnp.where(second, slot + slots // 2, slot))
            hit = row == place
            chosen.append(jnp.where(hit, 1.0, 0.0).astype(bf16))
            for i in range(2):
                gate = code[(i + 1) * local + e : (i + 1) * local + e + 1, :]
                spread[i, e * slots : (e + 1) * slots, :] = jnp.where(hit, gate, 0.0).astype(bf16)
        picked[...] = jnp.dot(
            jnp.concatenate(chosen, axis=0), tokens, preferred_element_type=f32
        ).astype(bf16)

        def one(e, carry):
            if first:
                for copy in weight_copies(e):
                    copy.wait()
            span = pl.ds(pl.multiple_of(e * slots, 16), slots)
            some = picked[span, :]
            gate_vals = jnp.dot(some, wg[e], preferred_element_type=f32)
            up_vals = jnp.dot(some, wu[e], preferred_element_type=f32)
            hidden = (gate_vals / (1.0 + jnp.exp(-gate_vals)) * up_vals).astype(bf16)
            produced[span, :] = jnp.dot(hidden, wd[e], preferred_element_type=f32).astype(bf16)
            return carry

        lax.fori_loop(0, local, one, 0, unroll=2)
        total = sum(
            lax.dot_general(
                spread[i], produced[...], (((0,), (0,)), ((), ())), preferred_element_type=f32
            )
            for i in range(2)
        )
        part_sums[pl.ds(2 * c, 2)] = total.reshape(2, rows, width)
        sendx[c] = part_sums[2 * c + 1 - x, parts[0]].astype(bf16)
        across(c).start()

    def across(c):
        return send(sendx.at[c], recvx.at[c], sx_sem.at[c], rx_sem.at[c], partner)

    def add_across(c):
        across(c).wait()
        part_sums[2 * c + x, parts[0]] += recvx[c].astype(f32)

    def place(c, piece):
        if piece == 0:
            return part_sums.at[2 * c + x, parts[0]], pl.ds(0, cut)
        return part_sums.at[2 * c + piece - 1, parts[1]], pl.ds(cut + (piece - 1) * tail, tail)

    def hop(c, piece, into, sem, device):
        span = place(c, piece)[1]
        return send(
            stage.at[c, span], into.at[c, span], st_sem.at[c, piece], sem.at[c, piece], device
        )

    def outward_hop(c, piece):
        return hop(c, piece, recv_out, ro_sem, toward)

    def center_hop(c, piece):
        return hop(c, piece, recv_in, ri_sem, toward)

    def back_hop(c, piece):
        return hop(c, piece, recv_in, ri_sem, outside)

    def emit(c, piece, hop_of):
        part, span = place(c, piece)
        stage[c, span] = part[...].astype(bf16)
        hop_of(c, piece).start()

    def fold(c, piece, hop_of, ref):
        hop_of(c, piece).wait_recv()
        part, span = place(c, piece)
        part[...] += ref[c, span].astype(f32)

    def relay(c, pieces, came, ref, hop_of):
        for piece in pieces:
            if piece == 0:
                add_across(c)
            fold(c, piece, came, ref)
            emit(c, piece, hop_of)

    def early(c):
        emit(c, 1, outward_hop)
        emit(c, 2, outward_hop)

    def late(c):
        add_across(c)
        emit(c, 0, outward_hop)

    upper = z // 2
    is_inner = (z + 1) // 2 % 2

    def mirrored(c):
        return c + upper * (3 - 2 * c)

    turns = [mirrored(c) for c in (0 * z, 1 + 2 * is_inner, 3 - is_inner, 2 - is_inner)]
    near_c, far_c, mid_c = mirrored(1), mirrored(3), mirrored(2)
    out_c = mirrored(0)

    def pair(c):
        return 2 * c + x, 2 * c + 1 - x

    def settle(h):
        o_in[h, me] = o_out[h, me]
        for peer in far:
            returns[h][1](peer).wait_recv()
        own = slice(h * half, (h + 1) * half)
        first = slice(h * half, h * half + half // 2)
        later = slice(h * half + half // 2, (h + 1) * half)
        for one_pair in range(QH // 2):
            n, m = 2 * one_pair, 2 * one_pair + 1
            one = o_in[h, n // RATIO, n % RATIO].astype(f32)
            two = o_in[h, m // RATIO, m % RATIO].astype(f32)
            span = slice(128 * one_pair, 128 * one_pair + 128)
            attended[first, span] = mix(one, flip(two)).astype(bf16)
            attended[later, span] = mix(flip(one), two).astype(bf16)
        for at in range(0, proj.shape[1], 512):
            span = slice(at, at + 512)
            mid_ref[own, span] = (
                stream_ref[own, span].astype(f32)
                + jnp.dot(attended[own, :], proj[:, span], preferred_element_type=f32)
            ).astype(bf16)
        mid = mid_ref[own, :].astype(f32)
        buf[me, own] = (
            mid
            * lax.rsqrt(jnp.mean(mid * mid, axis=-1, keepdims=True) + 1e-05)
            * gain_ref[...].reshape(1, -1)
        ).astype(bf16)

    proj_copy.wait()
    settle(1)
    to_partner(me, 1)
    to_center(me, 1)
    pl.when(inner)(lambda: to_outside(me, 1))
    settle(0)

    @pl.when(outer)
    def _():
        same, other = pair(near_c)
        to_partner(me, 0)
        to_center(me, 0)
        arrived(partner, 1)
        to_center(partner, 1)
        arrived(partner, 0)
        arrived(same, 1)
        arrived(same, 0)
        to_partner(same, 0)

    @pl.when(inner)
    def _():
        same, other = pair(out_c)
        far_same, far_other = pair(far_c)
        to_partner(me, 0)
        to_outside(me, 0)
        arrived(same, 1)
        to_center(same, 1)
        arrived(partner, 1)
        to_outside(partner, 1)
        to_center(partner, 1)
        arrived(same, 0)
        to_center(same, 0)
        to_partner(same, 0)
        arrived(other, 1)
        to_center(other, 1)
        to_center(me, 0)
        arrived(partner, 0)
        arrived(far_same, 1)
        to_outside(far_same, 1)
        in_same, in_other = pair(mid_c)
        arrived(in_same, 1)
        to_outside(in_same, 1)
        arrived(other, 0)

    compute(turns[0], True)

    @pl.when(outer)
    def _():
        same, other = pair(near_c)
        arrived(other, 1)
        arrived(other, 0)

    @pl.when(inner)
    def _():
        far_same, far_other = pair(far_c)
        in_same, in_other = pair(mid_c)
        arrived(far_same, 0)
        to_outside(far_same, 0)
        to_partner(far_same, 0)
        arrived(far_other, 1)
        to_outside(far_other, 1)
        arrived(in_same, 0)
        to_outside(in_same, 0)
        to_partner(in_same, 0)
        arrived(in_other, 1)
        to_outside(in_other, 1)
        arrived(far_other, 0)

    compute(turns[1], False)

    @pl.when(outer)
    def _():
        far_same, far_other = pair(far_c)
        early(near_c)
        arrived(far_same, 1)
        arrived(far_same, 0)
        to_partner(far_same, 0)
        late(near_c)
        arrived(far_other, 1)
        arrived(far_other, 0)

    @pl.when(inner)
    def _():
        arrived(pair(mid_c)[1], 0)

    compute(turns[2], False)

    @pl.when(outer)
    def _():
        in_same, in_other = pair(mid_c)
        early(far_c)
        arrived(in_same, 1)
        arrived(in_same, 0)
        to_partner(in_same, 0)
        late(far_c)
        arrived(in_other, 1)
        arrived(in_other, 0)

    compute(turns[3], False)

    @pl.when(outer)
    def _():
        early(mid_c)
        late(mid_c)

    @pl.when(inner)
    def _():
        relay(far_c, (1, 2, 0), outward_hop, recv_out, center_hop)
        relay(out_c, (1, 2), center_hop, recv_in, back_hop)
        relay(mid_c, (1, 2), outward_hop, recv_out, center_hop)
        relay(out_c, (0,), center_hop, recv_in, back_hop)
        relay(mid_c, (0,), outward_hop, recv_out, center_hop)

    add_across(z)
    for piece in (1, 2, 0):
        pl.when(inner)(lambda piece=piece: fold(z, piece, outward_hop, recv_out))
        fold(z, piece, center_hop, recv_in)
        if piece == 2:
            sendf[...] = part_sums[partner, parts[1]].astype(bf16)
            last = send(sendf, recvf, f_sem.at[0], f_sem.at[1], partner)
            last.start()
    o_ref[:cut, :] = (mid_ref[:cut, :].astype(f32) + part_sums[me, parts[0]]).astype(bf16)
    last.wait()
    o_ref[cut:, :] = (
        mid_ref[cut:, :].astype(f32) + (part_sums[me, parts[1]] + recvf[...].astype(f32))
    ).astype(bf16)

    for c in chunks[1:]:
        for piece in range(3):
            center_hop(c, piece).wait_send()

    for shard, part in [(me, 0), (me, 1)] + [(2 * c + x, 0) for c in chunks[1:]]:
        token_copy(shard, part, 0).wait_send()
    for shard, part in ((me, 0), (me, 1), (partner, 1)):
        way_copy(shard, part, toward, 1).wait_send()

    @pl.when(inner)
    def _():
        for way, cs in ((1, (out_c,)), (2, (z, mid_c, far_c))):
            for c in cs:
                same, other = pair(c)
                for shard, part in ((same, 0), (same, 1), (other, 1)):
                    way_copy(shard, part, toward, way).wait_send()
    for to in (q_to, s_to, p_to, returns[0][0], returns[1][0], c_to):
        for peer in near:
            to(peer).wait_send()


def layer(
    q, suffix, pool, table, segments, packed, stream, gain, ids, gates, proj, gate_proj, up_proj, down_proj
):
    rows = q.shape[0]
    half_dim = HD // 2
    frequency = np.tile(ROPE_BASE ** (-np.arange(half_dim) / half_dim), 4)
    frequency = jnp.asarray(frequency.astype(np.float32).reshape(1, 128))
    page_rows = pool.shape[0]
    width = stream.shape[1]
    local, _, hidden = gate_proj.shape
    cut = 5 * rows // 8
    legs = 2 * rows - cut
    vmem = pl.BlockSpec(memory_space=pltpu.VMEM)
    anywhere = pl.BlockSpec(memory_space=pl.ANY)
    bf16, f32 = jnp.bfloat16, jnp.float32
    dma = pltpu.SemaphoreType.DMA
    return pl.pallas_call(
        layer_kernel,
        out_shape=jax.ShapeDtypeStruct(stream.shape, bf16),
        in_specs=[vmem] * 11 + [anywhere] * 4,
        out_specs=vmem,
        scratch_shapes=[
            pltpu.VMEM(stream.shape, bf16),
            pltpu.VMEM((page_rows + rows, 128), f32),
            pltpu.VMEM((page_rows + rows, 128), f32),
            pltpu.VMEM(proj.shape, bf16),
            pltpu.VMEM((8, 16, rows), bf16),
            pltpu.VMEM((8, 16, rows), bf16),
            pltpu.VMEM((8, RATIO, rows // 2, 128), bf16),
            pltpu.VMEM((8, RATIO, rows // 2, 128), bf16),
            pltpu.VMEM((8, RATIO * rows, 128), bf16),
            pltpu.VMEM((8, page_rows, 128), bf16),
            pltpu.VMEM((8, page_rows, 128), bf16),
            pltpu.VMEM((8, rows, 128), bf16),
            pltpu.VMEM((8, rows, 128), bf16),
            pltpu.VMEM((2 * page_rows, 128), bf16),
            pltpu.VMEM((2, rows, 8), f32),
            pltpu.VMEM((8, RATIO * rows, 128), f32),
            pltpu.VMEM((8, RATIO * rows, 128), f32),
            pltpu.VMEM((2, 8, RATIO, rows // 4, 128), bf16),
            pltpu.VMEM((2, 8, RATIO, rows // 4, 128), bf16),
            pltpu.VMEM(q.shape, bf16),
            dma(()),
        ]
        + [dma((8,))] * 6
        + [dma((2, 8))] * 2
        + [dma((8,))] * 2
        + [
            pltpu.VMEM((local, width, hidden), bf16),
            pltpu.VMEM((local, width, hidden), bf16),
            pltpu.VMEM((local, hidden, width), bf16),
            pltpu.VMEM((8, rows, width), bf16),
            pltpu.VMEM((8, rows, width), f32),
            pltpu.VMEM((local * 2 * CAP, width), bf16),
            pltpu.VMEM((local * 2 * CAP, width), bf16),
            pltpu.VMEM((2, local * 2 * CAP, 2 * rows), bf16),
            pltpu.VMEM((4, cut, width), bf16),
            pltpu.VMEM((4, cut, width), bf16),
            pltpu.VMEM((4, legs, width), bf16),
            pltpu.VMEM((4, legs, width), bf16),
            pltpu.VMEM((4, legs, width), bf16),
            pltpu.VMEM((rows - cut, width), bf16),
            pltpu.VMEM((rows - cut, width), bf16),
            dma((local, 3)),
            dma((8, 2, 3)),
            dma((8, 2)),
            dma((4,)),
            dma((4,)),
            dma((4, 3)),
            dma((4, 3)),
            dma((4, 3)),
            dma((2,)),
        ],
        compiler_params=pltpu.CompilerParams(
            collective_id=1, has_side_effects=True, vmem_limit_bytes=60 << 20
        ),
    )(
        q,
        suffix,
        pool,
        frequency,
        table,
        segments,
        packed,
        stream,
        gain,
        ids,
        gates,
        proj,
        gate_proj,
        up_proj,
        down_proj,
    )


def shards(
    queries,
    suffix_cache,
    stream_in,
    page_pool,
    page_table,
    segment_ids,
    dealing,
    out_proj,
    norm_gain,
    expert_ids,
    expert_gates,
    gate_proj,
    up_proj,
    down_proj,
):
    tok_count = lax.axis_size("tok")
    tok_index = lax.axis_index("tok")
    rows_dev = queries.shape[1]
    width = KVH * HD
    table = page_table[0]
    pages_all = table.shape[0]
    pages_dev = page_pool.shape[1]
    page_len = page_pool.shape[2]
    pool_rows = pages_dev * page_len
    prefix_len = pages_all * page_len
    repeats = tok_count // KVH
    head_groups = [[r * KVH + h for h in range(KVH)] for r in range(repeats)]
    same_head = [[r * KVH + h for r in range(repeats)] for h in range(KVH)]
    sub = dict(axis_index_groups=head_groups) if repeats > 1 else {}

    gate_dense = jnp.sum(
        jnp.where(
            expert_ids[0][:, :, None] == jnp.arange(EXPERTS, dtype=jnp.int32)[None, None, :],
            expert_gates[0][:, :, None],
            0.0,
        ),
        axis=1,
    )

    my_slots = tok_index * pages_dev + jnp.arange(pages_dev, dtype=jnp.int32)
    logical_page = jnp.sum(
        jnp.where(
            table[:, None] == my_slots[None, :],
            jnp.arange(pages_all, dtype=jnp.int32)[:, None],
            0,
        ),
        axis=0,
    )
    pool_positions = (
        logical_page[:, None] * page_len + jnp.arange(page_len, dtype=jnp.int32)[None, :]
    ).reshape(-1)
    dealt = dealing[0]
    requests = jnp.arange(REQS, dtype=jnp.int32)
    starts = jnp.sum((segment_ids[0][:, None] < requests[None, :]).astype(jnp.int32), axis=0)
    low_all = jnp.max(
        jnp.where(starts[None, :] <= dealt[:, None], starts[None, :], 0), axis=1
    )
    my_start = tok_index * rows_dev
    my_dealt = lax.dynamic_slice_in_dim(dealt, my_start, rows_dev)
    my_low = lax.dynamic_slice_in_dim(low_all, my_start, rows_dev)
    my_positions = prefix_len + my_dealt - my_low

    if tok_count == 8:
        return layer(
            queries[0],
            suffix_cache[0],
            page_pool.reshape(pool_rows, 2 * width),
            page_table,
            segment_ids,
            dealing,
            stream_in[0],
            norm_gain,
            expert_ids[0].T,
            expert_gates[0].T,
            out_proj,
            gate_proj,
            up_proj,
            down_proj,
        )[None]

    cache = jnp.concatenate([page_pool.reshape(pool_rows, 2 * width), suffix_cache[0]], axis=0)
    positions = jnp.concatenate([pool_positions, my_positions])
    count = pool_rows + rows_dev
    keys = rotate(cache[:, :width].reshape(count, KVH, HD), positions)
    values = cache[:, width:].reshape(count, KVH, HD)
    outgoing = jnp.concatenate([keys, values], axis=-1).transpose(1, 0, 2)
    arrived = lax.all_to_all(outgoing, "tok", split_axis=0, concat_axis=0, tiled=True, **sub)
    if repeats > 1:
        arrived = lax.all_gather(
            arrived, "tok", axis=0, tiled=True, axis_index_groups=same_head
        )
    kv = jnp.concatenate(
        [
            arrived[:, :pool_rows].reshape(-1, 2 * HD),
            arrived[:, pool_rows:].reshape(-1, 2 * HD),
        ],
        axis=0,
    )

    half = rows_dev // 2
    roped = rotate(queries[0].reshape(rows_dev, QH, HD), my_positions)
    packed_q = (
        roped.reshape(2, half, KVH, RATIO, HD)
        .transpose(2, 3, 1, 0, 4)
        .reshape(KVH, RATIO, half, 2 * HD)
    )
    got_q = lax.all_to_all(packed_q, "tok", split_axis=0, concat_axis=0, tiled=True, **sub)
    got_q = jnp.concatenate([got_q[..., :HD], got_q[..., HD:]], axis=2)
    got_q = jnp.pad(got_q, ((0, 0), (0, 0), (0, 0), (0, HD)))
    row_count = KVH * rows_dev
    first_row = (tok_index // KVH) * row_count
    low_q = lax.dynamic_slice_in_dim(low_all, first_row, row_count)
    high_q = lax.dynamic_slice_in_dim(dealt, first_row, row_count)
    out = attention(got_q, kv, low_q, high_q, dealt, prefix_len)
    back = lax.all_to_all(out, "tok", split_axis=0, concat_axis=0, tiled=True, **sub)
    attended = (
        back.reshape(KVH, RATIO, half, 2, HD)
        .transpose(3, 2, 0, 1, 4)
        .reshape(rows_dev, QH * HD)
    )

    mid_round = lax.optimization_barrier(
        (
            stream_in[0].astype(jnp.float32)
            + jnp.dot(attended, out_proj, preferred_element_type=jnp.float32)
        ).astype(jnp.bfloat16)
    )
    mid_float = mid_round.astype(jnp.float32)
    normed = (
        mid_float
        * lax.rsqrt(jnp.mean(mid_float * mid_float, axis=-1, keepdims=True) + 1e-05)
        * norm_gain
    ).astype(jnp.bfloat16)

    local = gate_proj.shape[0]
    gates_all = lax.all_gather(gate_dense, "tok", axis=0, tiled=True)
    gates_mine = lax.dynamic_slice_in_dim(gates_all, tok_index * local, local, axis=1)
    gates_mine = gates_mine.T.reshape(local, tok_count * rows_dev, 1)
    tokens = lax.all_gather(normed, "tok", axis=0, tiled=True)
    sums = expert_sums(tokens, gates_mine, gate_proj, up_proj, down_proj)
    mixed = lax.psum_scatter(sums, "tok", scatter_dimension=0, tiled=True)
    return (mid_float + mixed.astype(jnp.float32)).astype(jnp.bfloat16)[None]


def solution(mesh):
    placed = (
        P("group", "tok", None),
        P("group", "tok", None),
        P("group", "tok", None),
        P("group", "tok", None, None),
        P("group", None),
        P("group", None),
        P("group", None),
        P(),
        P(),
        P("group", "tok", None),
        P("group", "tok", None),
        P("tok", None, None),
        P("tok", None, None),
        P("tok", None, None),
    )
    return jax.shard_map(
        shards, mesh=mesh, in_specs=placed, out_specs=P("group", "tok", None), check_vma=False
    )
```
